32 devices in a mesh: modes: 4 (over y, core), gz: 8 (over z, x).
Axes of the slice: x: 2, y: 2, z: 4, core: 2. Of those that a mesh axis runs over, the one named last changes fastest.
Arguments:
- source_field: float32 [128, 2, 8, 2048], P('gz', None, None, 'modes'), may hold values from -0.075 to 0.075
- coupling_below: float32 [128], P('gz'), may hold values from 0.5 to 2
- coupling_above: float32 [128], P('gz'), may hold values from 0.5 to 2
- eigen_stream: float32 [8], replicated, may hold values from 0.000390625 to 0.015625
- eigen_span: float32 [2048], replicated, may hold values from 0.000390625 to 0.015625
Outputs:
- pressure: float32 [128, 2, 8, 2048], P('gz', None, 'modes')
The draws below stay inside these ranges and needn't reach their ends.
All inputs are finite; a program needn't handle non-finite values.
Results may differ from the reference program's by a relative error of at most 0.0003.
Values sent between devices are 32-bit elements; how exact they have to be, the bound alone decides.
No kernel may reach another device: no remote copies, remote signals or barrier semaphores. Data moves between devices by JAX's collectives and lax.ppermute only.
A program may use at most 64 MiB of HBM per device.

```python
import math
import jax
import jax.numpy as jnp
from jax import lax

CZ = 16
KY = 2048
KX = 8
NZ = 128


def draw_source_field(key, part):
    spread = 0.2 / CZ
    dims = (NZ, 2, KX, KY)
    return jnp.clip(jax.random.normal(key, dims, jnp.float32), -6.0, 6.0) * spread


def shard_levels(own_key, shape, pieces, smallest, top_value):
    def one(axis_at, parts):
        heights = jax.random.uniform(jax.random.fold_in(jax.random.fold_in(own_key, 6), axis_at), (parts,), jnp.float32, smallest / len(pieces), top_value / len(pieces))
        return jnp.repeat(jnp.exp(heights), shape[axis_at] // parts).reshape((-1,) + (1,) * (len(shape) - axis_at - 1))

    factor_of = one(*pieces[0])
    for cut in pieces[1:]:
        factor_of = factor_of * one(*cut)
    return factor_of


def setup_inputs(seed: int = 0) -> dict:
    splits = jax.random.split(jax.random.key(seed), 6)
    return {
        "source_field": draw_source_field(jax.random.fold_in(splits[5], 71), 0),
        "coupling_below": jnp.clip(jnp.exp(math.log(2.0) - 1.3862944 * jax.random.uniform(splits[1], (NZ,), jnp.float32) ** shard_levels(splits[1], (NZ,), ((0, 8),), -0.2, 0.2)), 0.5, 2.0),
        "coupling_above": jnp.clip(jnp.exp(math.log(2.0) - 1.3862944 * jax.random.uniform(splits[2], (NZ,), jnp.float32) ** shard_levels(splits[2], (NZ,), ((0, 8),), -0.2, 0.2)), 0.5, 2.0),
        "eigen_stream": jnp.clip(jnp.exp(jax.random.uniform(splits[3], (KX,), jnp.float32, math.log(0.000390625), math.log(0.015625))), 0.000390625, 0.015625),
        "eigen_span": jnp.clip(jnp.exp(jax.random.uniform(splits[4], (KY,), jnp.float32, math.log(0.000390625), math.log(0.015625))), 0.000390625, 0.015625),
    }


def reference(source_field, coupling_below, coupling_above, eigen_stream, eigen_span):
    planes = jnp.arange(NZ)
    lower_coef = jnp.where(planes == 0, jnp.zeros_like(coupling_below), coupling_below)
    upper_coef = jnp.where(planes == NZ - 1, jnp.zeros_like(coupling_above), coupling_above)

    def per_stream(inputs):
        eigen_one, block = inputs
        spectral = eigen_one + eigen_span
        central = lower_coef[None, :] + upper_coef[None, :] + spectral[:, None]
        below_band = jnp.broadcast_to(-lower_coef[None, :], central.shape)
        above_band = jnp.broadcast_to(-upper_coef[None, :], central.shape)
        rights = jnp.transpose(block, (2, 0, 1))
        solved = lax.linalg.tridiagonal_solve(below_band, central, above_band, rights)
        return jnp.transpose(solved, (1, 2, 0))
    stacked = lax.map(per_stream, (eigen_stream, jnp.moveaxis(source_field, 2, 0)))
    return jnp.moveaxis(stacked, 0, 2)
```

```python
import functools

import jax
import jax.numpy as jnp
from jax import lax
from jax.experimental import pallas as pl
from jax.experimental.pallas import tpu as pltpu
from jax.sharding import PartitionSpec as P

LANES = 128


def total(axis_size):
    return axis_size


def reduce_kernel(sizes, lower_ref, upper_ref, stream_ref, span_ref, source_ref, ports_ref, couple_ref):
    mode_count, rows, kx_count, tiles = sizes
    me = lax.axis_index("modes")
    lower = [lower_ref[k] for k in range(rows)]
    upper = [upper_ref[k] for k in range(rows)]
    lane = lax.broadcasted_iota(jnp.int32, (8, LANES), 1)
    sub = lax.broadcasted_iota(jnp.int32, (8, LANES), 0)
    table = jnp.zeros((8, LANES), jnp.float32)
    for k in range(rows):
        table = jnp.where((lane == k) & (sub == 0), lower[k], table)
        table = jnp.where((lane == k) & (sub == 1), upper[k], table)
    couple_ref[...] = table
    for dest in range(mode_count):
        spectral = spectral_block(sizes, stream_ref, span_ref, dest, me)
        grown = jnp.ones_like(spectral)
        passed = jnp.ones_like(spectral)
        partial = [jnp.zeros_like(spectral)] * 2
        first = [jnp.zeros_like(spectral)] * 2
        for k in range(rows):
            held = spectral + lower[k] * grown
            inverse = 1.0 / (upper[k] + held)
            factor = upper[k] * inverse
            grown = held * inverse
            for c in range(2):
                partial[c] = (source_ref[dest, k, c] + lower[k] * partial[c]) * inverse
                first[c] = first[c] + passed * partial[c]
            passed = passed * factor
        for c in range(2):
            ports_ref[dest, c] = first[c]
            ports_ref[dest, 2 + c] = partial[c]


def spectral_block(sizes, stream_ref, span_ref, dest, origin):
    _, _, kx_count, tiles = sizes
    height = tiles * kx_count
    sub = lax.broadcasted_iota(jnp.int32, (height, LANES), 0)
    streamwise = jnp.zeros((height, LANES), jnp.float32)
    for j in range(kx_count):
        streamwise = jnp.where(sub % kx_count == j, stream_ref[dest * kx_count + j], streamwise)
    spanwise = jnp.zeros((height, LANES), jnp.float32)
    for t in range(tiles):
        row = span_ref[pl.ds(origin * tiles + t, 1), :]
        spanwise = jnp.where(sub // kx_count == t, jnp.broadcast_to(row, (height, LANES)), spanwise)
    return streamwise + spanwise


def spread(table, i, k, shape):
    return jnp.broadcast_to(table[i : i + 1, k : k + 1], shape)


def climb(spectral, state, below, above):
    num, den = state
    product = None
    for near, far in zip(below, above):
        num = spectral * den + near * num
        before = den
        den = num + far * den
        product = near if product is None else product * near
    return num, den, far * before, product


def merge_kernel(sizes, stream_ref, span_ref, own_ref, pair_ref, own_table, pair_table, merged_ref, table_ref):
    mode_count, rows, kx_count, tiles = sizes
    shape = (tiles * kx_count, LANES)
    me = lax.axis_index("modes")
    upside = lax.axis_index("gz") % 2 == 1
    own, pair = own_table[...], pair_table[...]
    low_table = jnp.where(upside, pair, own)
    high_table = jnp.where(upside, own, pair)
    sub = lax.broadcasted_iota(jnp.int32, (8, LANES), 0)
    table_ref[...] = jnp.where(sub < 2, low_table, pltpu.roll(high_table, 2, 0))
    low_l = [spread(low_table, 0, k, shape) for k in range(rows)]
    low_u = [spread(low_table, 1, k, shape) for k in range(rows)]
    high_l = [spread(high_table, 0, k, shape) for k in range(rows)]
    high_u = [spread(high_table, 1, k, shape) for k in range(rows)]
    for d in range(mode_count):
        spectral = spectral_block(sizes, stream_ref, span_ref, me, me ^ d)
        one = jnp.ones(shape, jnp.float32)
        own_ports = [own_ref[d, i] for i in range(4)]
        pair_ports = [pair_ref[d, i] for i in range(4)]
        low = [jnp.where(upside, b, a) for a, b in zip(own_ports, pair_ports)]
        high = [jnp.where(upside, a, b) for a, b in zip(own_ports, pair_ports)]
        num, den, tail, _ = climb(spectral, (one, one), low_l, low_u)
        passed = tail / den
        _, den_all, _, product = climb(spectral, (num, den), high_l, high_u)
        ratio = product * den / den_all
        for c in range(2):
            merged_ref[d, 2 + c] = high[2 + c] + ratio * (low[2 + c] + passed * high[c])
        num, den, tail, _ = climb(spectral, (one, one), high_u[::-1], high_l[::-1])
        passed = tail / den
        _, den_all, _, product = climb(spectral, (num, den), low_u[::-1], low_l[::-1])
        ratio = product * den / den_all
        for c in range(2):
            merged_ref[d, c] = low[c] + ratio * (high[c] + passed * low[2 + c])


def final_kernel(sizes, pairs, lower_ref, upper_ref, stream_ref, span_ref, pair_ref, pair_table, *rest):
    mode_count, rows, kx_count, tiles = sizes
    shape = (tiles * kx_count, LANES)
    others = rest[: pairs - 1]
    tables = rest[pairs - 1 : 2 * (pairs - 1)]
    sources = rest[2 * (pairs - 1) : 2 * (pairs - 1) + mode_count]
    out_ref, factor_ref = rest[2 * (pairs - 1) + mode_count :]
    me = lax.axis_index("modes")
    partition = lax.axis_index("gz")
    upside = partition % 2 == 1
    level = partition // 2
    one = jnp.ones(shape, jnp.float32)
    zero = jnp.zeros(shape, jnp.float32)
    spectral = [spectral_block(sizes, stream_ref, span_ref, me, me ^ d) for d in range(mode_count)]
    start = ((one,) * mode_count, (zero,) * mode_count, (zero,) * (2 * mode_count))

    def enter(state, ports, enters, leaves, near, far):
        grown, passed, partial = state
        new_grown, new_passed, new_partial = [], [], []
        for d in range(mode_count):
            num, den, tail, product = climb(spectral[d], (grown[d], one), near, far)
            inverse = 1.0 / den
            ratio = product * inverse
            new_grown.append(num * inverse)
            new_passed.append(tail * inverse)
            for c in range(2):
                new_partial.append(
                    ports[d, leaves + c] + ratio * (partial[2 * d + c] + passed[d] * ports[d, enters + c])
                )
        return tuple(new_grown), tuple(new_passed), tuple(new_partial)

    def rows_of(table, which):
        low = [spread(table, i, k, shape) for i in which for k in range(rows)]
        return low

    def up(state, ports, table, blocks):
        near = rows_of(table, [2 * b for b in blocks])
        far = rows_of(table, [2 * b + 1 for b in blocks])
        return enter(state, ports, 0, 2, near, far)

    def down(state, ports, table, blocks):
        near = rows_of(table, [2 * b + 1 for b in blocks])[::-1]
        far = rows_of(table, [2 * b for b in blocks])[::-1]
        return enter(state, ports, 2, 0, near, far)

    from_below, from_above = start, start
    for d in range(pairs - 1, 0, -1):
        from_below = lax.cond(
            level >= d,
            lambda s, d=d: up(s, others[d - 1], tables[d - 1][...], (0, 1)),
            lambda s: s,
            from_below,
        )
    for d in range(1, pairs):
        from_above = lax.cond(
            level < d,
            lambda s, d=d: down(s, others[d - 1], tables[d - 1][...], (0, 1)),
            lambda s: s,
            from_above,
        )
    from_below = lax.cond(
        upside, lambda s: up(s, pair_ref, pair_table[...], (0,)), lambda s: s, from_below
    )
    from_above = lax.cond(
        upside, lambda s: s, lambda s: down(s, pair_ref, pair_table[...], (0,)), from_above
    )
    lower = [lower_ref[k] for k in range(rows)]
    upper = [upper_ref[k] for k in range(rows)]
    for d in range(mode_count):
        at = me ^ d
        grown = from_below[0][d]
        partial = list(from_below[2][2 * d : 2 * d + 2])
        for k in range(rows):
            held = spectral[d] + lower[k] * grown
            inverse = 1.0 / (upper[k] + held)
            factor = upper[k] * inverse
            grown = held * inverse
            factor_ref[k, d] = factor
            for c in range(2):
                partial[c] = (sources[d][k, c] + lower[k] * partial[c]) * inverse
                out_ref[k, c, at] = partial[c]
        rest_of = 1.0 / (grown + factor * from_above[0][d])
        for c in range(2):
            value = (partial[c] + factor * from_above[2][2 * d + c]) * rest_of
            out_ref[rows - 1, c, at] = value
            for k in range(rows - 2, -1, -1):
                value = out_ref[k, c, at] + factor_ref[k, d] * value
                out_ref[k, c, at] = value


SMEM = pl.BlockSpec(memory_space=pltpu.SMEM)
VMEM = pl.BlockSpec(memory_space=pltpu.VMEM)


def per_device(source_field, coupling_below, coupling_above, eigen_stream, eigen_span):
    rows, _, kx_total, ky_local = source_field.shape
    mode_count = lax.axis_size("modes")
    partitions = lax.axis_size("gz")
    chips = mode_count // 2
    pairs = partitions // 2
    kx_count = kx_total // mode_count
    tiles = ky_local // LANES
    height = tiles * kx_count
    sizes = (mode_count, rows, kx_count, tiles)
    me = lax.axis_index("modes")
    partition = lax.axis_index("gz")
    global_row = partition * rows + jnp.arange(rows)
    lower = jnp.where(global_row == 0, 0.0, coupling_below)
    upper = jnp.where(global_row == rows * partitions - 1, 0.0, coupling_above)
    span = eigen_span.reshape(-1, LANES)

    def move(array, modes_by=0, pair=0, level=0):
        links = []
        for m in range(mode_count):
            for g in range(partitions):
                to = ((g // 2 + level) % pairs) * 2 + ((g % 2) ^ pair)
                links.append((m * partitions + g, (m ^ modes_by) * partitions + to))
        return lax.ppermute(array, ("modes", "gz"), links)

    def piece(array, index):
        return lax.dynamic_index_in_dim(array, index, 0, keepdims=False)

    blocks = source_field.reshape(rows, 2, mode_count, kx_count, tiles, LANES)
    blocks = blocks.transpose(2, 0, 1, 4, 3, 5).reshape(mode_count, rows, 2, height, LANES)
    block_shape = jax.ShapeDtypeStruct((mode_count, 4, height, LANES), jnp.float32)
    table_shape = jax.ShapeDtypeStruct((8, LANES), jnp.float32)
    ports, table = pl.pallas_call(
        functools.partial(reduce_kernel, sizes),
        out_shape=(block_shape, table_shape),
        in_specs=[SMEM, SMEM, SMEM, VMEM, VMEM],
        out_specs=(VMEM, VMEM),
        name="reduce",
    )(lower, upper, eigen_stream, span, blocks)

    by_core = ports.reshape(chips, 2, 4, height, LANES)
    chip, core = me // 2, me % 2
    kept = lax.dynamic_index_in_dim(by_core, core, 1, keepdims=False)
    given = lax.dynamic_index_in_dim(by_core, core ^ 1, 1, keepdims=False)
    taken = move(given, modes_by=1)
    chip_blocks = jnp.stack([kept, taken], axis=1)
    own, partner = [], []
    table_pair = move(table, pair=1)
    for d in range(chips):
        block = piece(chip_blocks, chip ^ d)
        own.append(move(block, modes_by=2 * d) if d else block)
        partner.append(move(block, modes_by=2 * d, pair=1))
    own_ports = jnp.concatenate(own, axis=0)
    pair_ports = jnp.concatenate(partner, axis=0)
    merged, pair_table = pl.pallas_call(
        functools.partial(merge_kernel, sizes),
        out_shape=(block_shape, table_shape),
        in_specs=[SMEM] + [VMEM] * 5,
        out_specs=(VMEM, VMEM),
        name="merge",
    )(eigen_stream, span, own_ports, pair_ports, table, table_pair)
    message = jnp.concatenate([merged.reshape(-1, LANES), pair_table], axis=0)
    others, tables = [], []
    for d in range(1, pairs):
        got = move(message, level=d)
        others.append(got[:-8].reshape(merged.shape))
        tables.append(got[-8:])
    sources = [piece(blocks, me)] + [move(piece(blocks, me ^ d), modes_by=d) for d in range(1, mode_count)]
    out = pl.pallas_call(
        functools.partial(final_kernel, sizes, pairs),
        out_shape=jax.ShapeDtypeStruct((rows, 2, mode_count, height, LANES), jnp.float32),
        in_specs=[SMEM] * 3 + [VMEM] * (3 + 2 * (pairs - 1) + mode_count),
        out_specs=VMEM,
        scratch_shapes=[pltpu.VMEM((rows, mode_count, height, LANES), jnp.float32)],
        name="solve",
    )(lower, upper, eigen_stream, span, pair_ports, table_pair, *others, *tables, *sources)
    out = out.reshape(rows, 2, mode_count * tiles, kx_count, LANES).transpose(0, 1, 3, 2, 4)
    return out.reshape(rows, 2, kx_count, -1)


def solution(mesh):
    in_specs = (P("gz", None, None, "modes"), P("gz"), P("gz"), P(), P())
    out_specs = P("gz", None, "modes", None)
    return jax.shard_map(
        per_device, mesh=mesh, in_specs=in_specs, out_specs=out_specs, check_vma=False
    )
```

```python
import functools

import jax
import jax.numpy as jnp
from jax import lax
from jax.experimental import pallas as pl
from jax.experimental.pallas import tpu as pltpu
from jax.sharding import PartitionSpec as P

LANES = 128
SUBLANES = 8


def sizes_of(source_field):
    rows, _, kx_total, ky_local = source_field.shape
    mode_count = lax.axis_size("modes")
    kx_count, tiles = kx_total // mode_count, ky_local // LANES
    return rows, kx_total, kx_count, tiles, mode_count, kx_count * tiles


def chunks_of(rows):
    size = rows // 4 if rows % 4 == 0 else rows
    return [(first, size) for first in range(0, rows, size)]


def reduce_kernel(sizes, below_ref, above_ref, stream_ref, span_ref, source_hbm, ports_ref, table_ref, spectral_ref, source_ref, sems):
    rows, kx_total, kx_count, tiles, mode_count, height = sizes
    me, partition = lax.axis_index("modes"), lax.axis_index("gz")
    copies = []
    for i, (first, size) in enumerate(chunks_of(rows)):
        copies.append(
            pltpu.make_async_copy(source_hbm.at[pl.ds(first, size)], source_ref.at[pl.ds(first, size)], sems.at[i])
        )
        copies[-1].start()
    lower = [below_ref[k] for k in range(rows)]
    upper = [above_ref[k] for k in range(rows)]
    lower[0] = jnp.where(partition == 0, 0.0, lower[0])
    upper[-1] = jnp.where(partition == lax.axis_size("gz") - 1, 0.0, upper[-1])
    lane = lax.broadcasted_iota(jnp.int32, (SUBLANES, LANES), 1)
    sub = lax.broadcasted_iota(jnp.int32, (SUBLANES, LANES), 0)
    table = jnp.zeros((SUBLANES, LANES), jnp.float32)
    for k in range(rows):
        table = jnp.where(lane == k, jnp.where(sub == 0, lower[k], upper[k]), table)
    table_ref[...] = table
    for d in range(mode_count):
        for t in range(tiles):
            spanwise = span_ref[pl.ds((me ^ d) * tiles + t, 1), :]
            for j in range(kx_count):
                at = d * height + t * kx_count + j
                spectral_ref[at : at + 1, :] = spanwise + stream_ref[me * kx_count + j]
    shape = (kx_total, LANES)
    kx_at = lax.broadcasted_iota(jnp.int32, shape, 0)
    streamwise = jnp.zeros(shape, jnp.float32)
    for i in range(kx_total):
        streamwise = jnp.where(kx_at == i, stream_ref[i], streamwise)
    each = range(tiles)
    spectral = [streamwise + span_ref[pl.ds(me * tiles + t, 1), :] for t in each]
    one, zero = jnp.ones(shape, jnp.float32), jnp.zeros(shape, jnp.float32)
    grown, passed = [one] * tiles, [one] * tiles
    partial = [[zero] * tiles, [zero] * tiles]
    first_value = [[zero] * tiles, [zero] * tiles]
    starts = {first: i for i, (first, _) in enumerate(chunks_of(rows))}
    for k in range(rows):
        if k in starts:
            copies[starts[k]].wait()
        for t in each:
            held = spectral[t] + lower[k] * grown[t]
            inverse = 1.0 / (upper[k] + held)
            grown[t] = held * inverse
            for c in range(2):
                source = source_ref[k, c, :, t * LANES : (t + 1) * LANES]
                partial[c][t] = (source + lower[k] * partial[c][t]) * inverse
                first_value[c][t] = first_value[c][t] + passed[t] * partial[c][t]
            passed[t] = passed[t] * (upper[k] * inverse)
    values = first_value + partial
    for dest in range(mode_count):
        to = dest ^ me
        for i in range(4):
            for t in each:
                at = i * height + t * kx_count
                ports_ref[to % 2, to // 2, at : at + kx_count, :] = values[i][t][dest * kx_count : (dest + 1) * kx_count]


def regroup_kernel(sizes, source_hbm, blocks_ref, source_ref, sems):
    rows, kx_total, kx_count, tiles, mode_count, height = sizes
    me = lax.axis_index("modes")
    copies = []
    for i, (first, size) in enumerate(chunks_of(rows)):
        copies.append(
            pltpu.make_async_copy(source_hbm.at[pl.ds(first, size)], source_ref.at[pl.ds(first, size)], sems.at[i])
        )
        copies[-1].start()
    for i, (first, size) in enumerate(chunks_of(rows)):
        copies[i].wait()
        for k in range(first, first + size):
            for c in range(2):
                for t in range(tiles):
                    at = t * kx_count
                    for dest in range(mode_count):
                        blocks_ref[dest ^ me, k, c, at : at + kx_count, :] = source_ref[
                            k, c, dest * kx_count : (dest + 1) * kx_count, t * LANES : (t + 1) * LANES
                        ]


def climb(spectral, num, den, near, far):
    product = near[0]
    for k in range(len(near)):
        num = spectral * den + near[k] * num
        before = den
        den = num + far[k] * den
        if k:
            product = product * near[k]
    return num, den, far[-1] * before, product


def couplings(table, line, rows):
    return [table[line : line + 1, k : k + 1] for k in range(rows)]


def merge_kernel(sizes, spectral_ref, table_ref, ports_ref, taken_ref, side_ref, *rest):
    rows, kx_total, kx_count, tiles, mode_count, height = sizes
    chips = mode_count // 2
    own_refs, pair_refs, message_ref = rest[: chips - 1], rest[chips - 1 : 2 * (chips - 1)], rest[-1]
    total = mode_count * height
    port = 4 * height
    upside = lax.axis_index("gz") % 2 == 1

    def gather(i, chunk):
        return jnp.concatenate([chunk(d, i * height) for d in range(mode_count)], axis=0)

    def own_chunk(d, at):
        if d >= 2:
            start = (d % 2) * port + at
            return own_refs[d // 2 - 1][start : start + height, :]
        return ports_ref[0, 0, at : at + height, :] if d == 0 else taken_ref[0, at : at + height, :]

    def pair_chunk(d, at):
        start = (d % 2) * port + at
        ref = side_ref if d < 2 else pair_refs[d // 2 - 1]
        return ref[start : start + height, :]

    own_table, pair_table = table_ref[...], side_ref[2 * port :, :]
    low_table = jnp.where(upside, pair_table, own_table)
    high_table = jnp.where(upside, own_table, pair_table)
    sub = lax.broadcasted_iota(jnp.int32, (SUBLANES, LANES), 0)
    message_ref[4 * total :, :] = jnp.where(sub < 2, low_table, pltpu.roll(high_table, 2, 0))
    spectral = spectral_ref[...]
    one = jnp.ones((total, LANES), jnp.float32)
    own = [gather(i, own_chunk) for i in range(4)]
    pair = [gather(i, pair_chunk) for i in range(4)]
    low = [jnp.where(upside, b, a) for a, b in zip(own, pair)]
    high = [jnp.where(upside, a, b) for a, b in zip(own, pair)]
    low_l, low_u = couplings(low_table, 0, rows), couplings(low_table, 1, rows)
    high_l, high_u = couplings(high_table, 0, rows), couplings(high_table, 1, rows)

    def store(i, value):
        message_ref[i * total : (i + 1) * total, :] = value

    num, den, tail, _ = climb(spectral, one, one, low_l, low_u)
    passed = tail / den
    _, den_all, _, product = climb(spectral, num, den, high_l, high_u)
    ratio = product * den / den_all
    for c in range(2):
        store(2 + c, high[2 + c] + ratio * (low[2 + c] + passed * high[c]))
    num, den, tail, _ = climb(spectral, one, one, high_u[::-1], high_l[::-1])
    passed = tail / den
    _, den_all, _, product = climb(spectral, num, den, low_u[::-1], low_l[::-1])
    ratio = product * den / den_all
    for c in range(2):
        store(c, low[c] + ratio * (high[c] + passed * low[2 + c]))


def final_kernel(sizes, pairs, spectral_ref, table_ref, side_ref, *rest):
    rows, kx_total, kx_count, tiles, mode_count, height = sizes
    chips = mode_count // 2
    total = mode_count * height
    port = 4 * height
    pair_refs, rest = rest[: chips - 1], rest[chips - 1 :]
    messages, rest = rest[: pairs - 1], rest[pairs - 1 :]
    sources, rest = rest[:mode_count], rest[mode_count:]
    out_hbm, out_ref, factor_ref, partial_ref, sems = rest
    me, partition = lax.axis_index("modes"), lax.axis_index("gz")
    upside, level = partition % 2 == 1, partition // 2
    spectral = spectral_ref[...]
    one = jnp.ones((total, LANES), jnp.float32)
    zero = jnp.zeros((total, LANES), jnp.float32)
    start = (one, zero, zero, zero)

    def enter(state, ports, entry, leave, near, far):
        grown, passed, *partial = state
        num, den, tail, product = climb(spectral, grown, one, near, far)
        inverse = 1.0 / den
        ratio = product * inverse
        new = [ports(leave + c) + ratio * (partial[c] + passed * ports(entry + c)) for c in range(2)]
        return (num * inverse, tail * inverse, *new)

    def up(state, ports, table, blocks):
        near = [v for b in blocks for v in couplings(table, 2 * b, rows)]
        far = [v for b in blocks for v in couplings(table, 2 * b + 1, rows)]
        return enter(state, ports, 0, 2, near, far)

    def down(state, ports, table, blocks):
        near = [v for b in blocks for v in couplings(table, 2 * b + 1, rows)]
        far = [v for b in blocks for v in couplings(table, 2 * b, rows)]
        return enter(state, ports, 2, 0, near[::-1], far[::-1])

    def of_message(d):
        ref = messages[d - 1]
        return (lambda i: ref[i * total : (i + 1) * total, :]), ref[4 * total :, :], (0, 1)

    def pair_chunk(d, at):
        at += (d % 2) * port
        ref = side_ref if d < 2 else pair_refs[d // 2 - 1]
        return ref[at : at + height, :]

    def of_pair():
        def ports(i):
            return jnp.concatenate([pair_chunk(d, i * height) for d in range(mode_count)], axis=0)

        return ports, side_ref[2 * port :, :], (0,)

    below, above = start, start
    for d in range(pairs - 1, 0, -1):
        below = lax.cond(level >= d, lambda s, d=d: up(s, *of_message(d)), lambda s: s, below)
    for d in range(1, pairs):
        above = lax.cond(level < d, lambda s, d=d: down(s, *of_message(d)), lambda s: s, above)
    below = lax.cond(upside, lambda s: up(s, *of_pair()), lambda s: s, below)
    above = lax.cond(upside, lambda s: s, lambda s: down(s, *of_pair()), above)

    table = table_ref[...]
    lower, upper = couplings(table, 0, rows), couplings(table, 1, rows)
    grown, _, *partial = below
    for k in range(rows):
        held = spectral + lower[k] * grown
        inverse = 1.0 / (upper[k] + held)
        factor = upper[k] * inverse
        grown = held * inverse
        factor_ref[k] = factor
        for c in range(2):
            source = jnp.concatenate([sources[d][k, c] for d in range(mode_count)], axis=0)
            partial[c] = (source + lower[k] * partial[c]) * inverse
            partial_ref[k, c] = partial[c]
    inverse = 1.0 / (grown + factor * above[0])
    value = [(partial[c] + factor * above[2 + c]) * inverse for c in range(2)]
    chunks = {first: (i, size) for i, (first, size) in enumerate(chunks_of(rows))}
    copies = []
    for k in range(rows - 1, -1, -1):
        for c in range(2):
            if k < rows - 1:
                value[c] = partial_ref[k, c] + factor_ref[k] * value[c]
            for d in range(mode_count):
                out_ref[k, c, me ^ d] = value[c][d * height : (d + 1) * height]
        if k in chunks:
            i, size = chunks[k]
            copies.append(pltpu.make_async_copy(out_ref.at[pl.ds(k, size)], out_hbm.at[pl.ds(k, size)], sems.at[i]))
            copies[-1].start()
    for copy in copies:
        copy.wait()


SMEM = pl.BlockSpec(memory_space=pltpu.SMEM)
VMEM = pl.BlockSpec(memory_space=pltpu.VMEM)
ANY = pl.BlockSpec(memory_space=pl.ANY)


def near(*arrays):
    return [pltpu.with_memory_space_constraint(a, pltpu.VMEM) for a in arrays]


def per_device(source_field, coupling_below, coupling_above, eigen_stream, eigen_span):
    sizes = rows, kx_total, kx_count, tiles, mode_count, height = sizes_of(source_field)
    partitions = lax.axis_size("gz")
    chips, pairs = mode_count // 2, partitions // 2
    total = mode_count * height
    f32 = jnp.float32
    chunk_sems = pltpu.SemaphoreType.DMA((len(chunks_of(rows)),))

    def move(array, modes_by=0, pair=0, level=0):
        links = []
        for m in range(mode_count):
            for g in range(partitions):
                to = ((g // 2 + level) % pairs) * 2 + ((g % 2) ^ pair)
                links.append((m * partitions + g, (m ^ modes_by) * partitions + to))
        return lax.ppermute(array, ("modes", "gz"), links)

    ports, table, spectral = pl.pallas_call(
        functools.partial(reduce_kernel, sizes),
        out_shape=(
            pltpu.VMEM((2, chips, 4 * height, LANES), f32),
            pltpu.VMEM((SUBLANES, LANES), f32),
            pltpu.VMEM((total, LANES), f32),
        ),
        in_specs=[SMEM, SMEM, SMEM, VMEM, ANY],
        out_specs=(VMEM, VMEM, VMEM),
        scratch_shapes=[pltpu.VMEM(source_field.shape, f32), chunk_sems],
        name="reduce",
    )(coupling_below, coupling_above, eigen_stream, eigen_span.reshape(-1, LANES), source_field)
    blocks = pl.pallas_call(
        functools.partial(regroup_kernel, sizes),
        out_shape=pltpu.VMEM((mode_count, rows, 2, height, LANES), f32),
        in_specs=[ANY],
        out_specs=VMEM,
        scratch_shapes=[pltpu.VMEM(source_field.shape, f32), chunk_sems],
        name="regroup",
    )(source_field)

    taken = move(ports[1], modes_by=1)
    side = move(jnp.concatenate([ports[0, 0], taken[0], table], axis=0), pair=1)
    own_parts, pair_parts = [], []
    for d in range(1, chips):
        block = jnp.concatenate([ports[0, d], taken[d]], axis=0)
        own_parts.append(move(block, modes_by=2 * d))
        pair_parts.append(move(block, modes_by=2 * d, pair=1))
    message = pl.pallas_call(
        functools.partial(merge_kernel, sizes),
        out_shape=pltpu.VMEM((4 * total + SUBLANES, LANES), f32),
        in_specs=[VMEM] * (5 + 2 * (chips - 1)),
        out_specs=VMEM,
        name="merge",
    )(*near(spectral, table, ports, taken, side, *own_parts, *pair_parts))
    messages = [move(message, level=d) for d in range(1, pairs)]
    sources = [move(blocks[d], modes_by=d) if d else blocks[0] for d in range(mode_count)]
    out = pl.pallas_call(
        functools.partial(final_kernel, sizes, pairs),
        out_shape=jax.ShapeDtypeStruct((rows, 2, mode_count, height, LANES), f32),
        in_specs=[VMEM] * (3 + (chips - 1) + (pairs - 1) + mode_count),
        out_specs=ANY,
        scratch_shapes=[
            pltpu.VMEM((rows, 2, mode_count, height, LANES), f32),
            pltpu.VMEM((rows, total, LANES), f32),
            pltpu.VMEM((rows, 2, total, LANES), f32),
            chunk_sems,
        ],
        name="solve",
    )(*near(spectral, table, side, *pair_parts, *messages, *sources))
    out = out.reshape(rows, 2, mode_count * tiles, kx_count, LANES).transpose(0, 1, 3, 2, 4)
    return out.reshape(rows, 2, kx_count, -1)


def solution(mesh):
    in_specs = (P("gz", None, None, "modes"), P("gz"), P("gz"), P(), P())
    out_specs = P("gz", None, "modes", None)
    return jax.shard_map(
        per_device, mesh=mesh, in_specs=in_specs, out_specs=out_specs, check_vma=False
    )
```

```python
import functools

import jax
import jax.numpy as jnp
from jax import lax
from jax.experimental import pallas as pl
from jax.experimental.pallas import tpu as pltpu
from jax.sharding import PartitionSpec as P


LANES = 128
SUBLANES = 8


def sizes_of(source_field):
    rows, _, kx_total, ky_local = source_field.shape
    mode_count = lax.axis_size("modes")
    kx_count, tiles = kx_total // mode_count, ky_local // LANES
    return rows, kx_total, kx_count, tiles, mode_count, kx_count * tiles


def chunks_of(rows):
    size = rows // 4 if rows % 4 == 0 else rows
    return [(first, size) for first in range(0, rows, size)]


def reduce_kernel(sizes, below_ref, above_ref, stream_ref, span_ref, source_hbm, ports_ref, table_ref, spectral_ref, source_ref, sems):
    rows, kx_total, kx_count, tiles, mode_count, height = sizes
    me, partition = lax.axis_index("modes"), lax.axis_index("gz")
    copies = []
    for i, (first, size) in enumerate(chunks_of(rows)):
        copies.append(
            pltpu.make_async_copy(source_hbm.at[pl.ds(first, size)], source_ref.at[pl.ds(first, size)], sems.at[i])
        )
        copies[-1].start()
    lower = [below_ref[k] for k in range(rows)]
    upper = [above_ref[k] for k in range(rows)]
    lower[0] = jnp.where(partition == 0, 0.0, lower[0])
    upper[-1] = jnp.where(partition == lax.axis_size("gz") - 1, 0.0, upper[-1])
    lane = lax.broadcasted_iota(jnp.int32, (SUBLANES, LANES), 1)
    sub = lax.broadcasted_iota(jnp.int32, (SUBLANES, LANES), 0)
    table = jnp.zeros((SUBLANES, LANES), jnp.float32)
    for k in range(rows):
        table = jnp.where(lane == k, jnp.where(sub == 0, lower[k], upper[k]), table)
    table_ref[...] = table
    for d in range(mode_count):
        for t in range(tiles):
            spanwise = span_ref[pl.ds((me ^ d) * tiles + t, 1), :]
            for j in range(kx_count):
                at = d * height + t * kx_count + j
                spectral_ref[at : at + 1, :] = spanwise + stream_ref[me * kx_count + j]
    shape = (kx_total, LANES)
    kx_at = lax.broadcasted_iota(jnp.int32, shape, 0)
    streamwise = jnp.zeros(shape, jnp.float32)
    for i in range(kx_total):
        streamwise = jnp.where(kx_at == i, stream_ref[i], streamwise)
    each = range(tiles)
    spectral = [streamwise + span_ref[pl.ds(me * tiles + t, 1), :] for t in each]
    one, zero = jnp.ones(shape, jnp.float32), jnp.zeros(shape, jnp.float32)
    grown, passed = [one] * tiles, [one] * tiles
    partial = [[zero] * tiles, [zero] * tiles]
    first_value = [[zero] * tiles, [zero] * tiles]
    starts = {first: i for i, (first, _) in enumerate(chunks_of(rows))}
    for k in range(rows):
        if k in starts:
            copies[starts[k]].wait()
        for t in each:
            held = spectral[t] + lower[k] * grown[t]
            inverse = 1.0 / (upper[k] + held)
            grown[t] = held * inverse
            for c in range(2):
                source = source_ref[k, c, :, t * LANES : (t + 1) * LANES]
                partial[c][t] = (source + lower[k] * partial[c][t]) * inverse
                first_value[c][t] = first_value[c][t] + passed[t] * partial[c][t]
            passed[t] = passed[t] * (upper[k] * inverse)
    values = first_value + partial
    for dest in range(mode_count):
        to = dest ^ me
        for i in range(4):
            for t in each:
                at = i * height + t * kx_count
                ports_ref[to % 2, to // 2, at : at + kx_count, :] = values[i][t][dest * kx_count : (dest + 1) * kx_count]


def regroup_kernel(sizes, source_hbm, blocks_ref, source_ref, sems):
    rows, _, kx_count, tiles, mode_count, _ = sizes
    me = lax.axis_index("modes")
    copies = []
    for i, (first, size) in enumerate(chunks_of(rows)):
        copies.append(
            pltpu.make_async_copy(source_hbm.at[pl.ds(first, size)], source_ref.at[pl.ds(first, size)], sems.at[i])
        )
        copies[-1].start()
    for i, (first, size) in enumerate(chunks_of(rows)):
        copies[i].wait()
        for k in range(first, first + size):
            for c in range(2):
                for t in range(tiles):
                    at = t * kx_count
                    for dest in range(mode_count):
                        blocks_ref[dest ^ me, k, c, at : at + kx_count, :] = source_ref[
                            k, c, dest * kx_count : (dest + 1) * kx_count, t * LANES : (t + 1) * LANES
                        ]


def climb(spectral, num, den, near, far):
    product = near[0]
    for k in range(len(near)):
        num = spectral * den + near[k] * num
        before = den
        den = num + far[k] * den
        if k:
            product = product * near[k]
    return num, den, far[-1] * before, product


def couplings(table, line, rows):
    return [table[line : line + 1, k : k + 1] for k in range(rows)]


def merge_kernel(sizes, spectral_ref, table_ref, ports_ref, taken_ref, side_ref, *rest):
    rows, _, _, _, mode_count, height = sizes
    chips = mode_count // 2
    own_refs, pair_refs, message_ref = rest[: chips - 1], rest[chips - 1 : 2 * (chips - 1)], rest[-1]
    total = mode_count * height
    port = 4 * height
    upside = lax.axis_index("gz") % 2 == 1

    def gather(i, chunk):
        return jnp.concatenate([chunk(d, i * height) for d in range(mode_count)], axis=0)

    def own_chunk(d, at):
        if d >= 2:
            start = (d % 2) * port + at
            return own_refs[d // 2 - 1][start : start + height, :]
        return ports_ref[0, 0, at : at + height, :] if d == 0 else taken_ref[0, at : at + height, :]

    def pair_chunk(d, at):
        start = (d % 2) * port + at
        ref = side_ref if d < 2 else pair_refs[d // 2 - 1]
        return ref[start : start + height, :]

    own_table, pair_table = table_ref[...], side_ref[2 * port :, :]
    low_table = jnp.where(upside, pair_table, own_table)
    high_table = jnp.where(upside, own_table, pair_table)
    sub = lax.broadcasted_iota(jnp.int32, (SUBLANES, LANES), 0)
    message_ref[4 * total :, :] = jnp.where(sub < 2, low_table, pltpu.roll(high_table, 2, 0))
    spectral = spectral_ref[...]
    one = jnp.ones((total, LANES), jnp.float32)
    own = [gather(i, own_chunk) for i in range(4)]
    pair = [gather(i, pair_chunk) for i in range(4)]
    low = [jnp.where(upside, b, a) for a, b in zip(own, pair)]
    high = [jnp.where(upside, a, b) for a, b in zip(own, pair)]
    low_l, low_u = couplings(low_table, 0, rows), couplings(low_table, 1, rows)
    high_l, high_u = couplings(high_table, 0, rows), couplings(high_table, 1, rows)

    def store(i, value):
        message_ref[i * total : (i + 1) * total, :] = value

    num, den, tail, _ = climb(spectral, one, one, low_l, low_u)
    passed = tail / den
    _, den_all, _, product = climb(spectral, num, den, high_l, high_u)
    ratio = product * den / den_all
    for c in range(2):
        store(2 + c, high[2 + c] + ratio * (low[2 + c] + passed * high[c]))
    num, den, tail, _ = climb(spectral, one, one, high_u[::-1], high_l[::-1])
    passed = tail / den
    _, den_all, _, product = climb(spectral, num, den, low_u[::-1], low_l[::-1])
    ratio = product * den / den_all
    for c in range(2):
        store(c, low[c] + ratio * (high[c] + passed * low[2 + c]))


def final_kernel(sizes, pairs, spectral_ref, table_ref, side_ref, *rest):
    rows, _, _, _, mode_count, height = sizes
    chips = mode_count // 2
    total = mode_count * height
    port = 4 * height
    pair_refs, rest = rest[: chips - 1], rest[chips - 1 :]
    messages, rest = rest[: pairs - 1], rest[pairs - 1 :]
    sources, rest = rest[:mode_count], rest[mode_count:]
    out_hbm, out_ref, factor_ref, partial_ref, sems = rest
    me, partition = lax.axis_index("modes"), lax.axis_index("gz")
    upside, level = partition % 2 == 1, partition // 2
    spectral = spectral_ref[...]
    one = jnp.ones((total, LANES), jnp.float32)
    zero = jnp.zeros((total, LANES), jnp.float32)
    start = (one, zero, zero, zero)

    def enter(state, ports, entry, leave, near, far):
        grown, passed, *partial = state
        num, den, tail, product = climb(spectral, grown, one, near, far)
        inverse = 1.0 / den
        ratio = product * inverse
        new = [ports(leave + c) + ratio * (partial[c] + passed * ports(entry + c)) for c in range(2)]
        return (num * inverse, tail * inverse, *new)

    def up(state, ports, table, blocks):
        near = [v for b in blocks for v in couplings(table, 2 * b, rows)]
        far = [v for b in blocks for v in couplings(table, 2 * b + 1, rows)]
        return enter(state, ports, 0, 2, near, far)

    def down(state, ports, table, blocks):
        near = [v for b in blocks for v in couplings(table, 2 * b + 1, rows)]
        far = [v for b in blocks for v in couplings(table, 2 * b, rows)]
        return enter(state, ports, 2, 0, near[::-1], far[::-1])

    def of_message(d):
        ref = messages[d - 1]
        return (lambda i: ref[i * total : (i + 1) * total, :]), ref[4 * total :, :], (0, 1)

    def pair_chunk(d, at):
        at += (d % 2) * port
        ref = side_ref if d < 2 else pair_refs[d // 2 - 1]
        return ref[at : at + height, :]

    def of_pair():
        def ports(i):
            return jnp.concatenate([pair_chunk(d, i * height) for d in range(mode_count)], axis=0)

        return ports, side_ref[2 * port :, :], (0,)

    below, above = start, start
    for d in range(pairs - 1, 0, -1):
        below = lax.cond(level >= d, lambda s, d=d: up(s, *of_message(d)), lambda s: s, below)
    for d in range(1, pairs):
        above = lax.cond(level < d, lambda s, d=d: down(s, *of_message(d)), lambda s: s, above)
    below = lax.cond(upside, lambda s: up(s, *of_pair()), lambda s: s, below)
    above = lax.cond(upside, lambda s: s, lambda s: down(s, *of_pair()), above)

    table = table_ref[...]
    lower, upper = couplings(table, 0, rows), couplings(table, 1, rows)
    grown, _, *partial = below
    for k in range(rows):
        held = spectral + lower[k] * grown
        inverse = 1.0 / (upper[k] + held)
        factor = upper[k] * inverse
        grown = held * inverse
        factor_ref[k] = factor
        for c in range(2):
            source = jnp.concatenate([sources[d][k, c] for d in range(mode_count)], axis=0)
            partial[c] = (source + lower[k] * partial[c]) * inverse
            partial_ref[k, c] = partial[c]
    inverse = 1.0 / (grown + factor * above[0])
    value = [(partial[c] + factor * above[2 + c]) * inverse for c in range(2)]
    chunks = {first: (i, size) for i, (first, size) in enumerate(chunks_of(rows))}
    copies = []
    for k in range(rows - 1, -1, -1):
        for c in range(2):
            if k < rows - 1:
                value[c] = partial_ref[k, c] + factor_ref[k] * value[c]
            for d in range(mode_count):
                out_ref[k, c, me ^ d] = value[c][d * height : (d + 1) * height]
        if k in chunks:
            i, size = chunks[k]
            copies.append(pltpu.make_async_copy(out_ref.at[pl.ds(k, size)], out_hbm.at[pl.ds(k, size)], sems.at[i]))
            copies[-1].start()
    for copy in copies:
        copy.wait()


SMEM = pl.BlockSpec(memory_space=pltpu.SMEM)
VMEM = pl.BlockSpec(memory_space=pltpu.VMEM)
ANY = pl.BlockSpec(memory_space=pl.ANY)


def near(*arrays):
    return [pltpu.with_memory_space_constraint(a, pltpu.VMEM) for a in arrays]


def solve(source_field, coupling_below, coupling_above, eigen_stream, eigen_span):
    sizes = rows, kx_total, kx_count, tiles, mode_count, height = sizes_of(source_field)
    partitions = lax.axis_size("gz")
    chips, pairs = mode_count // 2, partitions // 2
    total = mode_count * height
    f32 = jnp.float32
    chunk_sems = pltpu.SemaphoreType.DMA((len(chunks_of(rows)),))

    def move(array, modes_by=0, pair=0, level=0):
        links = []
        for m in range(mode_count):
            for g in range(partitions):
                to = ((g // 2 + level) % pairs) * 2 + ((g % 2) ^ pair)
                links.append((m * partitions + g, (m ^ modes_by) * partitions + to))
        return lax.ppermute(array, ("modes", "gz"), links)

    ports, table, spectral = pl.pallas_call(
        functools.partial(reduce_kernel, sizes),
        out_shape=(
            pltpu.VMEM((2, chips, 4 * height, LANES), f32),
            pltpu.VMEM((SUBLANES, LANES), f32),
            pltpu.VMEM((total, LANES), f32),
        ),
        in_specs=[SMEM, SMEM, SMEM, VMEM, ANY],
        out_specs=(VMEM, VMEM, VMEM),
        scratch_shapes=[pltpu.VMEM(source_field.shape, f32), chunk_sems],
        name="reduce",
    )(coupling_below, coupling_above, eigen_stream, eigen_span.reshape(-1, LANES), source_field)
    blocks = pl.pallas_call(
        functools.partial(regroup_kernel, sizes),
        out_shape=pltpu.VMEM((mode_count, rows, 2, height, LANES), f32),
        in_specs=[ANY],
        out_specs=VMEM,
        scratch_shapes=[pltpu.VMEM(source_field.shape, f32), chunk_sems],
        name="regroup",
    )(source_field)

    taken = move(ports[1], modes_by=1)
    own_parts, pair_parts = [], []
    for d in range(1, chips):
        block = jnp.concatenate([ports[0, d], taken[d]], axis=0)
        pair_parts.append(move(block, modes_by=2 * d, pair=1))
        own_parts.append(move(block, modes_by=2 * d))
    side = move(jnp.concatenate([ports[0, 0], taken[0], table], axis=0), pair=1)
    message = pl.pallas_call(
        functools.partial(merge_kernel, sizes),
        out_shape=pltpu.VMEM((4 * total + SUBLANES, LANES), f32),
        in_specs=[VMEM] * (5 + 2 * (chips - 1)),
        out_specs=VMEM,
        name="merge",
    )(*near(spectral, table, ports, taken, side, *own_parts, *pair_parts))
    messages = [move(message, level=d) for d in range(1, pairs)]
    sources = [move(blocks[d], modes_by=d) if d else blocks[0] for d in range(mode_count)]
    out = pl.pallas_call(
        functools.partial(final_kernel, sizes, pairs),
        out_shape=jax.ShapeDtypeStruct((rows, 2, mode_count, height, LANES), f32),
        in_specs=[VMEM] * (3 + (chips - 1) + (pairs - 1) + mode_count),
        out_specs=ANY,
        scratch_shapes=[
            pltpu.VMEM((rows, 2, mode_count, height, LANES), f32),
            pltpu.VMEM((rows, total, LANES), f32),
            pltpu.VMEM((rows, 2, total, LANES), f32),
            chunk_sems,
        ],
        name="solve",
    )(*near(spectral, table, side, *pair_parts, *messages, *sources))
    out = out.reshape(rows, 2, mode_count * tiles, kx_count, LANES).transpose(0, 1, 3, 2, 4)
    return out.reshape(rows, 2, kx_count, -1)


def solution(mesh):
    in_specs = (P("gz", None, None, "modes"), P("gz"), P("gz"), P(), P())
    out_specs = P("gz", None, "modes", None)
    return jax.shard_map(solve, mesh=mesh, in_specs=in_specs, out_specs=out_specs, check_vma=False)
```

```python
import functools

import jax
import jax.numpy as jnp
from jax import lax
from jax.experimental import pallas as pl
from jax.experimental.pallas import tpu as pltpu
from jax.sharding import PartitionSpec as P


LANES = 128
SUBLANES = 8


def sizes_of(source_field):
    rows, _, kx_total, ky_local = source_field.shape
    mode_count = lax.axis_size("modes")
    kx_count, tiles = kx_total // mode_count, ky_local // LANES
    return rows, kx_total, kx_count, tiles, mode_count, kx_count * tiles


def chunks_of(rows):
    size = rows // 4 if rows % 4 == 0 else rows
    return [(first, size) for first in range(0, rows, size)]


def fetch(pairs, sems):
    copies = [pltpu.make_async_copy(source, to, sems.at[i]) for i, (source, to) in enumerate(pairs)]
    for copy in copies:
        copy.start()
    return copies


def reduce_kernel(
    sizes, below_hbm, above_hbm, stream_hbm, span_hbm, source_hbm,
    ports_ref, table_ref, spectral_ref, source_ref, below_ref, above_ref, stream_ref, span_ref, small_sems, sems,
):
    rows, kx_total, kx_count, tiles, mode_count, height = sizes
    me, partition = lax.axis_index("modes"), lax.axis_index("gz")
    small = fetch(
        [(below_hbm, below_ref), (above_hbm, above_ref), (stream_hbm, stream_ref), (span_hbm, span_ref)], small_sems
    )
    parts = [pl.ds(first, size) for first, size in chunks_of(rows)]
    copies = fetch([(source_hbm.at[p], source_ref.at[p]) for p in parts], sems)
    for copy in small:
        copy.wait()
    lower = [below_ref[k] for k in range(rows)]
    upper = [above_ref[k] for k in range(rows)]
    lower[0] = jnp.where(partition == 0, 0.0, lower[0])
    upper[-1] = jnp.where(partition == lax.axis_size("gz") - 1, 0.0, upper[-1])
    lane = lax.broadcasted_iota(jnp.int32, (SUBLANES, LANES), 1)
    sub = lax.broadcasted_iota(jnp.int32, (SUBLANES, LANES), 0)
    table = jnp.zeros((SUBLANES, LANES), jnp.float32)
    for k in range(rows):
        table = jnp.where(lane == k, jnp.where(sub == 0, lower[k], upper[k]), table)
    table_ref[...] = table
    for d in range(mode_count):
        for t in range(tiles):
            spanwise = span_ref[pl.ds((me ^ d) * tiles + t, 1), :]
            for j in range(kx_count):
                at = d * height + t * kx_count + j
                spectral_ref[at : at + 1, :] = spanwise + stream_ref[me * kx_count + j]
    shape = (kx_total, LANES)
    kx_at = lax.broadcasted_iota(jnp.int32, shape, 0)
    streamwise = jnp.zeros(shape, jnp.float32)
    for i in range(kx_total):
        streamwise = jnp.where(kx_at == i, stream_ref[i], streamwise)
    each = range(tiles)
    spectral = [streamwise + span_ref[pl.ds(me * tiles + t, 1), :] for t in each]
    one, zero = jnp.ones(shape, jnp.float32), jnp.zeros(shape, jnp.float32)
    grown, passed = [one] * tiles, [one] * tiles
    partial = [[zero] * tiles, [zero] * tiles]
    first_value = [[zero] * tiles, [zero] * tiles]
    starts = {first: i for i, (first, _) in enumerate(chunks_of(rows))}
    for k in range(rows):
        if k in starts:
            copies[starts[k]].wait()
        for t in each:
            held = spectral[t] + lower[k] * grown[t]
            inverse = 1.0 / (upper[k] + held)
            grown[t] = held * inverse
            for c in range(2):
                source = source_ref[k, c, :, t * LANES : (t + 1) * LANES]
                partial[c][t] = (source + lower[k] * partial[c][t]) * inverse
                first_value[c][t] = first_value[c][t] + passed[t] * partial[c][t]
            passed[t] = passed[t] * (upper[k] * inverse)
    values = first_value + partial
    for dest in range(mode_count):
        to = dest ^ me
        for i in range(4):
            for t in each:
                at = i * height + t * kx_count
                ports_ref[to % 2, to // 2, at : at + kx_count, :] = values[i][t][dest * kx_count : (dest + 1) * kx_count]


def regroup_kernel(sizes, source_ref, blocks_ref):
    rows, _, kx_count, tiles, mode_count, _ = sizes
    me = lax.axis_index("modes")
    for dest in range(mode_count):
        to = dest ^ me
        lines = slice(dest * kx_count, (dest + 1) * kx_count)
        for k in range(rows):
            for c in range(2):
                for t in range(tiles):
                    at = t * kx_count
                    blocks_ref[to, k, c, at : at + kx_count, :] = source_ref[k, c, lines, t * LANES : (t + 1) * LANES]


def climb(spectral, num, den, near, far):
    product = near[0]
    for k in range(len(near)):
        num = spectral * den + near[k] * num
        before = den
        den = num + far[k] * den
        if k:
            product = product * near[k]
    return num, den, far[-1] * before, product


def couplings(table, line, rows):
    return [table[line : line + 1, k : k + 1] for k in range(rows)]


def merge_kernel(sizes, spectral_ref, table_ref, ports_ref, taken_ref, side_ref, *rest):
    rows, _, _, _, mode_count, height = sizes
    chips = mode_count // 2
    own_refs, pair_refs, message_ref = rest[: chips - 1], rest[chips - 1 : 2 * (chips - 1)], rest[-1]
    total = mode_count * height
    port = 4 * height
    upside = lax.axis_index("gz") % 2 == 1

    def gather(i, chunk):
        return jnp.concatenate([chunk(d, i * height) for d in range(mode_count)], axis=0)

    def own_chunk(d, at):
        if d >= 2:
            start = (d % 2) * port + at
            return own_refs[d // 2 - 1][start : start + height, :]
        return ports_ref[0, 0, at : at + height, :] if d == 0 else taken_ref[0, at : at + height, :]

    def pair_chunk(d, at):
        start = (d % 2) * port + at
        ref = side_ref if d < 2 else pair_refs[d // 2 - 1]
        return ref[start : start + height, :]

    own_table, pair_table = table_ref[...], side_ref[2 * port :, :]
    low_table = jnp.where(upside, pair_table, own_table)
    high_table = jnp.where(upside, own_table, pair_table)
    sub = lax.broadcasted_iota(jnp.int32, (SUBLANES, LANES), 0)
    message_ref[4 * total :, :] = jnp.where(sub < 2, low_table, pltpu.roll(high_table, 2, 0))
    spectral = spectral_ref[...]
    one = jnp.ones((total, LANES), jnp.float32)
    own = [gather(i, own_chunk) for i in range(4)]
    pair = [gather(i, pair_chunk) for i in range(4)]
    low = [jnp.where(upside, b, a) for a, b in zip(own, pair)]
    high = [jnp.where(upside, a, b) for a, b in zip(own, pair)]
    low_l, low_u = couplings(low_table, 0, rows), couplings(low_table, 1, rows)
    high_l, high_u = couplings(high_table, 0, rows), couplings(high_table, 1, rows)

    def store(i, value):
        message_ref[i * total : (i + 1) * total, :] = value

    num, den, tail, _ = climb(spectral, one, one, low_l, low_u)
    passed = tail / den
    _, den_all, _, product = climb(spectral, num, den, high_l, high_u)
    ratio = product * den / den_all
    for c in range(2):
        store(2 + c, high[2 + c] + ratio * (low[2 + c] + passed * high[c]))
    num, den, tail, _ = climb(spectral, one, one, high_u[::-1], high_l[::-1])
    passed = tail / den
    _, den_all, _, product = climb(spectral, num, den, low_u[::-1], low_l[::-1])
    ratio = product * den / den_all
    for c in range(2):
        store(c, low[c] + ratio * (high[c] + passed * low[2 + c]))


def prepare_kernel(sizes, spectral_ref, table_ref, *rest):
    rows, _, _, _, mode_count, _ = sizes
    sources, (part_ref, low_ref, high_ref) = rest[:mode_count], rest[mode_count:]
    spectral, table = spectral_ref[...], table_ref[...]
    lower, upper = couplings(table, 0, rows), couplings(table, 1, rows)
    grown = jnp.ones(spectral.shape, jnp.float32)
    carried = grown
    partial = [jnp.zeros(spectral.shape, jnp.float32)] * 2
    for k in range(rows):
        held = spectral + lower[k] * grown
        inverse = 1.0 / (upper[k] + held)
        grown = held * inverse
        scaled = lower[k] * inverse
        carried = scaled * carried
        low_ref[k] = carried
        high_ref[k] = upper[k] * inverse
        for c in range(2):
            source = jnp.concatenate([sources[d][k, c] for d in range(mode_count)], axis=0)
            partial[c] = source * inverse + scaled * partial[c]
            part_ref[k, c] = partial[c]
    low, high = low_ref[rows - 1], high_ref[rows - 1]
    for k in range(rows - 2, -1, -1):
        factor = high_ref[k]
        low = low_ref[k] + factor * low
        low_ref[k] = low
        high = factor * high
        high_ref[k] = high
        for c in range(2):
            partial[c] = part_ref[k, c] + factor * partial[c]
            part_ref[k, c] = partial[c]


def final_kernel(sizes, pairs, spectral_ref, table_ref, side_ref, part_ref, low_ref, high_ref, *rest):
    rows, _, _, _, mode_count, height = sizes
    chips = mode_count // 2
    total = mode_count * height
    port = 4 * height
    pair_refs, rest = rest[: chips - 1], rest[chips - 1 :]
    messages, rest = rest[: pairs - 1], rest[pairs - 1 :]
    out_hbm, out_ref, level_ref, sems = rest
    me, partition = lax.axis_index("modes"), lax.axis_index("gz")
    upside, level = partition % 2 == 1, partition // 2
    for d in range(1, pairs):
        level_ref[level ^ d] = messages[d - 1][...]
    spectral = spectral_ref[...]
    one = jnp.ones((total, LANES), jnp.float32)
    zero = jnp.zeros((total, LANES), jnp.float32)
    start = (one, zero, zero, zero)

    def enter(state, ports, entry, leave, near, far):
        grown, passed, *partial = state
        num, den, tail, product = climb(spectral, grown, one, near, far)
        inverse = 1.0 / den
        ratio = product * inverse
        new = [ports(leave + c) + ratio * (partial[c] + passed * ports(entry + c)) for c in range(2)]
        return (num * inverse, tail * inverse, *new)

    def up(state, ports, table, blocks):
        near = [v for b in blocks for v in couplings(table, 2 * b, rows)]
        far = [v for b in blocks for v in couplings(table, 2 * b + 1, rows)]
        return enter(state, ports, 0, 2, near, far)

    def down(state, ports, table, blocks):
        near = [v for b in blocks for v in couplings(table, 2 * b + 1, rows)]
        far = [v for b in blocks for v in couplings(table, 2 * b, rows)]
        return enter(state, ports, 2, 0, near[::-1], far[::-1])

    def of_level(at):
        return (lambda i: level_ref[at, i * total : (i + 1) * total, :]), level_ref[at, 4 * total :, :], (0, 1)

    def pair_chunk(d, at):
        at += (d % 2) * port
        ref = side_ref if d < 2 else pair_refs[d // 2 - 1]
        return ref[at : at + height, :]

    def of_pair():
        def ports(i):
            return jnp.concatenate([pair_chunk(d, i * height) for d in range(mode_count)], axis=0)

        return ports, side_ref[2 * port :, :], (0,)

    def of_own():
        return (lambda i: part_ref[0 if i < 2 else rows - 1, i % 2]), table_ref[...], (0,)

    below, above = start, start
    for at in range(pairs - 1):
        below = lax.cond(at < level, lambda s, at=at: up(s, *of_level(at)), lambda s: s, below)
    for at in range(pairs - 1, 0, -1):
        above = lax.cond(at > level, lambda s, at=at: down(s, *of_level(at)), lambda s: s, above)
    below, above = lax.cond(
        upside, lambda b, a: (up(b, *of_pair()), a), lambda b, a: (b, down(a, *of_pair())), below, above
    )
    leaving_up, leaving_down = up(below, *of_own()), down(above, *of_own())
    inverse_up = 1.0 / (leaving_up[0] + leaving_up[1] * above[0])
    inverse_down = 1.0 / (leaving_down[0] + leaving_down[1] * below[0])
    under, over = [], []
    for c in range(2, 4):
        last = (leaving_up[c] + leaving_up[1] * above[c]) * inverse_up
        over.append(above[c] + above[1] * last)
        first = (leaving_down[c] + leaving_down[1] * below[c]) * inverse_down
        under.append(below[c] + below[1] * first)
    copies = []
    for i, (first, size) in enumerate(chunks_of(rows)):
        for k in range(first, first + size):
            low, high = low_ref[k], high_ref[k]
            for c in range(2):
                value = part_ref[k, c] + low * under[c] + high * over[c]
                for d in range(mode_count):
                    out_ref[k, c, me ^ d] = value[d * height : (d + 1) * height]
        part = pl.ds(first, size)
        copies.append(pltpu.make_async_copy(out_ref.at[part], out_hbm.at[part], sems.at[i]))
        copies[-1].start()
    for copy in copies:
        copy.wait()


VMEM = pl.BlockSpec(memory_space=pltpu.VMEM)
ANY = pl.BlockSpec(memory_space=pl.ANY)


def near(*arrays):
    return [pltpu.with_memory_space_constraint(a, pltpu.VMEM) for a in arrays]


def solve(source_field, coupling_below, coupling_above, eigen_stream, eigen_span):
    sizes = rows, kx_total, kx_count, tiles, mode_count, height = sizes_of(source_field)
    partitions = lax.axis_size("gz")
    chips, pairs = mode_count // 2, partitions // 2
    total = mode_count * height
    f32 = jnp.float32
    chunk_sems = pltpu.SemaphoreType.DMA((len(chunks_of(rows)),))

    def move(array, modes_by=0, pair=0, level=0):
        links = []
        for m in range(mode_count):
            for g in range(partitions):
                to = ((g // 2) ^ level) * 2 + ((g % 2) ^ pair)
                links.append((m * partitions + g, (m ^ modes_by) * partitions + to))
        return lax.ppermute(array, ("modes", "gz"), links)

    span = eigen_span.reshape(-1, LANES)
    ports, table, spectral, source = pl.pallas_call(
        functools.partial(reduce_kernel, sizes),
        out_shape=(
            pltpu.VMEM((2, chips, 4 * height, LANES), f32),
            pltpu.VMEM((SUBLANES, LANES), f32),
            pltpu.VMEM((total, LANES), f32),
            pltpu.VMEM(source_field.shape, f32),
        ),
        in_specs=[ANY] * 5,
        out_specs=(VMEM,) * 4,
        scratch_shapes=[
            pltpu.SMEM(coupling_below.shape, f32),
            pltpu.SMEM(coupling_above.shape, f32),
            pltpu.SMEM(eigen_stream.shape, f32),
            pltpu.VMEM(span.shape, f32),
            pltpu.SemaphoreType.DMA((4,)),
            chunk_sems,
        ],
        name="reduce",
    )(coupling_below, coupling_above, eigen_stream, span, source_field)
    blocks = pl.pallas_call(
        functools.partial(regroup_kernel, sizes),
        out_shape=pltpu.VMEM((mode_count, rows, 2, height, LANES), f32),
        in_specs=[VMEM],
        out_specs=VMEM,
        name="regroup",
    )(*near(source))

    taken = move(ports[1], modes_by=1)
    own_parts, pair_parts = [], []
    for d in range(1, chips):
        block = jnp.concatenate([ports[0, d], taken[d]], axis=0)
        pair_parts.append(move(block, modes_by=2 * d, pair=1))
        own_parts.append(move(block, modes_by=2 * d))
    side = move(jnp.concatenate([ports[0, 0], taken[0], table], axis=0), pair=1)
    sources = [move(blocks[d], modes_by=d) if d else blocks[0] for d in range(mode_count)]
    message = pl.pallas_call(
        functools.partial(merge_kernel, sizes),
        out_shape=pltpu.VMEM((4 * total + SUBLANES, LANES), f32),
        in_specs=[VMEM] * (5 + 2 * (chips - 1)),
        out_specs=VMEM,
        name="merge",
    )(*near(spectral, table, ports, taken, side, *own_parts, *pair_parts))
    messages = [move(message, level=d) for d in range(1, pairs)]
    local = pl.pallas_call(
        functools.partial(prepare_kernel, sizes),
        out_shape=(
            pltpu.VMEM((rows, 2, total, LANES), f32),
            pltpu.VMEM((rows, total, LANES), f32),
            pltpu.VMEM((rows, total, LANES), f32),
        ),
        in_specs=[VMEM] * (2 + mode_count),
        out_specs=(VMEM,) * 3,
        name="prepare",
    )(*near(spectral, table, *sources))
    out = pl.pallas_call(
        functools.partial(final_kernel, sizes, pairs),
        out_shape=jax.ShapeDtypeStruct((rows, 2, mode_count, height, LANES), f32),
        in_specs=[VMEM] * (6 + (chips - 1) + (pairs - 1)),
        out_specs=ANY,
        scratch_shapes=[
            pltpu.VMEM((rows, 2, mode_count, height, LANES), f32),
            pltpu.VMEM((pairs, 4 * total + SUBLANES, LANES), f32),
            chunk_sems,
        ],
        name="solve",
    )(*near(spectral, table, side, *local, *pair_parts, *messages))
    out = out.reshape(rows, 2, mode_count * tiles, kx_count, LANES).transpose(0, 1, 3, 2, 4)
    return out.reshape(rows, 2, kx_count, -1)


def solution(mesh):
    in_specs = (P("gz", None, None, "modes"), P("gz"), P("gz"), P(), P())
    out_specs = P("gz", None, "modes", None)
    return jax.shard_map(solve, mesh=mesh, in_specs=in_specs, out_specs=out_specs, check_vma=False)
```

```python
import functools

import jax
import jax.numpy as jnp
from jax import lax
from jax.experimental import pallas as pl
from jax.experimental.pallas import tpu as pltpu
from jax.sharding import PartitionSpec as P


LANES = 128
SUBLANES = 8


def sizes_of(source_field):
    rows, _, kx_total, ky_local = source_field.shape
    mode_count = lax.axis_size("modes")
    kx_count, tiles = kx_total // mode_count, ky_local // LANES
    return rows, kx_total, kx_count, tiles, mode_count, kx_count * tiles


def chunks_of(rows):
    size = rows // 4 if rows % 4 == 0 else rows
    return [(first, size) for first in range(0, rows, size)]


def fetch(pairs, sems):
    copies = [pltpu.make_async_copy(source, to, sems.at[i]) for i, (source, to) in enumerate(pairs)]
    for copy in copies:
        copy.start()
    return copies


def reduce_kernel(
    sizes, below_hbm, above_hbm, stream_hbm, span_hbm, source_hbm,
    ports_ref, table_ref, spectral_ref, source_ref, below_ref, above_ref, stream_ref, span_ref, small_sems, sems,
):
    rows, kx_total, kx_count, tiles, mode_count, height = sizes
    me, partition = lax.axis_index("modes"), lax.axis_index("gz")
    small = fetch(
        [(below_hbm, below_ref), (above_hbm, above_ref), (stream_hbm, stream_ref), (span_hbm, span_ref)], small_sems
    )
    parts = [pl.ds(first, size) for first, size in chunks_of(rows)]
    copies = fetch([(source_hbm.at[p], source_ref.at[p]) for p in parts], sems)
    for copy in small:
        copy.wait()
    lower = [below_ref[k] for k in range(rows)]
    upper = [above_ref[k] for k in range(rows)]
    lower[0] = jnp.where(partition == 0, 0.0, lower[0])
    upper[-1] = jnp.where(partition == lax.axis_size("gz") - 1, 0.0, upper[-1])
    lane = lax.broadcasted_iota(jnp.int32, (SUBLANES, LANES), 1)
    sub = lax.broadcasted_iota(jnp.int32, (SUBLANES, LANES), 0)
    table = jnp.zeros((SUBLANES, LANES), jnp.float32)
    for k in range(rows):
        table = jnp.where((lane == k) & (sub < 2), jnp.where(sub == 0, lower[k], upper[k]), table)
        table = jnp.where((lane == rows - 1 - k) & (sub >= 2), jnp.where(sub == 2, upper[k], lower[k]), table)
    table_ref[...] = table
    for d in range(mode_count):
        for t in range(tiles):
            spanwise = span_ref[pl.ds((me ^ d) * tiles + t, 1), :]
            for j in range(kx_count):
                at = d * height + t * kx_count + j
                spectral_ref[at : at + 1, :] = spanwise + stream_ref[me * kx_count + j]
    shape = (kx_total, LANES)
    kx_at = lax.broadcasted_iota(jnp.int32, shape, 0)
    streamwise = jnp.zeros(shape, jnp.float32)
    for i in range(kx_total):
        streamwise = jnp.where(kx_at == i, stream_ref[i], streamwise)
    each = range(tiles)
    spectral = [streamwise + span_ref[pl.ds(me * tiles + t, 1), :] for t in each]
    one, zero = jnp.ones(shape, jnp.float32), jnp.zeros(shape, jnp.float32)
    grown, passed = [one] * tiles, [one] * tiles
    partial = [[zero] * tiles, [zero] * tiles]
    first_value = [[zero] * tiles, [zero] * tiles]
    starts = {first: i for i, (first, _) in enumerate(chunks_of(rows))}
    for k in range(rows):
        if k in starts:
            copies[starts[k]].wait()
        for t in each:
            held = spectral[t] + lower[k] * grown[t]
            inverse = 1.0 / (upper[k] + held)
            grown[t] = held * inverse
            for c in range(2):
                source = source_ref[k, c, :, t * LANES : (t + 1) * LANES]
                partial[c][t] = (source + lower[k] * partial[c][t]) * inverse
                first_value[c][t] = first_value[c][t] + passed[t] * partial[c][t]
            passed[t] = passed[t] * (upper[k] * inverse)
    values = first_value + partial
    for dest in range(mode_count):
        to = dest ^ me
        for i in range(4):
            for t in each:
                at = i * height + t * kx_count
                ports_ref[to % 2, to // 2, at : at + kx_count, :] = values[i][t][dest * kx_count : (dest + 1) * kx_count]


def regroup_kernel(sizes, source_ref, blocks_ref):
    rows, _, kx_count, tiles, mode_count, _ = sizes
    me = lax.axis_index("modes")
    for dest in range(mode_count):
        to = dest ^ me
        lines = slice(dest * kx_count, (dest + 1) * kx_count)
        for k in range(rows):
            for c in range(2):
                for t in range(tiles):
                    at = t * kx_count
                    blocks_ref[to, k, c, at : at + kx_count, :] = source_ref[k, c, lines, t * LANES : (t + 1) * LANES]


def couplings(table, line, count):
    return [table[line : line + 1, k : k + 1] for k in range(count)]


def climb(spectral, num, den, near, far):
    product = near[0]
    for k in range(len(near)):
        step = near[k] * num
        num = spectral * den + step
        before = den
        den = (spectral + far[k]) * den + step
        if k:
            product = product * near[k]
    return num, den, far[-1] * before, product


def put_map(ref, lead, spectral, near, far):
    total = spectral.shape[0]
    num, den, tail = [near[0] + jnp.zeros_like(spectral), spectral], None, None
    den = [num[0], spectral + far[0]]
    tail = [jnp.zeros_like(spectral), far[0] + jnp.zeros_like(spectral)]
    product = near[0]
    for k in range(1, len(near)):
        held = spectral + far[k]
        if k == len(near) - 1:
            tail = [far[k] * den[i] for i in range(2)]
        step = [near[k] * num[i] for i in range(2)]
        num = [spectral * den[i] + step[i] for i in range(2)]
        den = [held * den[i] + step[i] for i in range(2)]
        product = product * near[k]
    for i, value in enumerate([*num, *den, *tail]):
        ref[(*lead, slice(i * total, (i + 1) * total), slice(None))] = value
    ref[(*lead, slice(6 * total, None), slice(None))] = jnp.broadcast_to(product, (SUBLANES, LANES))


def apply_map(block, state, leave, entry):
    grown, passed, *partial = state
    inverse = 1.0 / (block(2) * grown + block(3))
    ratio = block(6) * inverse
    new = [leave[c] + ratio * (partial[c] + passed * entry[c]) for c in range(2)]
    return ((block(0) * grown + block(1)) * inverse, (block(4) * grown + block(5)) * inverse, *new)


def map_of(ref, lead, total):
    def block(i):
        if i == 6:
            return ref[(*lead, slice(6 * total, 6 * total + 1), slice(None))]
        return ref[(*lead, slice(i * total, (i + 1) * total), slice(None))]

    return block


def merge_kernel(sizes, spectral_ref, table_ref, ports_ref, taken_ref, side_ref, *rest):
    rows, _, _, _, mode_count, height = sizes
    chips = mode_count // 2
    own_refs, pair_refs, message_ref = rest[: chips - 1], rest[chips - 1 : 2 * (chips - 1)], rest[-1]
    total = mode_count * height
    port = 4 * height
    upside = lax.axis_index("gz") % 2 == 1

    def gather(i, chunk):
        return jnp.concatenate([chunk(d, i * height) for d in range(mode_count)], axis=0)

    def own_chunk(d, at):
        if d >= 2:
            start = (d % 2) * port + at
            return own_refs[d // 2 - 1][start : start + height, :]
        return ports_ref[0, 0, at : at + height, :] if d == 0 else taken_ref[0, at : at + height, :]

    def pair_chunk(d, at):
        start = (d % 2) * port + at
        ref = side_ref if d < 2 else pair_refs[d // 2 - 1]
        return ref[start : start + height, :]

    own_table, pair_table = table_ref[...], side_ref[2 * port :, :]
    low_table = jnp.where(upside, pair_table, own_table)
    high_table = jnp.where(upside, own_table, pair_table)
    sub = lax.broadcasted_iota(jnp.int32, (SUBLANES, LANES), 0)
    lane = lax.broadcasted_iota(jnp.int32, (SUBLANES, LANES), 1)
    ahead = jnp.where(sub < 2, low_table, high_table)
    behind = jnp.where(sub < 2, high_table, low_table)
    message_ref[4 * total :, :] = jnp.where(lane < rows, ahead, pltpu.roll(behind, rows, 1))
    spectral = spectral_ref[...]
    one = jnp.ones((total, LANES), jnp.float32)
    own = [gather(i, own_chunk) for i in range(4)]
    pair = [gather(i, pair_chunk) for i in range(4)]
    low = [jnp.where(upside, b, a) for a, b in zip(own, pair)]
    high = [jnp.where(upside, a, b) for a, b in zip(own, pair)]

    def store(i, value):
        message_ref[i * total : (i + 1) * total, :] = value

    for near_line, first, second, near_side, far_side in ((0, low_table, high_table, 0, 2), (2, high_table, low_table, 2, 0)):
        lines = (near_line, near_line + 1)
        num, den, tail, _ = climb(spectral, one, one, *(couplings(first, i, rows) for i in lines))
        passed = tail / den
        _, den_all, _, product = climb(spectral, num, den, *(couplings(second, i, rows) for i in lines))
        ratio = product * den / den_all
        before, after = (low, high) if near_line == 0 else (high, low)
        for c in range(2):
            store(far_side + c, after[far_side + c] + ratio * (before[far_side + c] + passed * after[near_side + c]))


def prepare_kernel(sizes, spectral_ref, table_ref, side_ref, *rest):
    rows, _, _, _, mode_count, height = sizes
    sources, (part_ref, low_ref, high_ref, maps_ref) = rest[:mode_count], rest[mode_count:]
    spectral, table = spectral_ref[...], table_ref[...]
    lower, upper = couplings(table, 0, rows), couplings(table, 1, rows)
    grown = jnp.ones(spectral.shape, jnp.float32)
    carried = grown
    partial = [jnp.zeros(spectral.shape, jnp.float32)] * 2
    for k in range(rows):
        held = spectral + lower[k] * grown
        inverse = 1.0 / (upper[k] + held)
        grown = held * inverse
        scaled = lower[k] * inverse
        carried = scaled * carried
        low_ref[k] = carried
        high_ref[k] = upper[k] * inverse
        for c in range(2):
            source = jnp.concatenate([sources[d][k, c] for d in range(mode_count)], axis=0)
            partial[c] = source * inverse + scaled * partial[c]
            part_ref[k, c] = partial[c]
    low, high = low_ref[rows - 1], high_ref[rows - 1]
    for k in range(rows - 2, -1, -1):
        factor = high_ref[k]
        low = low_ref[k] + factor * low
        low_ref[k] = low
        high = factor * high
        high_ref[k] = high
        for c in range(2):
            partial[c] = part_ref[k, c] + factor * partial[c]
            part_ref[k, c] = partial[c]
    pair_table = side_ref[2 * 4 * height :, :]
    upside = lax.axis_index("gz") % 2 == 1
    put_map(maps_ref, (0,), spectral, lower, upper)
    put_map(maps_ref, (1,), spectral, couplings(table, 2, rows), couplings(table, 3, rows))
    lines = jnp.where(upside, pair_table[0:2], pair_table[2:4])
    put_map(maps_ref, (2,), spectral, couplings(lines, 0, rows), couplings(lines, 1, rows))


def put_level(sizes, level, d, message_ref, spectral, ref, lead):
    rows, total = sizes[0], spectral.shape[0]
    table = message_ref[4 * total :, :]
    lines = jnp.where((level ^ d) < level, table[0:2], table[2:4])
    put_map(ref, lead, spectral, couplings(lines, 0, 2 * rows), couplings(lines, 1, 2 * rows))


def level_kernel(sizes, levels, spectral_ref, *rest):
    messages, maps_ref = rest[:-1], rest[-1]
    level = lax.axis_index("gz") // 2
    for i, d in enumerate(levels):
        put_level(sizes, level, d, messages[i], spectral_ref[...], maps_ref, (d,))


def final_kernel(sizes, pairs, late, spectral_ref, side_ref, part_ref, low_ref, high_ref, maps_ref, levels_ref, *rest):
    rows, _, _, _, mode_count, height = sizes
    chips = mode_count // 2
    total = mode_count * height
    port = 4 * height
    pair_refs, rest = rest[: chips - 1], rest[chips - 1 :]
    messages, rest = rest[: pairs - 1], rest[pairs - 1 :]
    out_hbm, out_ref, late_ref, sems = rest
    me, partition = lax.axis_index("modes"), lax.axis_index("gz")
    upside, level = partition % 2 == 1, partition // 2
    put_level(sizes, level, late, messages[late - 1], spectral_ref[...], late_ref, ())
    one = jnp.ones((total, LANES), jnp.float32)
    zero = jnp.zeros((total, LANES), jnp.float32)
    start = (one, zero, zero, zero)

    def cross(state, d, leave, entry):
        ref = messages[d - 1]
        ports = [ref[i * total : (i + 1) * total, :] for i in (leave, leave + 1, entry, entry + 1)]
        block = map_of(late_ref, (), total) if d == late else map_of(levels_ref, (d,), total)
        return apply_map(block, state, ports[:2], ports[2:])

    def cross_levels(z, state, at):
        leave, entry = (2, 0) if at < z else (0, 2)
        return cross(state, z ^ at, leave, entry)

    def at_level(z):
        def states():
            below, above = start, start
            for at in range(z):
                below = cross_levels(z, below, at)
            for at in range(pairs - 1, z, -1):
                above = cross_levels(z, above, at)
            return below, above

        return states

    def pair_ports(i):
        chunks = []
        for d in range(mode_count):
            at = i * height + (d % 2) * port
            chunks.append((side_ref if d < 2 else pair_refs[d // 2 - 1])[at : at + height, :])
        return jnp.concatenate(chunks, axis=0)

    below, above = lax.switch(level, [at_level(z) for z in range(pairs)])
    ports = [pair_ports(i) for i in range(4)]
    near_state = [jnp.where(upside, b, a) for b, a in zip(below, above)]
    leave = [jnp.where(upside, ports[2 + c], ports[c]) for c in range(2)]
    entry = [jnp.where(upside, ports[c], ports[2 + c]) for c in range(2)]
    crossed = apply_map(map_of(maps_ref, (2,), total), near_state, leave, entry)
    below = [jnp.where(upside, new, old) for new, old in zip(crossed, below)]
    above = [jnp.where(upside, old, new) for new, old in zip(crossed, above)]
    own_first, own_last = [part_ref[0, c] for c in range(2)], [part_ref[rows - 1, c] for c in range(2)]
    leaving_up = apply_map(map_of(maps_ref, (0,), total), below, own_last, own_first)
    leaving_down = apply_map(map_of(maps_ref, (1,), total), above, own_first, own_last)
    inverse_up = 1.0 / (leaving_up[0] + leaving_up[1] * above[0])
    inverse_down = 1.0 / (leaving_down[0] + leaving_down[1] * below[0])
    under, over = [], []
    for c in range(2, 4):
        last = (leaving_up[c] + leaving_up[1] * above[c]) * inverse_up
        over.append(above[c] + above[1] * last)
        first = (leaving_down[c] + leaving_down[1] * below[c]) * inverse_down
        under.append(below[c] + below[1] * first)
    copies = []
    for i, (first, size) in enumerate(chunks_of(rows)):
        for k in range(first, first + size):
            low, high = low_ref[k], high_ref[k]
            for c in range(2):
                value = part_ref[k, c] + low * under[c] + high * over[c]
                for d in range(mode_count):
                    out_ref[k, c, me ^ d] = value[d * height : (d + 1) * height]
        part = pl.ds(first, size)
        copies.append(pltpu.make_async_copy(out_ref.at[part], out_hbm.at[part], sems.at[i]))
        copies[-1].start()
    for copy in copies:
        copy.wait()


LIMIT = pltpu.CompilerParams(vmem_limit_bytes=16 << 20)
VMEM = pl.BlockSpec(memory_space=pltpu.VMEM)
ANY = pl.BlockSpec(memory_space=pl.ANY)


def near(*arrays):
    return [pltpu.with_memory_space_constraint(a, pltpu.VMEM) for a in arrays]


def solve(source_field, coupling_below, coupling_above, eigen_stream, eigen_span):
    sizes = rows, kx_total, kx_count, tiles, mode_count, height = sizes_of(source_field)
    partitions = lax.axis_size("gz")
    chips, pairs = mode_count // 2, partitions // 2
    total = mode_count * height
    f32 = jnp.float32
    chunk_sems = pltpu.SemaphoreType.DMA((len(chunks_of(rows)),))

    def move(array, modes_by=0, pair=0, level=0):
        links = []
        for m in range(mode_count):
            for g in range(partitions):
                to = ((g // 2) ^ level) * 2 + ((g % 2) ^ pair)
                links.append((m * partitions + g, (m ^ modes_by) * partitions + to))
        return lax.ppermute(array, ("modes", "gz"), links)

    span = eigen_span.reshape(-1, LANES)
    ports, table, spectral, source = pl.pallas_call(
        functools.partial(reduce_kernel, sizes),
        out_shape=(
            pltpu.VMEM((2, chips, 4 * height, LANES), f32),
            pltpu.VMEM((SUBLANES, LANES), f32),
            pltpu.VMEM((total, LANES), f32),
            pltpu.VMEM(source_field.shape, f32),
        ),
        in_specs=[ANY] * 5,
        out_specs=(VMEM,) * 4,
        scratch_shapes=[
            pltpu.SMEM(coupling_below.shape, f32),
            pltpu.SMEM(coupling_above.shape, f32),
            pltpu.SMEM(eigen_stream.shape, f32),
            pltpu.VMEM(span.shape, f32),
            pltpu.SemaphoreType.DMA((4,)),
            chunk_sems,
        ],
        name="reduce",
        compiler_params=LIMIT,
    )(coupling_below, coupling_above, eigen_stream, span, source_field)
    blocks = pl.pallas_call(
        functools.partial(regroup_kernel, sizes),
        out_shape=pltpu.VMEM((mode_count, rows, 2, height, LANES), f32),
        in_specs=[VMEM],
        out_specs=VMEM,
        name="regroup",
        compiler_params=LIMIT,
    )(*near(source))

    taken = move(ports[1], modes_by=1)
    own_parts, pair_parts = [], []
    for d in range(1, chips):
        block = jnp.concatenate([ports[0, d], taken[d]], axis=0)
        pair_parts.append(move(block, modes_by=2 * d, pair=1))
        own_parts.append(move(block, modes_by=2 * d))
    side = move(jnp.concatenate([ports[0, 0], taken[0], table], axis=0), pair=1)
    sources = [move(blocks[d], modes_by=d) if d else blocks[0] for d in range(mode_count)]
    message = pl.pallas_call(
        functools.partial(merge_kernel, sizes),
        out_shape=pltpu.VMEM((4 * total + SUBLANES, LANES), f32),
        in_specs=[VMEM] * (5 + 2 * (chips - 1)),
        out_specs=VMEM,
        name="merge",
        compiler_params=LIMIT,
    )(*near(spectral, table, ports, taken, side, *own_parts, *pair_parts))
    messages = [move(message, level=d) for d in range(1, pairs)]
    map_lines = 6 * total + SUBLANES
    *local, maps = pl.pallas_call(
        functools.partial(prepare_kernel, sizes),
        out_shape=(
            pltpu.VMEM((rows, 2, total, LANES), f32),
            pltpu.VMEM((rows, total, LANES), f32),
            pltpu.VMEM((rows, total, LANES), f32),
            pltpu.VMEM((3, map_lines, LANES), f32),
        ),
        in_specs=[VMEM] * (3 + mode_count),
        out_specs=(VMEM,) * 4,
        name="prepare",
        compiler_params=LIMIT,
    )(*near(spectral, table, side, *sources))
    late = late_level(pairs)
    early = [d for d in range(1, pairs) if d != late]
    level_maps = pl.pallas_call(
        functools.partial(level_kernel, sizes, early),
        out_shape=pltpu.VMEM((pairs, map_lines, LANES), f32),
        in_specs=[VMEM] * (1 + len(early)),
        out_specs=VMEM,
        name="levels",
        compiler_params=LIMIT,
    )(*near(spectral, *(messages[d - 1] for d in early)))
    out = pl.pallas_call(
        functools.partial(final_kernel, sizes, pairs, late),
        out_shape=jax.ShapeDtypeStruct((rows, 2, mode_count, height, LANES), f32),
        in_specs=[VMEM] * (7 + (chips - 1) + (pairs - 1)),
        out_specs=ANY,
        scratch_shapes=[
            pltpu.VMEM((rows, 2, mode_count, height, LANES), f32),
            pltpu.VMEM((map_lines, LANES), f32),
            chunk_sems,
        ],
        name="solve",
        compiler_params=LIMIT,
    )(*near(spectral, side, *local, maps, level_maps, *pair_parts, *messages))
    out = out.reshape(rows, 2, mode_count * tiles, kx_count, LANES).transpose(0, 1, 3, 2, 4)
    return out.reshape(rows, 2, kx_count, -1)


def late_level(pairs):
    return min(2, pairs - 1)


def solution(mesh):
    in_specs = (P("gz", None, None, "modes"), P("gz"), P("gz"), P(), P())
    out_specs = P("gz", None, "modes", None)
    return jax.shard_map(solve, mesh=mesh, in_specs=in_specs, out_specs=out_specs, check_vma=False)
```

```python
import functools

import jax
import jax.numpy as jnp
from jax import lax
from jax.experimental import pallas as pl
from jax.experimental.pallas import tpu as pltpu
from jax.sharding import PartitionSpec as P


LANES = 128
SUBLANES = 8


def sizes_of(source_field):
    rows, _, kx_total, ky_local = source_field.shape
    mode_count = lax.axis_size("modes")
    kx_count, tiles = kx_total // mode_count, ky_local // LANES
    return rows, kx_total, kx_count, tiles, mode_count, kx_count * tiles


def chunks_of(rows):
    size = rows // 4 if rows % 4 == 0 else rows
    return [(first, size) for first in range(0, rows, size)]


def fetch(pairs, sems):
    copies = [pltpu.make_async_copy(source, to, sems.at[i]) for i, (source, to) in enumerate(pairs)]
    for copy in copies:
        copy.start()
    return copies


def reduce_kernel(
    sizes, below_hbm, above_hbm, stream_hbm, span_hbm, source_hbm,
    ports_ref, table_ref, spectral_ref, source_ref, below_ref, above_ref, stream_ref, span_ref, small_sems, sems,
):
    rows, kx_total, kx_count, tiles, mode_count, height = sizes
    me, partition = lax.axis_index("modes"), lax.axis_index("gz")
    small = fetch(
        [(below_hbm, below_ref), (above_hbm, above_ref), (stream_hbm, stream_ref), (span_hbm, span_ref)], small_sems
    )
    parts = [pl.ds(first, size) for first, size in chunks_of(rows)]
    copies = fetch([(source_hbm.at[p], source_ref.at[p]) for p in parts], sems)
    for copy in small:
        copy.wait()
    lower = [below_ref[k] for k in range(rows)]
    upper = [above_ref[k] for k in range(rows)]
    lower[0] = jnp.where(partition == 0, 0.0, lower[0])
    upper[-1] = jnp.where(partition == lax.axis_size("gz") - 1, 0.0, upper[-1])
    lane = lax.broadcasted_iota(jnp.int32, (SUBLANES, LANES), 1)
    sub = lax.broadcasted_iota(jnp.int32, (SUBLANES, LANES), 0)
    table = jnp.zeros((SUBLANES, LANES), jnp.float32)
    for k in range(rows):
        table = jnp.where((lane == k) & (sub < 2), jnp.where(sub == 0, lower[k], upper[k]), table)
        table = jnp.where((lane == rows - 1 - k) & (sub >= 2), jnp.where(sub == 2, upper[k], lower[k]), table)
    table_ref[...] = table
    for d in range(mode_count):
        for t in range(tiles):
            spanwise = span_ref[pl.ds((me ^ d) * tiles + t, 1), :]
            for j in range(kx_count):
                at = d * height + t * kx_count + j
                spectral_ref[at : at + 1, :] = spanwise + stream_ref[me * kx_count + j]
    shape = (kx_total, LANES)
    kx_at = lax.broadcasted_iota(jnp.int32, shape, 0)
    streamwise = jnp.zeros(shape, jnp.float32)
    for i in range(kx_total):
        streamwise = jnp.where(kx_at == i, stream_ref[i], streamwise)
    each = range(tiles)
    spectral = [streamwise + span_ref[pl.ds(me * tiles + t, 1), :] for t in each]
    one, zero = jnp.ones(shape, jnp.float32), jnp.zeros(shape, jnp.float32)
    grown, passed = [one] * tiles, [one] * tiles
    partial = [[zero] * tiles, [zero] * tiles]
    first_value = [[zero] * tiles, [zero] * tiles]
    starts = {first: i for i, (first, _) in enumerate(chunks_of(rows))}
    for k in range(rows):
        if k in starts:
            copies[starts[k]].wait()
        for t in each:
            held = spectral[t] + lower[k] * grown[t]
            inverse = 1.0 / (upper[k] + held)
            grown[t] = held * inverse
            for c in range(2):
                source = source_ref[k, c, :, t * LANES : (t + 1) * LANES]
                partial[c][t] = (source + lower[k] * partial[c][t]) * inverse
                first_value[c][t] = first_value[c][t] + passed[t] * partial[c][t]
            passed[t] = passed[t] * (upper[k] * inverse)
    values = first_value + partial
    for dest in range(mode_count):
        to = dest ^ me
        for i in range(4):
            for t in each:
                at = i * height + t * kx_count
                ports_ref[to % 2, to // 2, at : at + kx_count, :] = values[i][t][dest * kx_count : (dest + 1) * kx_count]


def regroup_kernel(sizes, source_ref, blocks_ref):
    rows, _, kx_count, tiles, mode_count, _ = sizes
    me = lax.axis_index("modes")
    for dest in range(mode_count):
        to = dest ^ me
        lines = slice(dest * kx_count, (dest + 1) * kx_count)
        for k in range(rows):
            for c in range(2):
                for t in range(tiles):
                    at = t * kx_count
                    blocks_ref[to, k, c, at : at + kx_count, :] = source_ref[k, c, lines, t * LANES : (t + 1) * LANES]


def couplings(table, line, count):
    return [table[line : line + 1, k : k + 1] for k in range(count)]


def climb(spectral, num, den, near, far):
    product = near[0]
    for k in range(len(near)):
        step = near[k] * num
        num = spectral * den + step
        before = den
        den = (spectral + far[k]) * den + step
        if k:
            product = product * near[k]
    return num, den, far[-1] * before, product


def put_map(ref, lead, spectral, near, far):
    total = spectral.shape[0]
    num, den, tail = [near[0] + jnp.zeros_like(spectral), spectral], None, None
    den = [num[0], spectral + far[0]]
    tail = [jnp.zeros_like(spectral), far[0] + jnp.zeros_like(spectral)]
    product = near[0]
    for k in range(1, len(near)):
        held = spectral + far[k]
        if k == len(near) - 1:
            tail = [far[k] * den[i] for i in range(2)]
        step = [near[k] * num[i] for i in range(2)]
        num = [spectral * den[i] + step[i] for i in range(2)]
        den = [held * den[i] + step[i] for i in range(2)]
        product = product * near[k]
    for i, value in enumerate([*num, *den, *tail]):
        ref[(*lead, slice(i * total, (i + 1) * total), slice(None))] = value
    ref[(*lead, slice(6 * total, None), slice(None))] = jnp.broadcast_to(product, (SUBLANES, LANES))


def apply_map(block, state, leave, entry):
    grown, passed, *partial = state
    inverse = 1.0 / (block(2) * grown + block(3))
    ratio = block(6) * inverse
    new = [leave[c] + ratio * (partial[c] + passed * entry[c]) for c in range(2)]
    return ((block(0) * grown + block(1)) * inverse, (block(4) * grown + block(5)) * inverse, *new)


def map_of(ref, lead, total):
    def block(i):
        if i == 6:
            return ref[(*lead, slice(6 * total, 6 * total + 1), slice(None))]
        return ref[(*lead, slice(i * total, (i + 1) * total), slice(None))]

    return block


def merge_kernel(sizes, spectral_ref, table_ref, ports_ref, taken_ref, side_ref, *rest):
    rows, _, _, _, mode_count, height = sizes
    chips = mode_count // 2
    own_refs, pair_refs, message_ref = rest[: chips - 1], rest[chips - 1 : 2 * (chips - 1)], rest[-1]
    total = mode_count * height
    port = 4 * height
    upside = lax.axis_index("gz") % 2 == 1

    def gather(i, chunk):
        return jnp.concatenate([chunk(d, i * height) for d in range(mode_count)], axis=0)

    def own_chunk(d, at):
        if d >= 2:
            start = (d % 2) * port + at
            return own_refs[d // 2 - 1][start : start + height, :]
        return ports_ref[0, 0, at : at + height, :] if d == 0 else taken_ref[0, at : at + height, :]

    def pair_chunk(d, at):
        start = (d % 2) * port + at
        ref = side_ref if d < 2 else pair_refs[d // 2 - 1]
        return ref[start : start + height, :]

    own_table, pair_table = table_ref[...], side_ref[2 * port :, :]
    low_table = jnp.where(upside, pair_table, own_table)
    high_table = jnp.where(upside, own_table, pair_table)
    sub = lax.broadcasted_iota(jnp.int32, (SUBLANES, LANES), 0)
    lane = lax.broadcasted_iota(jnp.int32, (SUBLANES, LANES), 1)
    ahead = jnp.where(sub < 2, low_table, high_table)
    behind = jnp.where(sub < 2, high_table, low_table)
    message_ref[4 * total :, :] = jnp.where(lane < rows, ahead, pltpu.roll(behind, rows, 1))
    spectral = spectral_ref[...]
    one = jnp.ones((total, LANES), jnp.float32)
    own = [gather(i, own_chunk) for i in range(4)]
    pair = [gather(i, pair_chunk) for i in range(4)]
    low = [jnp.where(upside, b, a) for a, b in zip(own, pair)]
    high = [jnp.where(upside, a, b) for a, b in zip(own, pair)]

    def store(i, value):
        message_ref[i * total : (i + 1) * total, :] = value

    for near_line, first, second, near_side, far_side in ((0, low_table, high_table, 0, 2), (2, high_table, low_table, 2, 0)):
        lines = (near_line, near_line + 1)
        num, den, tail, _ = climb(spectral, one, one, *(couplings(first, i, rows) for i in lines))
        passed = tail / den
        _, den_all, _, product = climb(spectral, num, den, *(couplings(second, i, rows) for i in lines))
        ratio = product * den / den_all
        before, after = (low, high) if near_line == 0 else (high, low)
        for c in range(2):
            store(far_side + c, after[far_side + c] + ratio * (before[far_side + c] + passed * after[near_side + c]))


def prepare_kernel(sizes, spectral_ref, table_ref, side_ref, *rest):
    rows, _, _, _, mode_count, height = sizes
    sources, (part_ref, low_ref, high_ref, maps_ref) = rest[:mode_count], rest[mode_count:]
    spectral, table = spectral_ref[...], table_ref[...]
    lower, upper = couplings(table, 0, rows), couplings(table, 1, rows)
    grown = jnp.ones(spectral.shape, jnp.float32)
    carried = grown
    partial = [jnp.zeros(spectral.shape, jnp.float32)] * 2
    for k in range(rows):
        held = spectral + lower[k] * grown
        inverse = 1.0 / (upper[k] + held)
        grown = held * inverse
        scaled = lower[k] * inverse
        carried = scaled * carried
        low_ref[k] = carried
        high_ref[k] = upper[k] * inverse
        for c in range(2):
            source = jnp.concatenate([sources[d][k, c] for d in range(mode_count)], axis=0)
            partial[c] = source * inverse + scaled * partial[c]
            part_ref[k, c] = partial[c]
    low, high = low_ref[rows - 1], high_ref[rows - 1]
    for k in range(rows - 2, -1, -1):
        factor = high_ref[k]
        low = low_ref[k] + factor * low
        low_ref[k] = low
        high = factor * high
        high_ref[k] = high
        for c in range(2):
            partial[c] = part_ref[k, c] + factor * partial[c]
            part_ref[k, c] = partial[c]
    pair_table = side_ref[2 * 4 * height :, :]
    upside = lax.axis_index("gz") % 2 == 1
    put_map(maps_ref, (0,), spectral, lower, upper)
    put_map(maps_ref, (1,), spectral, couplings(table, 2, rows), couplings(table, 3, rows))
    lines = jnp.where(upside, pair_table[0:2], pair_table[2:4])
    put_map(maps_ref, (2,), spectral, couplings(lines, 0, rows), couplings(lines, 1, rows))


def put_level(sizes, level, d, message_ref, spectral, ref, lead):
    rows, total = sizes[0], spectral.shape[0]
    table = message_ref[4 * total :, :]
    lines = jnp.where((level ^ d) < level, table[0:2], table[2:4])
    put_map(ref, lead, spectral, couplings(lines, 0, 2 * rows), couplings(lines, 1, 2 * rows))


def level_kernel(sizes, levels, spectral_ref, *rest):
    messages, maps_ref = rest[:-1], rest[-1]
    level = lax.axis_index("gz") // 2
    for i, d in enumerate(levels):
        put_level(sizes, level, d, messages[i], spectral_ref[...], maps_ref, (d,))


def final_kernel(sizes, pairs, late, spectral_ref, side_ref, part_ref, low_ref, high_ref, maps_ref, levels_ref, *rest):
    rows, _, _, _, mode_count, height = sizes
    chips = mode_count // 2
    total = mode_count * height
    port = 4 * height
    pair_refs, rest = rest[: chips - 1], rest[chips - 1 :]
    messages, rest = rest[: pairs - 1], rest[pairs - 1 :]
    out_hbm, out_ref, late_ref, sems = rest
    me, partition = lax.axis_index("modes"), lax.axis_index("gz")
    upside, level = partition % 2 == 1, partition // 2
    for i, d in enumerate(late):
        put_level(sizes, level, d, messages[d - 1], spectral_ref[...], late_ref, (i,))
    one = jnp.ones((total, LANES), jnp.float32)
    zero = jnp.zeros((total, LANES), jnp.float32)
    start = (one, zero, zero, zero)

    def cross(state, d, leave, entry):
        ref = messages[d - 1]
        ports = [ref[i * total : (i + 1) * total, :] for i in (leave, leave + 1, entry, entry + 1)]
        block = map_of(late_ref, (late.index(d),), total) if d in late else map_of(levels_ref, (d,), total)
        return apply_map(block, state, ports[:2], ports[2:])

    def cross_levels(z, state, at):
        leave, entry = (2, 0) if at < z else (0, 2)
        return cross(state, z ^ at, leave, entry)

    def at_level(z):
        def states():
            below, above = start, start
            for at in range(z):
                below = cross_levels(z, below, at)
            for at in range(pairs - 1, z, -1):
                above = cross_levels(z, above, at)
            return below, above

        return states

    def pair_ports(i):
        chunks = []
        for d in range(mode_count):
            at = i * height + (d % 2) * port
            chunks.append((side_ref if d < 2 else pair_refs[d // 2 - 1])[at : at + height, :])
        return jnp.concatenate(chunks, axis=0)

    below, above = lax.switch(level, [at_level(z) for z in range(pairs)])
    ports = [pair_ports(i) for i in range(4)]
    near_state = [jnp.where(upside, b, a) for b, a in zip(below, above)]
    leave = [jnp.where(upside, ports[2 + c], ports[c]) for c in range(2)]
    entry = [jnp.where(upside, ports[c], ports[2 + c]) for c in range(2)]
    crossed = apply_map(map_of(maps_ref, (2,), total), near_state, leave, entry)
    below = [jnp.where(upside, new, old) for new, old in zip(crossed, below)]
    above = [jnp.where(upside, old, new) for new, old in zip(crossed, above)]
    own_first, own_last = [part_ref[0, c] for c in range(2)], [part_ref[rows - 1, c] for c in range(2)]
    leaving_up = apply_map(map_of(maps_ref, (0,), total), below, own_last, own_first)
    leaving_down = apply_map(map_of(maps_ref, (1,), total), above, own_first, own_last)
    inverse_up = 1.0 / (leaving_up[0] + leaving_up[1] * above[0])
    inverse_down = 1.0 / (leaving_down[0] + leaving_down[1] * below[0])
    under, over = [], []
    for c in range(2, 4):
        last = (leaving_up[c] + leaving_up[1] * above[c]) * inverse_up
        over.append(above[c] + above[1] * last)
        first = (leaving_down[c] + leaving_down[1] * below[c]) * inverse_down
        under.append(below[c] + below[1] * first)
    copies = []
    for i, (first, size) in enumerate(chunks_of(rows)):
        for k in range(first, first + size):
            low, high = low_ref[k], high_ref[k]
            for c in range(2):
                value = part_ref[k, c] + low * under[c] + high * over[c]
                for d in range(mode_count):
                    out_ref[k, c, me ^ d] = value[d * height : (d + 1) * height]
        part = pl.ds(first, size)
        copies.append(pltpu.make_async_copy(out_ref.at[part], out_hbm.at[part], sems.at[i]))
        copies[-1].start()
    for copy in copies:
        copy.wait()


LIMIT = pltpu.CompilerParams(vmem_limit_bytes=16 << 20)
VMEM = pl.BlockSpec(memory_space=pltpu.VMEM)
ANY = pl.BlockSpec(memory_space=pl.ANY)


def near(*arrays):
    return [pltpu.with_memory_space_constraint(a, pltpu.VMEM) for a in arrays]


def solve(source_field, coupling_below, coupling_above, eigen_stream, eigen_span):
    sizes = rows, kx_total, kx_count, tiles, mode_count, height = sizes_of(source_field)
    partitions = lax.axis_size("gz")
    chips, pairs = mode_count // 2, partitions // 2
    total = mode_count * height
    f32 = jnp.float32
    chunk_sems = pltpu.SemaphoreType.DMA((len(chunks_of(rows)),))

    def move(array, modes_by=0, pair=0, level=0):
        links = []
        for m in range(mode_count):
            for g in range(partitions):
                to = ((g // 2) ^ level) * 2 + ((g % 2) ^ pair)
                links.append((m * partitions + g, (m ^ modes_by) * partitions + to))
        return lax.ppermute(array, ("modes", "gz"), links)

    span = eigen_span.reshape(-1, LANES)
    ports, table, spectral, source = pl.pallas_call(
        functools.partial(reduce_kernel, sizes),
        out_shape=(
            pltpu.VMEM((2, chips, 4 * height, LANES), f32),
            pltpu.VMEM((SUBLANES, LANES), f32),
            pltpu.VMEM((total, LANES), f32),
            pltpu.VMEM(source_field.shape, f32),
        ),
        in_specs=[ANY] * 5,
        out_specs=(VMEM,) * 4,
        scratch_shapes=[
            pltpu.SMEM(coupling_below.shape, f32),
            pltpu.SMEM(coupling_above.shape, f32),
            pltpu.SMEM(eigen_stream.shape, f32),
            pltpu.VMEM(span.shape, f32),
            pltpu.SemaphoreType.DMA((4,)),
            chunk_sems,
        ],
        name="reduce",
    )(coupling_below, coupling_above, eigen_stream, span, source_field)
    blocks = pl.pallas_call(
        functools.partial(regroup_kernel, sizes),
        out_shape=pltpu.VMEM((mode_count, rows, 2, height, LANES), f32),
        in_specs=[VMEM],
        out_specs=VMEM,
        name="regroup",
    )(*near(source))

    taken = move(ports[1], modes_by=1)
    own_parts, pair_parts = [], []
    for d in range(1, chips):
        block = jnp.concatenate([ports[0, d], taken[d]], axis=0)
        pair_parts.append(move(block, modes_by=2 * d, pair=1))
        own_parts.append(move(block, modes_by=2 * d))
    side = move(jnp.concatenate([ports[0, 0], taken[0], table], axis=0), pair=1)
    sources = [move(blocks[d], modes_by=d) if d else blocks[0] for d in range(mode_count)]
    message = pl.pallas_call(
        functools.partial(merge_kernel, sizes),
        out_shape=pltpu.VMEM((4 * total + SUBLANES, LANES), f32),
        in_specs=[VMEM] * (5 + 2 * (chips - 1)),
        out_specs=VMEM,
        name="merge",
    )(*near(spectral, table, ports, taken, side, *own_parts, *pair_parts))
    messages = [move(message, level=d) for d in range(1, pairs)]
    map_lines = 6 * total + SUBLANES
    *local, maps = pl.pallas_call(
        functools.partial(prepare_kernel, sizes),
        out_shape=(
            pltpu.VMEM((rows, 2, total, LANES), f32),
            pltpu.VMEM((rows, total, LANES), f32),
            pltpu.VMEM((rows, total, LANES), f32),
            pltpu.VMEM((3, map_lines, LANES), f32),
        ),
        in_specs=[VMEM] * (3 + mode_count),
        out_specs=(VMEM,) * 4,
        name="prepare",
    )(*near(spectral, table, side, *sources))
    late = late_levels(pairs)
    early = [d for d in range(1, pairs) if d not in late]
    level_maps = pl.pallas_call(
        functools.partial(level_kernel, sizes, early),
        out_shape=pltpu.VMEM((pairs, map_lines, LANES), f32),
        in_specs=[VMEM] * (1 + len(early)),
        out_specs=VMEM,
        name="levels",
        compiler_params=LIMIT,
    )(*near(spectral, *(messages[d - 1] for d in early)))
    out = pl.pallas_call(
        functools.partial(final_kernel, sizes, pairs, late),
        out_shape=jax.ShapeDtypeStruct((rows, 2, mode_count, height, LANES), f32),
        in_specs=[VMEM] * (7 + (chips - 1) + (pairs - 1)),
        out_specs=ANY,
        scratch_shapes=[
            pltpu.VMEM((rows, 2, mode_count, height, LANES), f32),
            pltpu.VMEM((len(late), map_lines, LANES), f32),
            chunk_sems,
        ],
        name="solve",
        compiler_params=LIMIT,
    )(*near(spectral, side, *local, maps, level_maps, *pair_parts, *messages))
    out = out.reshape(rows, 2, mode_count * tiles, kx_count, LANES).transpose(0, 1, 3, 2, 4)
    return out.reshape(rows, 2, kx_count, -1)


def late_levels(pairs):
    return [d for d in (1, 2) if d < pairs]


def solution(mesh):
    in_specs = (P("gz", None, None, "modes"), P("gz"), P("gz"), P(), P())
    out_specs = P("gz", None, "modes", None)
    return jax.shard_map(solve, mesh=mesh, in_specs=in_specs, out_specs=out_specs, check_vma=False)
```

```python
import functools

import jax
import jax.numpy as jnp
from jax import lax
from jax.experimental import pallas as pl
from jax.experimental.pallas import tpu as pltpu
from jax.sharding import PartitionSpec as P


LANES = 128
SUBLANES = 8


def sizes_of(source_field):
    rows, _, kx_total, ky_local = source_field.shape
    mode_count = lax.axis_size("modes")
    kx_count, tiles = kx_total // mode_count, ky_local // LANES
    return rows, kx_total, kx_count, tiles, mode_count, kx_count * tiles


def chunks_of(rows, count=4):
    size = rows // count if rows % count == 0 else rows
    return [(first, size) for first in range(0, rows, size)]


def fetch(pairs, sems):
    copies = [pltpu.make_async_copy(source, to, sems.at[i]) for i, (source, to) in enumerate(pairs)]
    for copy in copies:
        copy.start()
    return copies


def reduce_kernel(
    sizes, below_hbm, above_hbm, stream_hbm, span_hbm, source_hbm,
    ports_ref, table_ref, spectral_ref, source_ref, below_ref, above_ref, stream_ref, span_ref, small_sems, sems,
):
    rows, kx_total, kx_count, tiles, mode_count, height = sizes
    me, partition = lax.axis_index("modes"), lax.axis_index("gz")
    small = fetch(
        [(below_hbm, below_ref), (above_hbm, above_ref), (stream_hbm, stream_ref), (span_hbm, span_ref)], small_sems
    )
    parts = [pl.ds(first, size) for first, size in chunks_of(rows)]
    copies = fetch([(source_hbm.at[p], source_ref.at[p]) for p in parts], sems)
    for copy in small:
        copy.wait()
    lower = [below_ref[k] for k in range(rows)]
    upper = [above_ref[k] for k in range(rows)]
    lower[0] = jnp.where(partition == 0, 0.0, lower[0])
    upper[-1] = jnp.where(partition == lax.axis_size("gz") - 1, 0.0, upper[-1])
    lane = lax.broadcasted_iota(jnp.int32, (SUBLANES, LANES), 1)
    sub = lax.broadcasted_iota(jnp.int32, (SUBLANES, LANES), 0)
    table = jnp.zeros((SUBLANES, LANES), jnp.float32)
    for k in range(rows):
        table = jnp.where((lane == k) & (sub < 2), jnp.where(sub == 0, lower[k], upper[k]), table)
        table = jnp.where((lane == rows - 1 - k) & (sub >= 2), jnp.where(sub == 2, upper[k], lower[k]), table)
    table_ref[...] = table
    for d in range(mode_count):
        for t in range(tiles):
            spanwise = span_ref[pl.ds((me ^ d) * tiles + t, 1), :]
            for j in range(kx_count):
                at = d * height + t * kx_count + j
                spectral_ref[at : at + 1, :] = spanwise + stream_ref[me * kx_count + j]
    shape = (kx_total, LANES)
    kx_at = lax.broadcasted_iota(jnp.int32, shape, 0)
    streamwise = jnp.zeros(shape, jnp.float32)
    for i in range(kx_total):
        streamwise = jnp.where(kx_at == i, stream_ref[i], streamwise)
    each = range(tiles)
    spectral = [streamwise + span_ref[pl.ds(me * tiles + t, 1), :] for t in each]
    one, zero = jnp.ones(shape, jnp.float32), jnp.zeros(shape, jnp.float32)
    grown, passed = [one] * tiles, [one] * tiles
    partial = [[zero] * tiles, [zero] * tiles]
    first_value = [[zero] * tiles, [zero] * tiles]
    starts = {first: i for i, (first, _) in enumerate(chunks_of(rows))}
    for k in range(rows):
        if k in starts:
            copies[starts[k]].wait()
        for t in each:
            held = spectral[t] + lower[k] * grown[t]
            inverse = 1.0 / (upper[k] + held)
            grown[t] = held * inverse
            for c in range(2):
                source = source_ref[k, c, :, t * LANES : (t + 1) * LANES]
                partial[c][t] = (source + lower[k] * partial[c][t]) * inverse
                first_value[c][t] = first_value[c][t] + passed[t] * partial[c][t]
            passed[t] = passed[t] * (upper[k] * inverse)
    values = first_value + partial
    for dest in range(mode_count):
        to = dest ^ me
        for i in range(4):
            for t in each:
                at = i * height + t * kx_count
                ports_ref[to % 2, to // 2, at : at + kx_count, :] = values[i][t][dest * kx_count : (dest + 1) * kx_count]


def regroup_kernel(sizes, source_ref, blocks_ref):
    rows, _, kx_count, tiles, mode_count, _ = sizes
    me = lax.axis_index("modes")
    for dest in range(mode_count):
        to = dest ^ me
        lines = slice(dest * kx_count, (dest + 1) * kx_count)
        for k in range(rows):
            for c in range(2):
                for t in range(tiles):
                    at = t * kx_count
                    blocks_ref[to, k, c, at : at + kx_count, :] = source_ref[k, c, lines, t * LANES : (t + 1) * LANES]


def couplings(table, line, count):
    return [table[line : line + 1, k : k + 1] for k in range(count)]


def climb(spectral, num, den, near, far):
    product = near[0]
    for k in range(len(near)):
        step = near[k] * num
        num = spectral * den + step
        before = den
        den = (spectral + far[k]) * den + step
        if k:
            product = product * near[k]
    return num, den, far[-1] * before, product


MAP_PARTS = 7


def put_map(ref, lead, spectral, near, far):
    total = spectral.shape[0]
    zero = jnp.zeros_like(spectral)
    num = [near[0] + zero, spectral]
    den = [num[0], spectral + far[0]]
    tail = [zero, far[0] + zero]
    product = near[0]
    for k in range(1, len(near)):
        held = spectral + far[k]
        if k == len(near) - 1:
            tail = [far[k] * den[i] for i in range(2)]
        step = [near[k] * num[i] for i in range(2)]
        num = [spectral * den[i] + step[i] for i in range(2)]
        den = [held * den[i] + step[i] for i in range(2)]
        product = product * near[k]
    scale = 1.0 / (den[0] + den[1])
    for i, value in enumerate([*num, *den, *tail, product]):
        ref[(*lead, slice(i * total, (i + 1) * total), slice(None))] = value * scale


def apply_map(block, state, leave, entry):
    num, den, tail, *partial = state
    new_den = block(2) * num + block(3) * den
    new = [leave[c] * new_den + block(6) * (partial[c] + tail * entry[c]) for c in range(2)]
    return (block(0) * num + block(1) * den, new_den, block(4) * num + block(5) * den, *new)


def map_of(ref, lead, total):
    return lambda i: ref[(*lead, slice(i * total, (i + 1) * total), slice(None))]


def merge_kernel(sizes, spectral_ref, table_ref, ports_ref, taken_ref, side_ref, *rest):
    rows, _, _, _, mode_count, height = sizes
    chips = mode_count // 2
    own_refs, pair_refs, message_ref = rest[: chips - 1], rest[chips - 1 : 2 * (chips - 1)], rest[-1]
    total = mode_count * height
    port = 4 * height
    upside = lax.axis_index("gz") % 2 == 1

    def gather(i, chunk):
        return jnp.concatenate([chunk(d, i * height) for d in range(mode_count)], axis=0)

    def own_chunk(d, at):
        if d >= 2:
            start = (d % 2) * port + at
            return own_refs[d // 2 - 1][start : start + height, :]
        return ports_ref[0, 0, at : at + height, :] if d == 0 else taken_ref[0, at : at + height, :]

    def pair_chunk(d, at):
        start = (d % 2) * port + at
        ref = side_ref if d < 2 else pair_refs[d // 2 - 1]
        return ref[start : start + height, :]

    own_table, pair_table = table_ref[...], side_ref[2 * port :, :]
    low_table = jnp.where(upside, pair_table, own_table)
    high_table = jnp.where(upside, own_table, pair_table)
    sub = lax.broadcasted_iota(jnp.int32, (SUBLANES, LANES), 0)
    lane = lax.broadcasted_iota(jnp.int32, (SUBLANES, LANES), 1)
    ahead = jnp.where(sub < 2, low_table, high_table)
    behind = jnp.where(sub < 2, high_table, low_table)
    message_ref[4 * total :, :] = jnp.where(lane < rows, ahead, pltpu.roll(behind, rows, 1))
    spectral = spectral_ref[...]
    one = jnp.ones((total, LANES), jnp.float32)
    own = [gather(i, own_chunk) for i in range(4)]
    pair = [gather(i, pair_chunk) for i in range(4)]
    low = [jnp.where(upside, b, a) for a, b in zip(own, pair)]
    high = [jnp.where(upside, a, b) for a, b in zip(own, pair)]

    def store(i, value):
        message_ref[i * total : (i + 1) * total, :] = value

    for near_line, first, second, near_side, far_side in ((0, low_table, high_table, 0, 2), (2, high_table, low_table, 2, 0)):
        lines = (near_line, near_line + 1)
        num, den, tail, _ = climb(spectral, one, one, *(couplings(first, i, rows) for i in lines))
        passed = tail / den
        _, den_all, _, product = climb(spectral, num, den, *(couplings(second, i, rows) for i in lines))
        ratio = product * den / den_all
        before, after = (low, high) if near_line == 0 else (high, low)
        for c in range(2):
            store(far_side + c, after[far_side + c] + ratio * (before[far_side + c] + passed * after[near_side + c]))


def prepare_kernel(sizes, spectral_ref, table_ref, side_ref, *rest):
    rows, _, _, _, mode_count, height = sizes
    sources, (part_ref, low_ref, high_ref, maps_ref) = rest[:mode_count], rest[mode_count:]
    spectral, table = spectral_ref[...], table_ref[...]
    lower, upper = couplings(table, 0, rows), couplings(table, 1, rows)
    grown = jnp.ones(spectral.shape, jnp.float32)
    carried = grown
    partial = [jnp.zeros(spectral.shape, jnp.float32)] * 2
    for k in range(rows):
        held = spectral + lower[k] * grown
        inverse = 1.0 / (upper[k] + held)
        grown = held * inverse
        scaled = lower[k] * inverse
        carried = scaled * carried
        low_ref[k] = carried
        high_ref[k] = upper[k] * inverse
        for c in range(2):
            source = jnp.concatenate([sources[d][k, c] for d in range(mode_count)], axis=0)
            partial[c] = source * inverse + scaled * partial[c]
            part_ref[k, c] = partial[c]
    low, high = low_ref[rows - 1], high_ref[rows - 1]
    for k in range(rows - 2, -1, -1):
        factor = high_ref[k]
        low = low_ref[k] + factor * low
        low_ref[k] = low
        high = factor * high
        high_ref[k] = high
        for c in range(2):
            partial[c] = part_ref[k, c] + factor * partial[c]
            part_ref[k, c] = partial[c]
    pair_table = side_ref[2 * 4 * height :, :]
    upside = lax.axis_index("gz") % 2 == 1
    put_map(maps_ref, (0,), spectral, lower, upper)
    put_map(maps_ref, (1,), spectral, couplings(table, 2, rows), couplings(table, 3, rows))
    lines = jnp.where(upside, pair_table[0:2], pair_table[2:4])
    put_map(maps_ref, (2,), spectral, couplings(lines, 0, rows), couplings(lines, 1, rows))


def put_level(sizes, level, d, message_ref, spectral, ref, lead):
    rows, total = sizes[0], spectral.shape[0]
    table = message_ref[4 * total :, :]
    lines = jnp.where((level ^ d) < level, table[0:2], table[2:4])
    put_map(ref, lead, spectral, couplings(lines, 0, 2 * rows), couplings(lines, 1, 2 * rows))


def level_kernel(sizes, d, spectral_ref, message_ref, map_ref):
    put_level(sizes, lax.axis_index("gz") // 2, d, message_ref, spectral_ref[...], map_ref, ())


def final_kernel(sizes, pairs, late, spectral_ref, side_ref, part_ref, low_ref, high_ref, maps_ref, *rest):
    rows, _, _, _, mode_count, height = sizes
    chips = mode_count // 2
    total = mode_count * height
    port = 4 * height
    pair_refs, rest = rest[: chips - 1], rest[chips - 1 :]
    messages, rest = rest[: pairs - 1], rest[pairs - 1 :]
    level_maps, (out_hbm, out_ref, late_ref, sems) = list(rest[: pairs - 2]), rest[pairs - 2 :]
    level_maps.insert(late - 1, late_ref)
    me, partition = lax.axis_index("modes"), lax.axis_index("gz")
    upside, level = partition % 2 == 1, partition // 2
    put_level(sizes, level, late, messages[late - 1], spectral_ref[...], late_ref, ())
    one = jnp.ones((total, LANES), jnp.float32)
    zero = jnp.zeros((total, LANES), jnp.float32)
    start = (one, one, zero, zero, zero)

    def cross(state, d, leave, entry):
        ref = messages[d - 1]
        ports = [ref[i * total : (i + 1) * total, :] for i in (leave, leave + 1, entry, entry + 1)]
        return apply_map(map_of(level_maps[d - 1], (), total), state, ports[:2], ports[2:])

    def cross_levels(z, state, at):
        leave, entry = (2, 0) if at < z else (0, 2)
        return cross(state, z ^ at, leave, entry)

    def at_level(z):
        def states():
            below, above = start, start
            for at in range(z):
                below = cross_levels(z, below, at)
            for at in range(pairs - 1, z, -1):
                above = cross_levels(z, above, at)
            return below, above

        return states

    def pair_ports(i):
        chunks = []
        for d in range(mode_count):
            at = i * height + (d % 2) * port
            chunks.append((side_ref if d < 2 else pair_refs[d // 2 - 1])[at : at + height, :])
        return jnp.concatenate(chunks, axis=0)

    below, above = lax.switch(level, [at_level(z) for z in range(pairs)])
    ports = [pair_ports(i) for i in range(4)]
    near_state = [jnp.where(upside, b, a) for b, a in zip(below, above)]
    leave = [jnp.where(upside, ports[2 + c], ports[c]) for c in range(2)]
    entry = [jnp.where(upside, ports[c], ports[2 + c]) for c in range(2)]
    crossed = apply_map(map_of(maps_ref, (2,), total), near_state, leave, entry)
    below = [jnp.where(upside, new, old) for new, old in zip(crossed, below)]
    above = [jnp.where(upside, old, new) for new, old in zip(crossed, above)]
    own_first, own_last = [part_ref[0, c] for c in range(2)], [part_ref[rows - 1, c] for c in range(2)]
    leaving_up = apply_map(map_of(maps_ref, (0,), total), below, own_last, own_first)
    leaving_down = apply_map(map_of(maps_ref, (1,), total), above, own_first, own_last)
    inverse_up = 1.0 / (leaving_up[0] * above[1] + leaving_up[2] * above[0])
    inverse_down = 1.0 / (leaving_down[0] * below[1] + leaving_down[2] * below[0])
    inverse_below, inverse_above = 1.0 / below[1], 1.0 / above[1]
    under, over = [], []
    for c in range(3, 5):
        last = (leaving_up[c] * above[1] + leaving_up[2] * above[c]) * inverse_up
        over.append((above[c] + above[2] * last) * inverse_above)
        first = (leaving_down[c] * below[1] + leaving_down[2] * below[c]) * inverse_down
        under.append((below[c] + below[2] * first) * inverse_below)
    copies = []
    for i, (first, size) in enumerate(chunks_of(rows)):
        for k in range(first, first + size):
            low, high = low_ref[k], high_ref[k]
            for c in range(2):
                value = part_ref[k, c] + low * under[c] + high * over[c]
                for d in range(mode_count):
                    out_ref[k, c, me ^ d] = value[d * height : (d + 1) * height]
        part = pl.ds(first, size)
        copies.append(pltpu.make_async_copy(out_ref.at[part], out_hbm.at[part], sems.at[i]))
        copies[-1].start()
    for copy in copies:
        copy.wait()


LIMIT = pltpu.CompilerParams(vmem_limit_bytes=16 << 20)
VMEM = pl.BlockSpec(memory_space=pltpu.VMEM)
ANY = pl.BlockSpec(memory_space=pl.ANY)


def near(*arrays):
    return [pltpu.with_memory_space_constraint(a, pltpu.VMEM) for a in arrays]


def solve(source_field, coupling_below, coupling_above, eigen_stream, eigen_span):
    sizes = rows, kx_total, kx_count, tiles, mode_count, height = sizes_of(source_field)
    partitions = lax.axis_size("gz")
    chips, pairs = mode_count // 2, partitions // 2
    total = mode_count * height
    f32 = jnp.float32
    chunk_sems = pltpu.SemaphoreType.DMA((len(chunks_of(rows)),))

    def move(array, modes_by=0, pair=0, level=0):
        links = []
        for m in range(mode_count):
            for g in range(partitions):
                to = ((g // 2) ^ level) * 2 + ((g % 2) ^ pair)
                links.append((m * partitions + g, (m ^ modes_by) * partitions + to))
        return lax.ppermute(array, ("modes", "gz"), links)

    span = eigen_span.reshape(-1, LANES)
    ports, table, spectral, source = pl.pallas_call(
        functools.partial(reduce_kernel, sizes),
        out_shape=(
            pltpu.VMEM((2, chips, 4 * height, LANES), f32),
            pltpu.VMEM((SUBLANES, LANES), f32),
            pltpu.VMEM((total, LANES), f32),
            pltpu.VMEM(source_field.shape, f32),
        ),
        in_specs=[ANY] * 5,
        out_specs=(VMEM,) * 4,
        scratch_shapes=[
            pltpu.SMEM(coupling_below.shape, f32),
            pltpu.SMEM(coupling_above.shape, f32),
            pltpu.SMEM(eigen_stream.shape, f32),
            pltpu.VMEM(span.shape, f32),
            pltpu.SemaphoreType.DMA((4,)),
            chunk_sems,
        ],
        name="reduce",
    )(coupling_below, coupling_above, eigen_stream, span, source_field)
    blocks = pl.pallas_call(
        functools.partial(regroup_kernel, sizes),
        out_shape=pltpu.VMEM((mode_count, rows, 2, height, LANES), f32),
        in_specs=[VMEM],
        out_specs=VMEM,
        name="regroup",
    )(*near(source))

    taken = move(ports[1], modes_by=1)
    own_parts, pair_parts = [], []
    for d in range(1, chips):
        block = jnp.concatenate([ports[0, d], taken[d]], axis=0)
        pair_parts.append(move(block, modes_by=2 * d, pair=1))
        own_parts.append(move(block, modes_by=2 * d))
    side = move(jnp.concatenate([ports[0, 0], taken[0], table], axis=0), pair=1)
    sources = [move(blocks[d], modes_by=d) if d else blocks[0] for d in range(mode_count)]
    message = pl.pallas_call(
        functools.partial(merge_kernel, sizes),
        out_shape=pltpu.VMEM((4 * total + SUBLANES, LANES), f32),
        in_specs=[VMEM] * (5 + 2 * (chips - 1)),
        out_specs=VMEM,
        name="merge",
    )(*near(spectral, table, ports, taken, side, *own_parts, *pair_parts))
    messages = [move(message, level=d) for d in range(1, pairs)]
    map_lines = MAP_PARTS * total
    *local, maps = pl.pallas_call(
        functools.partial(prepare_kernel, sizes),
        out_shape=(
            pltpu.VMEM((rows, 2, total, LANES), f32),
            pltpu.VMEM((rows, total, LANES), f32),
            pltpu.VMEM((rows, total, LANES), f32),
            pltpu.VMEM((3, map_lines, LANES), f32),
        ),
        in_specs=[VMEM] * (3 + mode_count),
        out_specs=(VMEM,) * 4,
        name="prepare",
    )(*near(spectral, table, side, *sources))
    late = late_level(pairs)
    level_maps = []
    for d in range(1, pairs):
        if d != late:
            level_maps.append(
                pl.pallas_call(
                    functools.partial(level_kernel, sizes, d),
                    out_shape=pltpu.VMEM((map_lines, LANES), f32),
                    in_specs=[VMEM] * 2,
                    out_specs=VMEM,
                    name="levels",
                )(*near(spectral, messages[d - 1]))
            )
    out = pl.pallas_call(
        functools.partial(final_kernel, sizes, pairs, late),
        out_shape=jax.ShapeDtypeStruct((rows, 2, mode_count, height, LANES), f32),
        in_specs=[VMEM] * (6 + (chips - 1) + (pairs - 1) + len(level_maps)),
        out_specs=ANY,
        scratch_shapes=[
            pltpu.VMEM((rows, 2, mode_count, height, LANES), f32),
            pltpu.VMEM((map_lines, LANES), f32),
            chunk_sems,
        ],
        name="solve",
        compiler_params=LIMIT,
    )(*near(spectral, side, *local, maps, *pair_parts, *messages, *level_maps))
    out = out.reshape(rows, 2, mode_count * tiles, kx_count, LANES).transpose(0, 1, 3, 2, 4)
    return out.reshape(rows, 2, kx_count, -1)


def late_level(pairs):
    return min(2, pairs - 1)


def solution(mesh):
    in_specs = (P("gz", None, None, "modes"), P("gz"), P("gz"), P(), P())
    out_specs = P("gz", None, "modes", None)
    return jax.shard_map(solve, mesh=mesh, in_specs=in_specs, out_specs=out_specs, check_vma=False)
```

```python
import functools

import jax
import jax.numpy as jnp
from jax import lax
from jax.experimental import pallas as pl
from jax.experimental.pallas import tpu as pltpu
from jax.sharding import PartitionSpec as P


LANES = 128
SUBLANES = 8


def sizes_of(source_field):
    rows, _, kx_total, ky_local = source_field.shape
    mode_count = lax.axis_size("modes")
    kx_count, tiles = kx_total // mode_count, ky_local // LANES
    return rows, kx_total, kx_count, tiles, mode_count, kx_count * tiles


def chunks_of(rows, count=4):
    size = rows // count if rows % count == 0 else rows
    return [(first, size) for first in range(0, rows, size)]


def fetch(pairs, sems):
    copies = [pltpu.make_async_copy(source, to, sems.at[i]) for i, (source, to) in enumerate(pairs)]
    for copy in copies:
        copy.start()
    return copies


def reduce_kernel(
    sizes, below_hbm, above_hbm, stream_hbm, span_hbm, source_hbm,
    ports_ref, table_ref, spectral_ref, source_ref, below_ref, above_ref, stream_ref, span_ref, small_sems, sems,
):
    rows, kx_total, kx_count, tiles, mode_count, height = sizes
    me, partition = lax.axis_index("modes"), lax.axis_index("gz")
    small = fetch(
        [(below_hbm, below_ref), (above_hbm, above_ref), (stream_hbm, stream_ref), (span_hbm, span_ref)], small_sems
    )
    parts = [pl.ds(first, size) for first, size in chunks_of(rows)]
    copies = fetch([(source_hbm.at[p], source_ref.at[p]) for p in parts], sems)
    for copy in small:
        copy.wait()
    lower = [below_ref[k] for k in range(rows)]
    upper = [above_ref[k] for k in range(rows)]
    lower[0] = jnp.where(partition == 0, 0.0, lower[0])
    upper[-1] = jnp.where(partition == lax.axis_size("gz") - 1, 0.0, upper[-1])
    lane = lax.broadcasted_iota(jnp.int32, (SUBLANES, LANES), 1)
    sub = lax.broadcasted_iota(jnp.int32, (SUBLANES, LANES), 0)
    table = jnp.zeros((SUBLANES, LANES), jnp.float32)
    for k in range(rows):
        table = jnp.where((lane == k) & (sub < 2), jnp.where(sub == 0, lower[k], upper[k]), table)
        table = jnp.where((lane == rows - 1 - k) & (sub >= 2), jnp.where(sub == 2, upper[k], lower[k]), table)
    table_ref[...] = table
    for d in range(mode_count):
        for t in range(tiles):
            for owner in range(2):
                spanwise = span_ref[pl.ds((me ^ owner ^ d) * tiles + t, 1), :]
                for j in range(kx_count):
                    at = d * height + t * kx_count + j
                    spectral_ref[owner, at : at + 1, :] = spanwise + stream_ref[(me ^ owner) * kx_count + j]
    shape = (kx_total, LANES)
    kx_at = lax.broadcasted_iota(jnp.int32, shape, 0)
    streamwise = jnp.zeros(shape, jnp.float32)
    for i in range(kx_total):
        streamwise = jnp.where(kx_at == i, stream_ref[i], streamwise)
    each = range(tiles)
    spectral = [streamwise + span_ref[pl.ds(me * tiles + t, 1), :] for t in each]
    one, zero = jnp.ones(shape, jnp.float32), jnp.zeros(shape, jnp.float32)
    grown, passed = [one] * tiles, [one] * tiles
    partial = [[zero] * tiles, [zero] * tiles]
    first_value = [[zero] * tiles, [zero] * tiles]
    starts = {first: i for i, (first, _) in enumerate(chunks_of(rows))}
    for k in range(rows):
        if k in starts:
            copies[starts[k]].wait()
        for t in each:
            held = spectral[t] + lower[k] * grown[t]
            inverse = 1.0 / (upper[k] + held)
            grown[t] = held * inverse
            for c in range(2):
                source = source_ref[k, c, :, t * LANES : (t + 1) * LANES]
                partial[c][t] = (source + lower[k] * partial[c][t]) * inverse
                first_value[c][t] = first_value[c][t] + passed[t] * partial[c][t]
            passed[t] = passed[t] * (upper[k] * inverse)
    values = first_value + partial
    for dest in range(mode_count):
        to = dest ^ me
        for i in range(4):
            for t in each:
                at = i * height + t * kx_count
                ports_ref[to % 2, to // 2, at : at + kx_count, :] = values[i][t][dest * kx_count : (dest + 1) * kx_count]


def regroup_kernel(sizes, source_ref, blocks_ref):
    rows, _, kx_count, tiles, mode_count, _ = sizes
    me = lax.axis_index("modes")
    for dest in range(mode_count):
        to = dest ^ me
        lines = slice(dest * kx_count, (dest + 1) * kx_count)
        for k in range(rows):
            for c in range(2):
                for t in range(tiles):
                    at = t * kx_count
                    blocks_ref[to, k, c, at : at + kx_count, :] = source_ref[k, c, lines, t * LANES : (t + 1) * LANES]


def couplings(table, line, count):
    return [table[line : line + 1, k : k + 1] for k in range(count)]


def climb(spectral, num, den, near, far):
    product = near[0]
    for k in range(len(near)):
        step = near[k] * num
        num = spectral * den + step
        den = (spectral + far[k]) * den + step
        if k:
            product = product * near[k]
    return num, den, product


MAP_PARTS = 5


def put_map(ref, lead, spectral, near, far):
    total = spectral.shape[0]
    num = [near[0] + jnp.zeros_like(spectral), spectral]
    den = [num[0], spectral + far[0]]
    product = near[0]
    for k in range(1, len(near)):
        held = spectral + far[k]
        step = [near[k] * num[i] for i in range(2)]
        num = [spectral * den[i] + step[i] for i in range(2)]
        den = [held * den[i] + step[i] for i in range(2)]
        product = product * near[k]
    scale = 1.0 / (den[0] + den[1])
    for i, value in enumerate([*num, *den, product]):
        ref[(*lead, slice(i * total, (i + 1) * total), slice(None))] = value * scale


def leave_with(state, new_den, product, leave, entry):
    num, den, *partial = state
    return [leave[c] * new_den + product * (partial[c] + (den - num) * entry[c]) for c in range(2)]


def apply_map(block, state, leave, entry):
    num, den = state[:2]
    new_den = block(2) * num + block(3) * den
    return (block(0) * num + block(1) * den, new_den, *leave_with(state, new_den, block(4), leave, entry))


def choose(condition, first, second):
    return [jnp.where(condition, a, b) for a, b in zip(first, second)]


def map_of(ref, lead, total):
    return lambda i: ref[(*lead, slice(i * total, (i + 1) * total), slice(None))]


def merge_kernel(sizes, spectral_ref, table_ref, own_ref, side_ref, *rest):
    rows, _, _, _, mode_count, height = sizes
    chips = mode_count // 2
    own_refs, pair_refs, message_ref = rest[: chips - 1], rest[chips - 1 : 2 * (chips - 1)], rest[-1]
    total = mode_count * height
    port = 4 * height
    upside = lax.axis_index("gz") % 2 == 1

    def gather(i, chunk):
        return jnp.concatenate([chunk(d, i * height) for d in range(mode_count)], axis=0)

    def own_chunk(d, at):
        start = (d % 2) * port + at
        return (own_ref if d < 2 else own_refs[d // 2 - 1])[start : start + height, :]

    def pair_chunk(d, at):
        start = (d % 2) * port + at
        ref = side_ref if d < 2 else pair_refs[d // 2 - 1]
        return ref[start : start + height, :]

    own_table, pair_table = table_ref[...], side_ref[2 * port :, :]
    low_table = jnp.where(upside, pair_table, own_table)
    high_table = jnp.where(upside, own_table, pair_table)
    sub = lax.broadcasted_iota(jnp.int32, (SUBLANES, LANES), 0)
    lane = lax.broadcasted_iota(jnp.int32, (SUBLANES, LANES), 1)
    ahead = jnp.where(sub < 2, low_table, high_table)
    behind = jnp.where(sub < 2, high_table, low_table)
    message_ref[4 * total :, :] = jnp.where(lane < rows, ahead, pltpu.roll(behind, rows, 1))
    spectral = spectral_ref[...]
    one = jnp.ones((total, LANES), jnp.float32)
    own = [gather(i, own_chunk) for i in range(4)]
    pair = [gather(i, pair_chunk) for i in range(4)]
    low = [jnp.where(upside, b, a) for a, b in zip(own, pair)]
    high = [jnp.where(upside, a, b) for a, b in zip(own, pair)]

    def store(i, value):
        message_ref[i * total : (i + 1) * total, :] = value

    for near_line, first, second, near_side, far_side in ((0, low_table, high_table, 0, 2), (2, high_table, low_table, 2, 0)):
        lines = (near_line, near_line + 1)
        num, den, _ = climb(spectral, one, one, *(couplings(first, i, rows) for i in lines))
        passed = (den - num) / den
        _, den_all, product = climb(spectral, num, den, *(couplings(second, i, rows) for i in lines))
        ratio = product * den / den_all
        before, after = (low, high) if near_line == 0 else (high, low)
        for c in range(2):
            store(far_side + c, after[far_side + c] + ratio * (before[far_side + c] + passed * after[near_side + c]))


def prepare_kernel(sizes, spectral_ref, table_ref, side_ref, *rest):
    rows, _, _, _, mode_count, height = sizes
    sources, (part_ref, low_ref, high_ref, maps_ref) = rest[:mode_count], rest[mode_count:]
    spectral, table = spectral_ref[...], table_ref[...]
    lower, upper = couplings(table, 0, rows), couplings(table, 1, rows)
    grown = jnp.ones(spectral.shape, jnp.float32)
    carried = grown
    partial = [jnp.zeros(spectral.shape, jnp.float32)] * 2
    for k in range(rows):
        held = spectral + lower[k] * grown
        inverse = 1.0 / (upper[k] + held)
        grown = held * inverse
        scaled = lower[k] * inverse
        carried = scaled * carried
        low_ref[k] = carried
        high_ref[k] = upper[k] * inverse
        for c in range(2):
            source = jnp.concatenate([sources[d][k, c] for d in range(mode_count)], axis=0)
            partial[c] = source * inverse + scaled * partial[c]
            part_ref[k, c] = partial[c]
    low, high = low_ref[rows - 1], high_ref[rows - 1]
    for k in range(rows - 2, -1, -1):
        factor = high_ref[k]
        low = low_ref[k] + factor * low
        low_ref[k] = low
        high = factor * high
        high_ref[k] = high
        for c in range(2):
            partial[c] = part_ref[k, c] + factor * partial[c]
            part_ref[k, c] = partial[c]
    pair_table = side_ref[2 * 4 * height :, :]
    upside = lax.axis_index("gz") % 2 == 1
    put_map(maps_ref, (0,), spectral, lower, upper)
    put_map(maps_ref, (1,), spectral, couplings(table, 2, rows), couplings(table, 3, rows))
    lines = jnp.where(upside, pair_table[0:2], pair_table[2:4])
    put_map(maps_ref, (2,), spectral, couplings(lines, 0, rows), couplings(lines, 1, rows))


def level_couplings(sizes, message_ref, total, downwards):
    table = message_ref[4 * total :, :]
    lines = jnp.where(downwards, table[2:4], table[0:2])
    return couplings(lines, 0, 2 * sizes[0]), couplings(lines, 1, 2 * sizes[0])


def level_kernel(sizes, d, spectral_ref, message_ref, map_ref):
    level = lax.axis_index("gz") // 2
    spectral = spectral_ref[...]
    put_map(map_ref, (), spectral, *level_couplings(sizes, message_ref, spectral.shape[0], (level ^ d) > level))


def quad_kernel(sizes, spectral_ref, own_ref, neighbour_ref, edge_ref):
    spectral = spectral_ref[...]
    total = spectral.shape[0]
    level = lax.axis_index("gz") // 2
    lower, outer = level < 2, (level == 0) | (level == 3)

    def ports(ref, at):
        return [ref[(at + c) * total : (at + c + 1) * total, :] for c in range(2)]

    def of(ref):
        return choose(lower, ports(ref, 2), ports(ref, 0)), choose(lower, ports(ref, 0), ports(ref, 2))

    own, neighbour = of(own_ref), of(neighbour_ref)
    leave_first = choose(outer, own[0], neighbour[0])
    leave_then, entry_then = choose(outer, neighbour[0], own[0]), choose(outer, neighbour[1], own[1])
    own_table, neighbour_table = own_ref[4 * total :, :], neighbour_ref[4 * total :, :]
    own_lines = jnp.where(lower, own_table[0:2], own_table[2:4])
    neighbour_lines = jnp.where(lower, neighbour_table[0:2], neighbour_table[2:4])
    first, then = jnp.where(outer, own_lines, neighbour_lines), jnp.where(outer, neighbour_lines, own_lines)
    count = 2 * sizes[0]
    one = jnp.ones_like(spectral)
    num, den, _ = climb(spectral, one, one, couplings(first, 0, count), couplings(first, 1, count))
    scale = 1.0 / den
    state = (num * scale, one, *leave_first)
    num, den, product = climb(spectral, state[0], one, couplings(then, 0, count), couplings(then, 1, count))
    scale = 1.0 / den
    for i, value in enumerate([num, *leave_with(state, den, product, leave_then, entry_then)]):
        edge_ref[i * total : (i + 1) * total, :] = value * scale


def quads_kernel(sizes, part_ref, low_ref, high_ref, maps_ref, neighbour_map, neighbour_ref, other_ref, side_ref, *rest):
    _, _, _, _, mode_count, height = sizes
    total = mode_count * height
    pair_refs, (out_hbm, out_ref, sems) = rest[: mode_count // 2 - 1], rest[mode_count // 2 - 1 :]
    level = lax.axis_index("gz") // 2
    odd, outer = level % 2 == 1, (level == 0) | (level == 3)
    one, zero = jnp.ones((total, LANES), jnp.float32), jnp.zeros((total, LANES), jnp.float32)
    wall = (one, one, zero, zero)
    values = [other_ref[i * total : (i + 1) * total, :] for i in range(3)]
    other = (values[0], one, *values[1:])
    ports = [neighbour_ref[i * total : (i + 1) * total, :] for i in range(4)]
    leave, entry = choose(odd, ports[2:], ports[:2]), choose(odd, ports[:2], ports[2:])
    crossed = apply_map(map_of(neighbour_map, (), total), choose(outer, other, wall), leave, entry)
    plain = choose(outer, wall, other)
    below, above = choose(odd, crossed, plain), choose(odd, plain, crossed)
    finish(sizes, below, above, part_ref, low_ref, high_ref, maps_ref, side_ref, pair_refs, out_hbm, out_ref, sems)


def levels_kernel(sizes, pairs, late, spectral_ref, side_ref, part_ref, low_ref, high_ref, maps_ref, *rest):
    _, _, _, _, mode_count, height = sizes
    chips = mode_count // 2
    total = mode_count * height
    pair_refs, rest = rest[: chips - 1], rest[chips - 1 :]
    messages, rest = rest[: pairs - 1], rest[pairs - 1 :]
    level_maps, (out_hbm, out_ref, sems) = list(rest[: pairs - 2]), rest[pairs - 2 :]
    level_maps.insert(late - 1, None)
    spectral = spectral_ref[...]
    level = lax.axis_index("gz") // 2
    late_near, late_far = level_couplings(sizes, messages[late - 1], total, (level ^ late) > level)
    one, zero = jnp.ones((total, LANES), jnp.float32), jnp.zeros((total, LANES), jnp.float32)
    start = (one, one, zero, zero)

    def cross(state, d, leave, entry):
        ref = messages[d - 1]
        ports = [ref[i * total : (i + 1) * total, :] for i in (leave, leave + 1, entry, entry + 1)]
        if d != late:
            return apply_map(map_of(level_maps[d - 1], (), total), state, ports[:2], ports[2:])
        num, den, product = climb(spectral, *state[:2], late_near, late_far)
        return (num, den, *leave_with(state, den, product, ports[:2], ports[2:]))

    def cross_all(z, ats):
        state = start
        for i, at in enumerate(ats):
            if i and i % 4 == 0:
                inverse = 1.0 / state[1]
                state = tuple(value * inverse for value in state)
            state = cross(state, z ^ at, *((2, 0) if at < z else (0, 2)))
        return state

    def at_level(z):
        return lambda: (cross_all(z, range(z)), cross_all(z, range(pairs - 1, z, -1)))

    below, above = lax.switch(level, [at_level(z) for z in range(pairs)])
    finish(sizes, below, above, part_ref, low_ref, high_ref, maps_ref, side_ref, pair_refs, out_hbm, out_ref, sems)


def finish(sizes, below, above, part_ref, low_ref, high_ref, maps_ref, side_ref, pair_refs, out_hbm, out_ref, sems):
    rows, _, _, _, mode_count, height = sizes
    total = mode_count * height
    port = 4 * height
    me, upside = lax.axis_index("modes"), lax.axis_index("gz") % 2 == 1

    def pair_ports(i):
        chunks = []
        for d in range(mode_count):
            at = i * height + (d % 2) * port
            chunks.append((side_ref if d < 2 else pair_refs[d // 2 - 1])[at : at + height, :])
        return jnp.concatenate(chunks, axis=0)

    ports = [pair_ports(i) for i in range(4)]
    leave, entry = choose(upside, ports[2:], ports[:2]), choose(upside, ports[:2], ports[2:])
    crossed = apply_map(map_of(maps_ref, (2,), total), choose(upside, below, above), leave, entry)
    below, above = choose(upside, crossed, below), choose(upside, above, crossed)
    own_first, own_last = [part_ref[0, c] for c in range(2)], [part_ref[rows - 1, c] for c in range(2)]
    up = apply_map(map_of(maps_ref, (0,), total), below, own_last, own_first)
    down = apply_map(map_of(maps_ref, (1,), total), above, own_first, own_last)
    up_passed, down_passed = up[1] - up[0], down[1] - down[0]
    inverse_up = 1.0 / (up[0] * above[1] + up_passed * above[0])
    inverse_down = 1.0 / (down[0] * below[1] + down_passed * below[0])
    inverse_below, inverse_above = 1.0 / below[1], 1.0 / above[1]
    under, over = [], []
    for c in range(2, 4):
        last = (up[c] * above[1] + up_passed * above[c]) * inverse_up
        over.append((above[c] + (above[1] - above[0]) * last) * inverse_above)
        first = (down[c] * below[1] + down_passed * below[c]) * inverse_down
        under.append((below[c] + (below[1] - below[0]) * first) * inverse_below)
    copies = []
    for i, (first, size) in enumerate(chunks_of(rows)):
        for k in range(first, first + size):
            low, high = low_ref[k], high_ref[k]
            for c in range(2):
                value = part_ref[k, c] + low * under[c] + high * over[c]
                for d in range(mode_count):
                    out_ref[k, c, me ^ d] = value[d * height : (d + 1) * height]
        part = pl.ds(first, size)
        copies.append(pltpu.make_async_copy(out_ref.at[part], out_hbm.at[part], sems.at[i]))
        copies[-1].start()
    for copy in copies:
        copy.wait()


LIMIT = pltpu.CompilerParams(vmem_limit_bytes=16 << 20)
VMEM = pl.BlockSpec(memory_space=pltpu.VMEM)
ANY = pl.BlockSpec(memory_space=pl.ANY)


def near(*arrays):
    return [pltpu.with_memory_space_constraint(a, pltpu.VMEM) for a in arrays]


def solve(source_field, coupling_below, coupling_above, eigen_stream, eigen_span):
    sizes = rows, kx_total, kx_count, tiles, mode_count, height = sizes_of(source_field)
    partitions = lax.axis_size("gz")
    chips, pairs = mode_count // 2, partitions // 2
    total = mode_count * height
    f32 = jnp.float32
    chunk_sems = pltpu.SemaphoreType.DMA((len(chunks_of(rows)),))

    def move(array, modes_by=0, pair=0, level=0, core=lambda z: 0):
        links = []
        for m in range(mode_count):
            for g in range(partitions):
                to = ((g // 2) ^ level) * 2 + ((g % 2) ^ pair)
                links.append((m * partitions + g, (m ^ modes_by ^ core(g // 2)) * partitions + to))
        return lax.ppermute(array, ("modes", "gz"), links)

    span = eigen_span.reshape(-1, LANES)
    ports, table, spectral, source = pl.pallas_call(
        functools.partial(reduce_kernel, sizes),
        out_shape=(
            pltpu.VMEM((2, chips, 4 * height, LANES), f32),
            pltpu.VMEM((SUBLANES, LANES), f32),
            pltpu.VMEM((2, total, LANES), f32),
            pltpu.VMEM(source_field.shape, f32),
        ),
        in_specs=[ANY] * 5,
        out_specs=(VMEM,) * 4,
        scratch_shapes=[
            pltpu.SMEM(coupling_below.shape, f32),
            pltpu.SMEM(coupling_above.shape, f32),
            pltpu.SMEM(eigen_stream.shape, f32),
            pltpu.VMEM(span.shape, f32),
            pltpu.SemaphoreType.DMA((4,)),
            chunk_sems,
        ],
        name="reduce",
    )(coupling_below, coupling_above, eigen_stream, span, source_field)
    blocks = pl.pallas_call(
        functools.partial(regroup_kernel, sizes),
        out_shape=pltpu.VMEM((mode_count, rows, 2, height, LANES), f32),
        in_specs=[VMEM],
        out_specs=VMEM,
        name="regroup",
    )(*near(source))

    quads = pairs == 4
    even = (lax.axis_index("gz") // 2) % 2 == 0
    swapped = (lambda z: 1 - z % 2) if quads else (lambda z: 0)
    if quads:
        taken = move(ports, modes_by=1)
        theirs = taken[1]
    else:
        theirs = move(ports[1], modes_by=1)
    blocks_out = [jnp.concatenate([ports[0, d], theirs[d]], axis=0) for d in range(chips)]
    own_parts, pair_parts = [], []
    for d in range(1, chips):
        pair_parts.append(move(blocks_out[d], modes_by=2 * d, pair=1, core=swapped))
        own_parts.append(move(blocks_out[d], modes_by=2 * d, core=swapped))
    side = move(jnp.concatenate([blocks_out[0], table], axis=0), pair=1, core=swapped)
    sources = [move(blocks[d], modes_by=d) if d else blocks[0] for d in range(mode_count)]
    both_spectral = spectral
    own_block, merged_spectral, spectral = blocks_out[0], spectral[0], spectral[0]
    if quads:
        own_block = jnp.where(even, jnp.concatenate([taken[0, 0], ports[1, 0]], axis=0), own_block)
        merged_spectral = jnp.where(even, both_spectral[1], spectral)
    message = pl.pallas_call(
        functools.partial(merge_kernel, sizes),
        out_shape=pltpu.VMEM((4 * total + SUBLANES, LANES), f32),
        in_specs=[VMEM] * (4 + 2 * (chips - 1)),
        out_specs=VMEM,
        name="merge",
    )(*near(merged_spectral, table, own_block, side, *own_parts, *pair_parts))
    if quads:
        messages = [move(message, modes_by=1, level=1)]
        edge = pl.pallas_call(
            functools.partial(quad_kernel, sizes),
            out_shape=pltpu.VMEM((3 * total, LANES), f32),
            in_specs=[VMEM] * 3,
            out_specs=VMEM,
            name="quad",
        )(*near(merged_spectral, message, messages[0]))
        other = move(edge, level=2, core=swapped)
        parcel = jnp.concatenate([side, *pair_parts, messages[0][: 4 * total]], axis=0)
        parcel = jnp.where(even, move(parcel, modes_by=1), parcel)
        lines = side.shape[0]
        owned = [parcel[lines * 0 : lines]]
        for d in range(1, chips):
            owned.append(parcel[lines + (d - 1) * 8 * height : lines + d * 8 * height])
        owned_neighbour = parcel[lines + (chips - 1) * 8 * height :]
    else:
        messages = [move(message, level=d) for d in range(1, pairs)]
    map_lines = MAP_PARTS * total
    *local, maps = pl.pallas_call(
        functools.partial(prepare_kernel, sizes),
        out_shape=(
            pltpu.VMEM((rows, 2, total, LANES), f32),
            pltpu.VMEM((rows, total, LANES), f32),
            pltpu.VMEM((rows, total, LANES), f32),
            pltpu.VMEM((3, map_lines, LANES), f32),
        ),
        in_specs=[VMEM] * (3 + mode_count),
        out_specs=(VMEM,) * 4,
        name="prepare",
    )(*near(spectral, table, side, *sources))
    late = None if quads else late_level(pairs)
    level_maps = []
    for d in range(1, 2 if quads else pairs):
        if d != late:
            level_maps.append(
                pl.pallas_call(
                    functools.partial(level_kernel, sizes, d),
                    out_shape=pltpu.VMEM((map_lines, LANES), f32),
                    in_specs=[VMEM] * 2,
                    out_specs=VMEM,
                    name="levels",
                )(*near(spectral, messages[d - 1]))
            )
    if quads:
        kernel = functools.partial(quads_kernel, sizes)
        operands = (*local, maps, level_maps[0], owned_neighbour, other, *owned)
    else:
        kernel = functools.partial(levels_kernel, sizes, pairs, late)
        operands = (spectral, side, *local, maps, *pair_parts, *messages, *level_maps)
    out = pl.pallas_call(
        kernel,
        out_shape=jax.ShapeDtypeStruct((rows, 2, mode_count, height, LANES), f32),
        in_specs=[VMEM] * len(operands),
        out_specs=ANY,
        scratch_shapes=[pltpu.VMEM((rows, 2, mode_count, height, LANES), f32), chunk_sems],
        name="solve",
        compiler_params=LIMIT,
    )(*near(*operands))
    out = out.reshape(rows, 2, mode_count * tiles, kx_count, LANES).transpose(0, 1, 3, 2, 4)
    return out.reshape(rows, 2, kx_count, -1)


def late_level(pairs):
    return min(2, pairs - 1)


def solution(mesh):
    in_specs = (P("gz", None, None, "modes"), P("gz"), P("gz"), P(), P())
    out_specs = P("gz", None, "modes", None)
    return jax.shard_map(solve, mesh=mesh, in_specs=in_specs, out_specs=out_specs, check_vma=False)
```

```python
import functools

import jax
import jax.numpy as jnp
from jax import lax
from jax.experimental import pallas as pl
from jax.experimental.pallas import tpu as pltpu
from jax.sharding import PartitionSpec as P


LANES = 128
SUBLANES = 8


def sizes_of(source_field):
    rows, _, kx_total, ky_local = source_field.shape
    mode_count = lax.axis_size("modes")
    kx_count, tiles = kx_total // mode_count, ky_local // LANES
    return rows, kx_total, kx_count, tiles, mode_count, kx_count * tiles


def chunks_of(rows, count=4):
    size = rows // count if rows % count == 0 else rows
    return [(first, size) for first in range(0, rows, size)]


def fetch(pairs, sems):
    copies = [pltpu.make_async_copy(source, to, sems.at[i]) for i, (source, to) in enumerate(pairs)]
    for copy in copies:
        copy.start()
    return copies


def reduce_kernel(
    sizes, below_hbm, above_hbm, stream_hbm, span_hbm, source_hbm,
    ports_ref, table_ref, spectral_ref, source_ref, below_ref, above_ref, stream_ref, span_ref, small_sems, sems,
):
    rows, kx_total, kx_count, tiles, mode_count, height = sizes
    me, partition = lax.axis_index("modes"), lax.axis_index("gz")
    small = fetch(
        [(below_hbm, below_ref), (above_hbm, above_ref), (stream_hbm, stream_ref), (span_hbm, span_ref)], small_sems
    )
    parts = [pl.ds(first, size) for first, size in chunks_of(rows)]
    copies = fetch([(source_hbm.at[p], source_ref.at[p]) for p in parts], sems)
    for copy in small:
        copy.wait()
    lower = [below_ref[k] for k in range(rows)]
    upper = [above_ref[k] for k in range(rows)]
    lower[0] = jnp.where(partition == 0, 0.0, lower[0])
    upper[-1] = jnp.where(partition == lax.axis_size("gz") - 1, 0.0, upper[-1])
    lane = lax.broadcasted_iota(jnp.int32, (SUBLANES, LANES), 1)
    sub = lax.broadcasted_iota(jnp.int32, (SUBLANES, LANES), 0)
    table = jnp.zeros((SUBLANES, LANES), jnp.float32)
    for k in range(rows):
        table = jnp.where((lane == k) & (sub < 2), jnp.where(sub == 0, lower[k], upper[k]), table)
        table = jnp.where((lane == rows - 1 - k) & (sub >= 2), jnp.where(sub == 2, upper[k], lower[k]), table)
    table_ref[...] = table
    for d in range(mode_count):
        for t in range(tiles):
            for owner in range(2):
                spanwise = span_ref[pl.ds((me ^ owner ^ d) * tiles + t, 1), :]
                for j in range(kx_count):
                    at = d * height + t * kx_count + j
                    spectral_ref[owner, at : at + 1, :] = spanwise + stream_ref[(me ^ owner) * kx_count + j]
    shape = (kx_total, LANES)
    kx_at = lax.broadcasted_iota(jnp.int32, shape, 0)
    streamwise = jnp.zeros(shape, jnp.float32)
    for i in range(kx_total):
        streamwise = jnp.where(kx_at == i, stream_ref[i], streamwise)
    each = range(tiles)
    spectral = [streamwise + span_ref[pl.ds(me * tiles + t, 1), :] for t in each]
    one, zero = jnp.ones(shape, jnp.float32), jnp.zeros(shape, jnp.float32)
    grown, passed = [one] * tiles, [one] * tiles
    partial = [[zero] * tiles, [zero] * tiles]
    first_value = [[zero] * tiles, [zero] * tiles]
    starts = {first: i for i, (first, _) in enumerate(chunks_of(rows))}
    for k in range(rows):
        if k in starts:
            copies[starts[k]].wait()
        for t in each:
            held = spectral[t] + lower[k] * grown[t]
            inverse = 1.0 / (upper[k] + held)
            grown[t] = held * inverse
            for c in range(2):
                source = source_ref[k, c, :, t * LANES : (t + 1) * LANES]
                partial[c][t] = (source + lower[k] * partial[c][t]) * inverse
                first_value[c][t] = first_value[c][t] + passed[t] * partial[c][t]
            passed[t] = passed[t] * (upper[k] * inverse)
    values = first_value + partial
    for dest in range(mode_count):
        to = dest ^ me
        for i in range(4):
            for t in each:
                at = i * height + t * kx_count
                ports_ref[to % 2, to // 2, at : at + kx_count, :] = values[i][t][dest * kx_count : (dest + 1) * kx_count]


def regroup_kernel(sizes, source_ref, blocks_ref):
    rows, _, kx_count, tiles, mode_count, _ = sizes
    me = lax.axis_index("modes")
    for dest in range(mode_count):
        to = dest ^ me
        lines = slice(dest * kx_count, (dest + 1) * kx_count)
        for k in range(rows):
            for c in range(2):
                for t in range(tiles):
                    at = t * kx_count
                    blocks_ref[to, k, c, at : at + kx_count, :] = source_ref[k, c, lines, t * LANES : (t + 1) * LANES]


def couplings(table, line, count):
    return [table[line : line + 1, k : k + 1] for k in range(count)]


def climb(spectral, num, den, near, far):
    product = near[0]
    for k in range(len(near)):
        step = near[k] * num
        num = spectral * den + step
        den = (spectral + far[k]) * den + step
        if k:
            product = product * near[k]
    return num, den, product


MAP_PARTS = 5


def put_map(ref, lead, spectral, near, far):
    total = spectral.shape[0]
    num = [near[0] + jnp.zeros_like(spectral), spectral]
    den = [num[0], spectral + far[0]]
    product = near[0]
    for k in range(1, len(near)):
        held = spectral + far[k]
        step = [near[k] * num[i] for i in range(2)]
        num = [spectral * den[i] + step[i] for i in range(2)]
        den = [held * den[i] + step[i] for i in range(2)]
        product = product * near[k]
    scale = 1.0 / (den[0] + den[1])
    for i, value in enumerate([*num, *den, product]):
        ref[(*lead, slice(i * total, (i + 1) * total), slice(None))] = value * scale


def leave_with(state, new_den, product, leave, entry):
    num, den, *partial = state
    return [leave[c] * new_den + product * (partial[c] + (den - num) * entry[c]) for c in range(2)]


def apply_map(block, state, leave, entry):
    num, den = state[:2]
    new_den = block(2) * num + block(3) * den
    return (block(0) * num + block(1) * den, new_den, *leave_with(state, new_den, block(4), leave, entry))


def choose(condition, first, second):
    return [jnp.where(condition, a, b) for a, b in zip(first, second)]


def map_of(ref, lead, total):
    return lambda i: ref[(*lead, slice(i * total, (i + 1) * total), slice(None))]


def merge_kernel(sizes, spectral_ref, table_ref, own_ref, side_ref, *rest):
    rows, _, _, _, mode_count, height = sizes
    chips = mode_count // 2
    own_refs, pair_refs, message_ref = rest[: chips - 1], rest[chips - 1 : 2 * (chips - 1)], rest[-1]
    total = mode_count * height
    port = 4 * height
    upside = lax.axis_index("gz") % 2 == 1

    def gather(i, chunk):
        return jnp.concatenate([chunk(d, i * height) for d in range(mode_count)], axis=0)

    def own_chunk(d, at):
        start = (d % 2) * port + at
        return (own_ref if d < 2 else own_refs[d // 2 - 1])[start : start + height, :]

    def pair_chunk(d, at):
        start = (d % 2) * port + at
        ref = side_ref if d < 2 else pair_refs[d // 2 - 1]
        return ref[start : start + height, :]

    own_table, pair_table = table_ref[...], side_ref[2 * port :, :]
    low_table = jnp.where(upside, pair_table, own_table)
    high_table = jnp.where(upside, own_table, pair_table)
    sub = lax.broadcasted_iota(jnp.int32, (SUBLANES, LANES), 0)
    lane = lax.broadcasted_iota(jnp.int32, (SUBLANES, LANES), 1)
    ahead = jnp.where(sub < 2, low_table, high_table)
    behind = jnp.where(sub < 2, high_table, low_table)
    message_ref[4 * total :, :] = jnp.where(lane < rows, ahead, pltpu.roll(behind, rows, 1))
    spectral = spectral_ref[...]
    one = jnp.ones((total, LANES), jnp.float32)
    own = [gather(i, own_chunk) for i in range(4)]
    pair = [gather(i, pair_chunk) for i in range(4)]
    low = [jnp.where(upside, b, a) for a, b in zip(own, pair)]
    high = [jnp.where(upside, a, b) for a, b in zip(own, pair)]

    def store(i, value):
        message_ref[i * total : (i + 1) * total, :] = value

    for near_line, first, second, near_side, far_side in ((0, low_table, high_table, 0, 2), (2, high_table, low_table, 2, 0)):
        lines = (near_line, near_line + 1)
        num, den, _ = climb(spectral, one, one, *(couplings(first, i, rows) for i in lines))
        passed = (den - num) / den
        _, den_all, product = climb(spectral, num, den, *(couplings(second, i, rows) for i in lines))
        ratio = product * den / den_all
        before, after = (low, high) if near_line == 0 else (high, low)
        for c in range(2):
            store(far_side + c, after[far_side + c] + ratio * (before[far_side + c] + passed * after[near_side + c]))


def prepare_kernel(sizes, spectral_ref, table_ref, side_ref, *rest):
    rows, _, _, _, mode_count, height = sizes
    sources, (part_ref, low_ref, high_ref, maps_ref) = rest[:mode_count], rest[mode_count:]
    spectral, table = spectral_ref[...], table_ref[...]
    lower, upper = couplings(table, 0, rows), couplings(table, 1, rows)
    grown = jnp.ones(spectral.shape, jnp.float32)
    carried = grown
    partial = [jnp.zeros(spectral.shape, jnp.float32)] * 2
    for k in range(rows):
        held = spectral + lower[k] * grown
        inverse = 1.0 / (upper[k] + held)
        grown = held * inverse
        scaled = lower[k] * inverse
        carried = scaled * carried
        low_ref[k] = carried
        high_ref[k] = upper[k] * inverse
        for c in range(2):
            source = jnp.concatenate([sources[d][k, c] for d in range(mode_count)], axis=0)
            partial[c] = source * inverse + scaled * partial[c]
            part_ref[k, c] = partial[c]
    low, high = low_ref[rows - 1], high_ref[rows - 1]
    for k in range(rows - 2, -1, -1):
        factor = high_ref[k]
        low = low_ref[k] + factor * low
        low_ref[k] = low
        high = factor * high
        high_ref[k] = high
        for c in range(2):
            partial[c] = part_ref[k, c] + factor * partial[c]
            part_ref[k, c] = partial[c]
    pair_table = side_ref[2 * 4 * height :, :]
    upside = lax.axis_index("gz") % 2 == 1
    put_map(maps_ref, (0,), spectral, lower, upper)
    put_map(maps_ref, (1,), spectral, couplings(table, 2, rows), couplings(table, 3, rows))
    lines = jnp.where(upside, pair_table[0:2], pair_table[2:4])
    put_map(maps_ref, (2,), spectral, couplings(lines, 0, rows), couplings(lines, 1, rows))


def level_couplings(sizes, message_ref, total, downwards):
    table = message_ref[4 * total :, :]
    lines = jnp.where(downwards, table[2:4], table[0:2])
    return couplings(lines, 0, 2 * sizes[0]), couplings(lines, 1, 2 * sizes[0])


def level_kernel(sizes, d, spectral_ref, message_ref, map_ref):
    level = lax.axis_index("gz") // 2
    spectral = spectral_ref[...]
    put_map(map_ref, (), spectral, *level_couplings(sizes, message_ref, spectral.shape[0], (level ^ d) > level))


def ahead_kernel(sizes, spectral_ref, own_ref, map_ref):
    spectral = spectral_ref[...]
    lower = lax.axis_index("gz") // 2 < 2
    put_map(map_ref, (), spectral, *level_couplings(sizes, own_ref, spectral.shape[0], jnp.logical_not(lower)))


def quad_kernel(sizes, spectral_ref, map_ref, own_ref, neighbour_ref, edge_ref):
    spectral = spectral_ref[...]
    total = spectral.shape[0]
    level = lax.axis_index("gz") // 2
    lower, outer = level < 2, (level == 0) | (level == 3)

    def ports(ref):
        low, high = ([ref[(at + c) * total : (at + c + 1) * total, :] for c in range(2)] for at in (0, 2))
        return choose(lower, high, low), choose(lower, low, high)

    own, neighbour = ports(own_ref), ports(neighbour_ref)
    own_map = map_of(map_ref, (), total)
    one, zero = jnp.ones_like(spectral), jnp.zeros_like(spectral)
    start = choose(outer, (own_map(0) + own_map(1), one, *own[0]), (one, one, zero, zero))
    num, den, product = climb(
        spectral, start[0], one, *level_couplings(sizes, neighbour_ref, total, jnp.logical_not(lower))
    )
    passed = (num, den, *leave_with(start, den, product, *neighbour))
    num, den, *partial = choose(outer, passed, apply_map(own_map, passed, *own))
    scale = 1.0 / den
    for i, value in enumerate([num, *partial]):
        edge_ref[i * total : (i + 1) * total, :] = value * scale


def quads_kernel(sizes, part_ref, low_ref, high_ref, maps_ref, neighbour_map, neighbour_ref, other_ref, side_ref, *rest):
    _, _, _, _, mode_count, height = sizes
    total = mode_count * height
    pair_refs, (out_hbm, out_ref, sems) = rest[: mode_count // 2 - 1], rest[mode_count // 2 - 1 :]
    level = lax.axis_index("gz") // 2
    odd, outer = level % 2 == 1, (level == 0) | (level == 3)
    one, zero = jnp.ones((total, LANES), jnp.float32), jnp.zeros((total, LANES), jnp.float32)
    wall = (one, one, zero, zero)
    values = [other_ref[i * total : (i + 1) * total, :] for i in range(3)]
    other = (values[0], one, *values[1:])
    ports = [neighbour_ref[i * total : (i + 1) * total, :] for i in range(4)]
    leave, entry = choose(odd, ports[2:], ports[:2]), choose(odd, ports[:2], ports[2:])
    crossed = apply_map(map_of(neighbour_map, (), total), choose(outer, other, wall), leave, entry)
    plain = choose(outer, wall, other)
    below, above = choose(odd, crossed, plain), choose(odd, plain, crossed)
    finish(sizes, below, above, part_ref, low_ref, high_ref, maps_ref, side_ref, pair_refs, out_hbm, out_ref, sems)


def levels_kernel(sizes, pairs, late, spectral_ref, side_ref, part_ref, low_ref, high_ref, maps_ref, *rest):
    _, _, _, _, mode_count, height = sizes
    chips = mode_count // 2
    total = mode_count * height
    pair_refs, rest = rest[: chips - 1], rest[chips - 1 :]
    messages, rest = rest[: pairs - 1], rest[pairs - 1 :]
    level_maps, (out_hbm, out_ref, sems) = list(rest[: pairs - 2]), rest[pairs - 2 :]
    level_maps.insert(late - 1, None)
    spectral = spectral_ref[...]
    level = lax.axis_index("gz") // 2
    late_near, late_far = level_couplings(sizes, messages[late - 1], total, (level ^ late) > level)
    one, zero = jnp.ones((total, LANES), jnp.float32), jnp.zeros((total, LANES), jnp.float32)
    start = (one, one, zero, zero)

    def cross(state, d, leave, entry):
        ref = messages[d - 1]
        ports = [ref[i * total : (i + 1) * total, :] for i in (leave, leave + 1, entry, entry + 1)]
        if d != late:
            return apply_map(map_of(level_maps[d - 1], (), total), state, ports[:2], ports[2:])
        num, den, product = climb(spectral, *state[:2], late_near, late_far)
        return (num, den, *leave_with(state, den, product, ports[:2], ports[2:]))

    def cross_all(z, ats):
        state = start
        for i, at in enumerate(ats):
            if i and i % 4 == 0:
                inverse = 1.0 / state[1]
                state = tuple(value * inverse for value in state)
            state = cross(state, z ^ at, *((2, 0) if at < z else (0, 2)))
        return state

    def at_level(z):
        return lambda: (cross_all(z, range(z)), cross_all(z, range(pairs - 1, z, -1)))

    below, above = lax.switch(level, [at_level(z) for z in range(pairs)])
    finish(sizes, below, above, part_ref, low_ref, high_ref, maps_ref, side_ref, pair_refs, out_hbm, out_ref, sems)


def finish(sizes, below, above, part_ref, low_ref, high_ref, maps_ref, side_ref, pair_refs, out_hbm, out_ref, sems):
    rows, _, _, _, mode_count, height = sizes
    total = mode_count * height
    port = 4 * height
    me, upside = lax.axis_index("modes"), lax.axis_index("gz") % 2 == 1

    def pair_ports(i):
        chunks = []
        for d in range(mode_count):
            at = i * height + (d % 2) * port
            chunks.append((side_ref if d < 2 else pair_refs[d // 2 - 1])[at : at + height, :])
        return jnp.concatenate(chunks, axis=0)

    ports = [pair_ports(i) for i in range(4)]
    leave, entry = choose(upside, ports[2:], ports[:2]), choose(upside, ports[:2], ports[2:])
    crossed = apply_map(map_of(maps_ref, (2,), total), choose(upside, below, above), leave, entry)
    below, above = choose(upside, crossed, below), choose(upside, above, crossed)
    own_first, own_last = [part_ref[0, c] for c in range(2)], [part_ref[rows - 1, c] for c in range(2)]
    up = apply_map(map_of(maps_ref, (0,), total), below, own_last, own_first)
    down = apply_map(map_of(maps_ref, (1,), total), above, own_first, own_last)
    up_passed, down_passed = up[1] - up[0], down[1] - down[0]
    inverse_up = 1.0 / (up[0] * above[1] + up_passed * above[0])
    inverse_down = 1.0 / (down[0] * below[1] + down_passed * below[0])
    inverse_below, inverse_above = 1.0 / below[1], 1.0 / above[1]
    under, over = [], []
    for c in range(2, 4):
        last = (up[c] * above[1] + up_passed * above[c]) * inverse_up
        over.append((above[c] + (above[1] - above[0]) * last) * inverse_above)
        first = (down[c] * below[1] + down_passed * below[c]) * inverse_down
        under.append((below[c] + (below[1] - below[0]) * first) * inverse_below)
    copies = []
    for i, (first, size) in enumerate(chunks_of(rows)):
        for k in range(first, first + size):
            low, high = low_ref[k], high_ref[k]
            for c in range(2):
                value = part_ref[k, c] + low * under[c] + high * over[c]
                for d in range(mode_count):
                    out_ref[k, c, me ^ d] = value[d * height : (d + 1) * height]
        part = pl.ds(first, size)
        copies.append(pltpu.make_async_copy(out_ref.at[part], out_hbm.at[part], sems.at[i]))
        copies[-1].start()
    for copy in copies:
        copy.wait()


AWAY = (1, 0, 1, 1)

LIMIT = pltpu.CompilerParams(vmem_limit_bytes=16 << 20)
VMEM = pl.BlockSpec(memory_space=pltpu.VMEM)
ANY = pl.BlockSpec(memory_space=pl.ANY)


def near(*arrays):
    return [pltpu.with_memory_space_constraint(a, pltpu.VMEM) for a in arrays]


def solve(source_field, coupling_below, coupling_above, eigen_stream, eigen_span):
    sizes = rows, kx_total, kx_count, tiles, mode_count, height = sizes_of(source_field)
    partitions = lax.axis_size("gz")
    chips, pairs = mode_count // 2, partitions // 2
    total = mode_count * height
    f32 = jnp.float32
    chunk_sems = pltpu.SemaphoreType.DMA((len(chunks_of(rows)),))

    def move(array, modes_by=0, pair=0, level=0, core=lambda z: 0):
        links = []
        for m in range(mode_count):
            for g in range(partitions):
                to = ((g // 2) ^ level) * 2 + ((g % 2) ^ pair)
                links.append((m * partitions + g, (m ^ modes_by ^ core(g // 2)) * partitions + to))
        return lax.ppermute(array, ("modes", "gz"), links)

    span = eigen_span.reshape(-1, LANES)
    ports, table, spectral, source = pl.pallas_call(
        functools.partial(reduce_kernel, sizes),
        out_shape=(
            pltpu.VMEM((2, chips, 4 * height, LANES), f32),
            pltpu.VMEM((SUBLANES, LANES), f32),
            pltpu.VMEM((2, total, LANES), f32),
            pltpu.VMEM(source_field.shape, f32),
        ),
        in_specs=[ANY] * 5,
        out_specs=(VMEM,) * 4,
        scratch_shapes=[
            pltpu.SMEM(coupling_below.shape, f32),
            pltpu.SMEM(coupling_above.shape, f32),
            pltpu.SMEM(eigen_stream.shape, f32),
            pltpu.VMEM(span.shape, f32),
            pltpu.SemaphoreType.DMA((4,)),
            chunk_sems,
        ],
        name="reduce",
    )(coupling_below, coupling_above, eigen_stream, span, source_field)
    blocks = pl.pallas_call(
        functools.partial(regroup_kernel, sizes),
        out_shape=pltpu.VMEM((mode_count, rows, 2, height, LANES), f32),
        in_specs=[VMEM],
        out_specs=VMEM,
        name="regroup",
    )(*near(source))

    quads = pairs == 4
    away = functools.reduce(lambda a, z: a | (lax.axis_index("gz") // 2 == z), [z for z in range(4) if AWAY[z]], False)
    swapped = (lambda z: AWAY[z]) if quads else (lambda z: 0)
    if quads:
        taken = move(ports, modes_by=1)
        theirs = taken[1]
    else:
        theirs = move(ports[1], modes_by=1)
    blocks_out = [jnp.concatenate([ports[0, d], theirs[d]], axis=0) for d in range(chips)]
    own_parts, pair_parts = [], []
    for d in range(1, chips):
        pair_parts.append(move(blocks_out[d], modes_by=2 * d, pair=1, core=swapped))
        own_parts.append(move(blocks_out[d], modes_by=2 * d, core=swapped))
    side = move(jnp.concatenate([blocks_out[0], table], axis=0), pair=1, core=swapped)
    sources = [move(blocks[d], modes_by=d) if d else blocks[0] for d in range(mode_count)]
    both_spectral = spectral
    own_block, merged_spectral, spectral = blocks_out[0], spectral[0], spectral[0]
    if quads:
        own_block = jnp.where(away, jnp.concatenate([taken[0, 0], ports[1, 0]], axis=0), own_block)
        merged_spectral = jnp.where(away, both_spectral[1], spectral)
    message = pl.pallas_call(
        functools.partial(merge_kernel, sizes),
        out_shape=pltpu.VMEM((4 * total + SUBLANES, LANES), f32),
        in_specs=[VMEM] * (4 + 2 * (chips - 1)),
        out_specs=VMEM,
        name="merge",
    )(*near(merged_spectral, table, own_block, side, *own_parts, *pair_parts))
    if quads:
        messages = [move(message, level=1, core=lambda z: AWAY[z] ^ AWAY[z ^ 1])]
        ahead = pl.pallas_call(
            functools.partial(ahead_kernel, sizes),
            out_shape=pltpu.VMEM((MAP_PARTS * total, LANES), f32),
            in_specs=[VMEM] * 2,
            out_specs=VMEM,
            name="ahead",
        )(*near(merged_spectral, message))
        edge = pl.pallas_call(
            functools.partial(quad_kernel, sizes),
            out_shape=pltpu.VMEM((3 * total, LANES), f32),
            in_specs=[VMEM] * 4,
            out_specs=VMEM,
            name="quad",
        )(*near(merged_spectral, ahead, message, messages[0]))
        other = move(edge, level=2, core=swapped)
        parcel = jnp.concatenate([side, *pair_parts, messages[0][: 4 * total]], axis=0)
        parcel = jnp.where(away, move(parcel, modes_by=1), parcel)
        lines = side.shape[0]
        owned = [parcel[lines * 0 : lines]]
        for d in range(1, chips):
            owned.append(parcel[lines + (d - 1) * 8 * height : lines + d * 8 * height])
        owned_neighbour = parcel[lines + (chips - 1) * 8 * height :]
    else:
        messages = [move(message, level=d) for d in range(1, pairs)]
    map_lines = MAP_PARTS * total
    *local, maps = pl.pallas_call(
        functools.partial(prepare_kernel, sizes),
        out_shape=(
            pltpu.VMEM((rows, 2, total, LANES), f32),
            pltpu.VMEM((rows, total, LANES), f32),
            pltpu.VMEM((rows, total, LANES), f32),
            pltpu.VMEM((3, map_lines, LANES), f32),
        ),
        in_specs=[VMEM] * (3 + mode_count),
        out_specs=(VMEM,) * 4,
        name="prepare",
    )(*near(spectral, table, side, *sources))
    late = None if quads else late_level(pairs)
    level_maps = []
    for d in range(1, 2 if quads else pairs):
        if d != late:
            level_maps.append(
                pl.pallas_call(
                    functools.partial(level_kernel, sizes, d),
                    out_shape=pltpu.VMEM((map_lines, LANES), f32),
                    in_specs=[VMEM] * 2,
                    out_specs=VMEM,
                    name="levels",
                )(*near(spectral, messages[d - 1]))
            )
    if quads:
        kernel = functools.partial(quads_kernel, sizes)
        operands = (*local, maps, level_maps[0], owned_neighbour, other, *owned)
    else:
        kernel = functools.partial(levels_kernel, sizes, pairs, late)
        operands = (spectral, side, *local, maps, *pair_parts, *messages, *level_maps)
    out = pl.pallas_call(
        kernel,
        out_shape=jax.ShapeDtypeStruct((rows, 2, mode_count, height, LANES), f32),
        in_specs=[VMEM] * len(operands),
        out_specs=ANY,
        scratch_shapes=[pltpu.VMEM((rows, 2, mode_count, height, LANES), f32), chunk_sems],
        name="solve",
        compiler_params=LIMIT,
    )(*near(*operands))
    out = out.reshape(rows, 2, mode_count * tiles, kx_count, LANES).transpose(0, 1, 3, 2, 4)
    return out.reshape(rows, 2, kx_count, -1)


def late_level(pairs):
    return min(2, pairs - 1)


def solution(mesh):
    in_specs = (P("gz", None, None, "modes"), P("gz"), P("gz"), P(), P())
    out_specs = P("gz", None, "modes", None)
    return jax.shard_map(solve, mesh=mesh, in_specs=in_specs, out_specs=out_specs, check_vma=False)
```

```python
import functools

import jax
import jax.numpy as jnp
from jax import lax
from jax.experimental import pallas as pl
from jax.experimental.pallas import tpu as pltpu
from jax.sharding import PartitionSpec as P


LANES = 128
SUBLANES = 8


def sizes_of(source_field):
    rows, _, kx_total, ky_local = source_field.shape
    mode_count = lax.axis_size("modes")
    kx_count, tiles = kx_total // mode_count, ky_local // LANES
    return rows, kx_total, kx_count, tiles, mode_count, kx_count * tiles


def chunks_of(rows, count=4):
    size = rows // count if rows % count == 0 else rows
    return [(first, size) for first in range(0, rows, size)]


def fetch(pairs, sems):
    copies = [pltpu.make_async_copy(source, to, sems.at[i]) for i, (source, to) in enumerate(pairs)]
    for copy in copies:
        copy.start()
    return copies


def reduce_kernel(
    sizes, below_hbm, above_hbm, stream_hbm, span_hbm, source_hbm,
    ports_ref, table_ref, spectral_ref, source_ref, below_ref, above_ref, stream_ref, span_ref, small_sems, sems,
):
    rows, kx_total, kx_count, tiles, mode_count, height = sizes
    me, partition = lax.axis_index("modes"), lax.axis_index("gz")
    small = fetch(
        [(below_hbm, below_ref), (above_hbm, above_ref), (stream_hbm, stream_ref), (span_hbm, span_ref)], small_sems
    )
    parts = [pl.ds(first, size) for first, size in chunks_of(rows)]
    copies = fetch([(source_hbm.at[p], source_ref.at[p]) for p in parts], sems)
    for copy in small:
        copy.wait()
    lower = [below_ref[k] for k in range(rows)]
    upper = [above_ref[k] for k in range(rows)]
    lower[0] = jnp.where(partition == 0, 0.0, lower[0])
    upper[-1] = jnp.where(partition == lax.axis_size("gz") - 1, 0.0, upper[-1])
    lane = lax.broadcasted_iota(jnp.int32, (SUBLANES, LANES), 1)
    sub = lax.broadcasted_iota(jnp.int32, (SUBLANES, LANES), 0)
    table = jnp.zeros((SUBLANES, LANES), jnp.float32)
    for k in range(rows):
        table = jnp.where((lane == k) & (sub < 2), jnp.where(sub == 0, lower[k], upper[k]), table)
        table = jnp.where((lane == rows - 1 - k) & (sub >= 2), jnp.where(sub == 2, upper[k], lower[k]), table)
    table_ref[...] = table
    for d in range(mode_count):
        for t in range(tiles):
            for owner in range(2):
                spanwise = span_ref[pl.ds((me ^ owner ^ d) * tiles + t, 1), :]
                for j in range(kx_count):
                    at = d * height + t * kx_count + j
                    spectral_ref[owner, at : at + 1, :] = spanwise + stream_ref[(me ^ owner) * kx_count + j]
    shape = (kx_total, LANES)
    kx_at = lax.broadcasted_iota(jnp.int32, shape, 0)
    streamwise = jnp.zeros(shape, jnp.float32)
    for i in range(kx_total):
        streamwise = jnp.where(kx_at == i, stream_ref[i], streamwise)
    each = range(tiles)
    spectral = [streamwise + span_ref[pl.ds(me * tiles + t, 1), :] for t in each]
    one, zero = jnp.ones(shape, jnp.float32), jnp.zeros(shape, jnp.float32)
    grown, passed = [one] * tiles, [one] * tiles
    partial = [[zero] * tiles, [zero] * tiles]
    first_value = [[zero] * tiles, [zero] * tiles]
    starts = {first: i for i, (first, _) in enumerate(chunks_of(rows))}
    for k in range(rows):
        if k in starts:
            copies[starts[k]].wait()
        for t in each:
            held = spectral[t] + lower[k] * grown[t]
            inverse = 1.0 / (upper[k] + held)
            grown[t] = held * inverse
            for c in range(2):
                source = source_ref[k, c, :, t * LANES : (t + 1) * LANES]
                partial[c][t] = (source + lower[k] * partial[c][t]) * inverse
                first_value[c][t] = first_value[c][t] + passed[t] * partial[c][t]
            passed[t] = passed[t] * (upper[k] * inverse)
    values = first_value + partial
    for dest in range(mode_count):
        to = dest ^ me
        for i in range(4):
            for t in each:
                at = i * height + t * kx_count
                ports_ref[to % 2, to // 2, at : at + kx_count, :] = values[i][t][dest * kx_count : (dest + 1) * kx_count]


def regroup_kernel(sizes, source_ref, blocks_ref):
    rows, _, kx_count, tiles, mode_count, _ = sizes
    me = lax.axis_index("modes")
    for dest in range(mode_count):
        to = dest ^ me
        lines = slice(dest * kx_count, (dest + 1) * kx_count)
        for k in range(rows):
            for c in range(2):
                for t in range(tiles):
                    at = t * kx_count
                    blocks_ref[to, k, c, at : at + kx_count, :] = source_ref[k, c, lines, t * LANES : (t + 1) * LANES]


def couplings(table, line, count):
    return [table[line : line + 1, k : k + 1] for k in range(count)]


def climb(spectral, num, den, near, far):
    product = near[0]
    for k in range(len(near)):
        step = near[k] * num
        num = spectral * den + step
        den = (spectral + far[k]) * den + step
        if k:
            product = product * near[k]
    return num, den, product


MAP_PARTS = 5


def put_map(ref, lead, spectral, near, far):
    total = spectral.shape[0]
    num = [near[0] + jnp.zeros_like(spectral), spectral]
    den = [num[0], spectral + far[0]]
    product = near[0]
    for k in range(1, len(near)):
        held = spectral + far[k]
        step = [near[k] * num[i] for i in range(2)]
        num = [spectral * den[i] + step[i] for i in range(2)]
        den = [held * den[i] + step[i] for i in range(2)]
        product = product * near[k]
    scale = 1.0 / (den[0] + den[1])
    for i, value in enumerate([*num, *den, product]):
        ref[(*lead, slice(i * total, (i + 1) * total), slice(None))] = value * scale


def leave_with(state, new_den, product, leave, entry):
    num, den, *partial = state
    return [leave[c] * new_den + product * (partial[c] + (den - num) * entry[c]) for c in range(2)]


def apply_map(block, state, leave, entry):
    num, den = state[:2]
    new_den = block(2) * num + block(3) * den
    return (block(0) * num + block(1) * den, new_den, *leave_with(state, new_den, block(4), leave, entry))


def choose(condition, first, second):
    return [jnp.where(condition, a, b) for a, b in zip(first, second)]


def map_of(ref, lead, total):
    return lambda i: ref[(*lead, slice(i * total, (i + 1) * total), slice(None))]


def locals_kernel(sizes, spectral_ref, table_ref, maps_ref):
    spectral, table = spectral_ref[...], table_ref[...]
    for i in range(2):
        put_map(maps_ref, (i,), spectral, *(couplings(table, 2 * i + j, sizes[0]) for j in range(2)))


def merge_kernel(sizes, spectral_ref, table_ref, maps_ref, own_ref, side_ref, *rest):
    rows, _, _, _, mode_count, height = sizes
    chips = mode_count // 2
    own_refs, pair_refs, message_ref = rest[: chips - 1], rest[chips - 1 : 2 * (chips - 1)], rest[-1]
    total = mode_count * height
    port = 4 * height
    upside = lax.axis_index("gz") % 2 == 1

    def gather(first_ref, refs, i):
        chunks = []
        for d in range(mode_count):
            start = i * height + (d % 2) * port
            chunks.append((first_ref if d < 2 else refs[d // 2 - 1])[start : start + height, :])
        return jnp.concatenate(chunks, axis=0)

    own_table, pair_table = table_ref[...], side_ref[2 * port :, :]
    low_table = jnp.where(upside, pair_table, own_table)
    high_table = jnp.where(upside, own_table, pair_table)
    sub = lax.broadcasted_iota(jnp.int32, (SUBLANES, LANES), 0)
    lane = lax.broadcasted_iota(jnp.int32, (SUBLANES, LANES), 1)
    ahead = jnp.where(sub < 2, low_table, high_table)
    behind = jnp.where(sub < 2, high_table, low_table)
    message_ref[4 * total :, :] = jnp.where(lane < rows, ahead, pltpu.roll(behind, rows, 1))
    spectral = spectral_ref[...]
    one = jnp.ones((total, LANES), jnp.float32)
    own = [gather(own_ref, own_refs, i) for i in range(4)]
    pair = [gather(side_ref, pair_refs, i) for i in range(4)]
    far_own, near_own = choose(upside, own[:2], own[2:]), choose(upside, own[2:], own[:2])
    far_pair, near_pair = choose(upside, pair[:2], pair[2:]), choose(upside, pair[2:], pair[:2])
    away_lines = jnp.where(upside, pair_table[2:4], pair_table[0:2])
    back_lines = jnp.where(upside, pair_table[0:2], pair_table[2:4])
    turn = lax.axis_index("gz") % 2
    away_map, back_map = map_of(maps_ref, (turn,), total), map_of(maps_ref, (1 - turn,), total)
    state = (away_map(0) + away_map(1), one, *far_own)
    num, den, product = climb(spectral, state[0], one, *(couplings(away_lines, i, rows) for i in range(2)))
    scale = 1.0 / den
    away = [value * scale for value in leave_with(state, den, product, far_pair, near_pair)]
    num, den, _ = climb(spectral, one, one, *(couplings(back_lines, i, rows) for i in range(2)))
    state = apply_map(back_map, (num, den, *(value * den for value in near_pair)), near_own, far_own)
    scale = 1.0 / state[1]
    back = [value * scale for value in state[2:]]
    for i, value in enumerate([*choose(upside, away, back), *choose(upside, back, away)]):
        message_ref[i * total : (i + 1) * total, :] = value


def prepare_kernel(sizes, spectral_ref, table_ref, side_ref, *rest):
    rows, _, _, _, mode_count, height = sizes
    sources, (part_ref, low_ref, high_ref, maps_ref) = rest[:mode_count], rest[mode_count:]
    spectral, table = spectral_ref[...], table_ref[...]
    lower, upper = couplings(table, 0, rows), couplings(table, 1, rows)
    grown = jnp.ones(spectral.shape, jnp.float32)
    carried = grown
    partial = [jnp.zeros(spectral.shape, jnp.float32)] * 2
    for k in range(rows):
        held = spectral + lower[k] * grown
        inverse = 1.0 / (upper[k] + held)
        grown = held * inverse
        scaled = lower[k] * inverse
        carried = scaled * carried
        low_ref[k] = carried
        high_ref[k] = upper[k] * inverse
        for c in range(2):
            source = jnp.concatenate([sources[d][k, c] for d in range(mode_count)], axis=0)
            partial[c] = source * inverse + scaled * partial[c]
            part_ref[k, c] = partial[c]
    low, high = low_ref[rows - 1], high_ref[rows - 1]
    for k in range(rows - 2, -1, -1):
        factor = high_ref[k]
        low = low_ref[k] + factor * low
        low_ref[k] = low
        high = factor * high
        high_ref[k] = high
        for c in range(2):
            partial[c] = part_ref[k, c] + factor * partial[c]
            part_ref[k, c] = partial[c]
    pair_table = side_ref[2 * 4 * height :, :]
    upside = lax.axis_index("gz") % 2 == 1
    put_map(maps_ref, (0,), spectral, lower, upper)
    put_map(maps_ref, (1,), spectral, couplings(table, 2, rows), couplings(table, 3, rows))
    lines = jnp.where(upside, pair_table[0:2], pair_table[2:4])
    put_map(maps_ref, (2,), spectral, couplings(lines, 0, rows), couplings(lines, 1, rows))


def level_couplings(sizes, message_ref, total, downwards):
    table = message_ref[4 * total :, :]
    lines = jnp.where(downwards, table[2:4], table[0:2])
    return couplings(lines, 0, 2 * sizes[0]), couplings(lines, 1, 2 * sizes[0])


def level_kernel(sizes, d, spectral_ref, message_ref, map_ref):
    level = lax.axis_index("gz") // 2
    spectral = spectral_ref[...]
    put_map(map_ref, (), spectral, *level_couplings(sizes, message_ref, spectral.shape[0], (level ^ d) > level))


def ahead_kernel(sizes, spectral_ref, own_ref, map_ref):
    spectral = spectral_ref[...]
    lower = lax.axis_index("gz") // 2 < 2
    put_map(map_ref, (), spectral, *level_couplings(sizes, own_ref, spectral.shape[0], jnp.logical_not(lower)))


def quad_kernel(sizes, spectral_ref, map_ref, own_ref, neighbour_ref, edge_ref):
    spectral = spectral_ref[...]
    total = spectral.shape[0]
    level = lax.axis_index("gz") // 2
    lower, outer = level < 2, (level == 0) | (level == 3)

    def ports(ref):
        low, high = ([ref[(at + c) * total : (at + c + 1) * total, :] for c in range(2)] for at in (0, 2))
        return choose(lower, high, low), choose(lower, low, high)

    own, neighbour = ports(own_ref), ports(neighbour_ref)
    own_map = map_of(map_ref, (), total)
    one, zero = jnp.ones_like(spectral), jnp.zeros_like(spectral)
    start = choose(outer, (own_map(0) + own_map(1), one, *own[0]), (one, one, zero, zero))
    num, den, product = climb(
        spectral, start[0], one, *level_couplings(sizes, neighbour_ref, total, jnp.logical_not(lower))
    )
    passed = (num, den, *leave_with(start, den, product, *neighbour))
    num, den, *partial = choose(outer, passed, apply_map(own_map, passed, *own))
    scale = 1.0 / den
    for i, value in enumerate([num, *partial]):
        edge_ref[i * total : (i + 1) * total, :] = value * scale


def quads_kernel(sizes, part_ref, low_ref, high_ref, maps_ref, neighbour_map, neighbour_ref, other_ref, side_ref, *rest):
    _, _, _, _, mode_count, height = sizes
    total = mode_count * height
    pair_refs, (out_hbm, out_ref, sems) = rest[: mode_count // 2 - 1], rest[mode_count // 2 - 1 :]
    level = lax.axis_index("gz") // 2
    odd, outer = level % 2 == 1, (level == 0) | (level == 3)
    one, zero = jnp.ones((total, LANES), jnp.float32), jnp.zeros((total, LANES), jnp.float32)
    wall = (one, one, zero, zero)
    values = [other_ref[i * total : (i + 1) * total, :] for i in range(3)]
    other = (values[0], one, *values[1:])
    ports = [neighbour_ref[i * total : (i + 1) * total, :] for i in range(4)]
    leave, entry = choose(odd, ports[2:], ports[:2]), choose(odd, ports[:2], ports[2:])
    crossed = apply_map(map_of(neighbour_map, (), total), choose(outer, other, wall), leave, entry)
    plain = choose(outer, wall, other)
    below, above = choose(odd, crossed, plain), choose(odd, plain, crossed)
    finish(sizes, below, above, part_ref, low_ref, high_ref, maps_ref, side_ref, pair_refs, out_hbm, out_ref, sems)


def levels_kernel(sizes, pairs, late, spectral_ref, side_ref, part_ref, low_ref, high_ref, maps_ref, *rest):
    _, _, _, _, mode_count, height = sizes
    chips = mode_count // 2
    total = mode_count * height
    pair_refs, rest = rest[: chips - 1], rest[chips - 1 :]
    messages, rest = rest[: pairs - 1], rest[pairs - 1 :]
    level_maps, (out_hbm, out_ref, sems) = list(rest[: pairs - 2]), rest[pairs - 2 :]
    level_maps.insert(late - 1, None)
    spectral = spectral_ref[...]
    level = lax.axis_index("gz") // 2
    late_near, late_far = level_couplings(sizes, messages[late - 1], total, (level ^ late) > level)
    one, zero = jnp.ones((total, LANES), jnp.float32), jnp.zeros((total, LANES), jnp.float32)
    start = (one, one, zero, zero)

    def cross(state, d, leave, entry):
        ref = messages[d - 1]
        ports = [ref[i * total : (i + 1) * total, :] for i in (leave, leave + 1, entry, entry + 1)]
        if d != late:
            return apply_map(map_of(level_maps[d - 1], (), total), state, ports[:2], ports[2:])
        num, den, product = climb(spectral, *state[:2], late_near, late_far)
        return (num, den, *leave_with(state, den, product, ports[:2], ports[2:]))

    def cross_all(z, ats):
        state = start
        for i, at in enumerate(ats):
            if i and i % 4 == 0:
                inverse = 1.0 / state[1]
                state = tuple(value * inverse for value in state)
            state = cross(state, z ^ at, *((2, 0) if at < z else (0, 2)))
        return state

    def at_level(z):
        return lambda: (cross_all(z, range(z)), cross_all(z, range(pairs - 1, z, -1)))

    below, above = lax.switch(level, [at_level(z) for z in range(pairs)])
    finish(sizes, below, above, part_ref, low_ref, high_ref, maps_ref, side_ref, pair_refs, out_hbm, out_ref, sems)


def finish(sizes, below, above, part_ref, low_ref, high_ref, maps_ref, side_ref, pair_refs, out_hbm, out_ref, sems):
    rows, _, _, _, mode_count, height = sizes
    total = mode_count * height
    port = 4 * height
    me, upside = lax.axis_index("modes"), lax.axis_index("gz") % 2 == 1

    def pair_ports(i):
        chunks = []
        for d in range(mode_count):
            at = i * height + (d % 2) * port
            chunks.append((side_ref if d < 2 else pair_refs[d // 2 - 1])[at : at + height, :])
        return jnp.concatenate(chunks, axis=0)

    ports = [pair_ports(i) for i in range(4)]
    leave, entry = choose(upside, ports[2:], ports[:2]), choose(upside, ports[:2], ports[2:])
    crossed = apply_map(map_of(maps_ref, (2,), total), choose(upside, below, above), leave, entry)
    below, above = choose(upside, crossed, below), choose(upside, above, crossed)
    own_first, own_last = [part_ref[0, c] for c in range(2)], [part_ref[rows - 1, c] for c in range(2)]
    up = apply_map(map_of(maps_ref, (0,), total), below, own_last, own_first)
    down = apply_map(map_of(maps_ref, (1,), total), above, own_first, own_last)
    up_passed, down_passed = up[1] - up[0], down[1] - down[0]
    inverse_up = 1.0 / (up[0] * above[1] + up_passed * above[0])
    inverse_down = 1.0 / (down[0] * below[1] + down_passed * below[0])
    inverse_below, inverse_above = 1.0 / below[1], 1.0 / above[1]
    under, over = [], []
    for c in range(2, 4):
        last = (up[c] * above[1] + up_passed * above[c]) * inverse_up
        over.append((above[c] + (above[1] - above[0]) * last) * inverse_above)
        first = (down[c] * below[1] + down_passed * below[c]) * inverse_down
        under.append((below[c] + (below[1] - below[0]) * first) * inverse_below)
    copies = []
    for i, (first, size) in enumerate(chunks_of(rows)):
        for k in range(first, first + size):
            low, high = low_ref[k], high_ref[k]
            for c in range(2):
                value = part_ref[k, c] + low * under[c] + high * over[c]
                for d in range(mode_count):
                    out_ref[k, c, me ^ d] = value[d * height : (d + 1) * height]
        part = pl.ds(first, size)
        copies.append(pltpu.make_async_copy(out_ref.at[part], out_hbm.at[part], sems.at[i]))
        copies[-1].start()
    for copy in copies:
        copy.wait()


AWAY = (1, 0, 1, 1)

LIMIT = pltpu.CompilerParams(vmem_limit_bytes=16 << 20)
VMEM = pl.BlockSpec(memory_space=pltpu.VMEM)
ANY = pl.BlockSpec(memory_space=pl.ANY)


def near(*arrays):
    return [pltpu.with_memory_space_constraint(a, pltpu.VMEM) for a in arrays]


def solve(source_field, coupling_below, coupling_above, eigen_stream, eigen_span):
    sizes = rows, kx_total, kx_count, tiles, mode_count, height = sizes_of(source_field)
    partitions = lax.axis_size("gz")
    chips, pairs = mode_count // 2, partitions // 2
    total = mode_count * height
    f32 = jnp.float32
    chunk_sems = pltpu.SemaphoreType.DMA((len(chunks_of(rows)),))

    def move(array, modes_by=0, pair=0, level=0, core=lambda z: 0):
        links = []
        for m in range(mode_count):
            for g in range(partitions):
                to = ((g // 2) ^ level) * 2 + ((g % 2) ^ pair)
                links.append((m * partitions + g, (m ^ modes_by ^ core(g // 2)) * partitions + to))
        return lax.ppermute(array, ("modes", "gz"), links)

    span = eigen_span.reshape(-1, LANES)
    ports, table, spectral, source = pl.pallas_call(
        functools.partial(reduce_kernel, sizes),
        out_shape=(
            pltpu.VMEM((2, chips, 4 * height, LANES), f32),
            pltpu.VMEM((SUBLANES, LANES), f32),
            pltpu.VMEM((2, total, LANES), f32),
            pltpu.VMEM(source_field.shape, f32),
        ),
        in_specs=[ANY] * 5,
        out_specs=(VMEM,) * 4,
        scratch_shapes=[
            pltpu.SMEM(coupling_below.shape, f32),
            pltpu.SMEM(coupling_above.shape, f32),
            pltpu.SMEM(eigen_stream.shape, f32),
            pltpu.VMEM(span.shape, f32),
            pltpu.SemaphoreType.DMA((4,)),
            chunk_sems,
        ],
        name="reduce",
    )(coupling_below, coupling_above, eigen_stream, span, source_field)
    blocks = pl.pallas_call(
        functools.partial(regroup_kernel, sizes),
        out_shape=pltpu.VMEM((mode_count, rows, 2, height, LANES), f32),
        in_specs=[VMEM],
        out_specs=VMEM,
        name="regroup",
    )(*near(source))

    quads = pairs == 4
    away = functools.reduce(lambda a, z: a | (lax.axis_index("gz") // 2 == z), [z for z in range(4) if AWAY[z]], False)
    swapped = (lambda z: AWAY[z]) if quads else (lambda z: 0)
    if quads:
        taken = move(ports, modes_by=1)
        theirs = taken[1]
    else:
        theirs = move(ports[1], modes_by=1)
    blocks_out = [jnp.concatenate([ports[0, d], theirs[d]], axis=0) for d in range(chips)]
    own_parts, pair_parts = [], []
    for d in range(1, chips):
        pair_parts.append(move(blocks_out[d], modes_by=2 * d, pair=1, core=swapped))
        own_parts.append(move(blocks_out[d], modes_by=2 * d, core=swapped))
    side = move(jnp.concatenate([blocks_out[0], table], axis=0), pair=1, core=swapped)
    sources = [move(blocks[d], modes_by=d) if d else blocks[0] for d in range(mode_count)]
    both_spectral = spectral
    own_block, merged_spectral, spectral = blocks_out[0], spectral[0], spectral[0]
    if quads:
        own_block = jnp.where(away, jnp.concatenate([taken[0, 0], ports[1, 0]], axis=0), own_block)
        merged_spectral = jnp.where(away, both_spectral[1], spectral)
    local_maps = pl.pallas_call(
        functools.partial(locals_kernel, sizes),
        out_shape=pltpu.VMEM((2, MAP_PARTS * total, LANES), f32),
        in_specs=[VMEM] * 2,
        out_specs=VMEM,
        name="locals",
    )(*near(merged_spectral, table))
    message = pl.pallas_call(
        functools.partial(merge_kernel, sizes),
        out_shape=pltpu.VMEM((4 * total + SUBLANES, LANES), f32),
        in_specs=[VMEM] * (5 + 2 * (chips - 1)),
        out_specs=VMEM,
        name="merge",
    )(*near(merged_spectral, table, local_maps, own_block, side, *own_parts, *pair_parts))
    if quads:
        messages = [move(message, level=1, core=lambda z: AWAY[z] ^ AWAY[z ^ 1])]
        ahead = pl.pallas_call(
            functools.partial(ahead_kernel, sizes),
            out_shape=pltpu.VMEM((MAP_PARTS * total, LANES), f32),
            in_specs=[VMEM] * 2,
            out_specs=VMEM,
            name="ahead",
        )(*near(merged_spectral, message))
        edge = pl.pallas_call(
            functools.partial(quad_kernel, sizes),
            out_shape=pltpu.VMEM((3 * total, LANES), f32),
            in_specs=[VMEM] * 4,
            out_specs=VMEM,
            name="quad",
        )(*near(merged_spectral, ahead, message, messages[0]))
        other = move(edge, level=2, core=swapped)
        parcel = jnp.concatenate([side, *pair_parts, messages[0][: 4 * total]], axis=0)
        parcel = jnp.where(away, move(parcel, modes_by=1), parcel)
        lines = side.shape[0]
        owned = [parcel[lines * 0 : lines]]
        for d in range(1, chips):
            owned.append(parcel[lines + (d - 1) * 8 * height : lines + d * 8 * height])
        owned_neighbour = parcel[lines + (chips - 1) * 8 * height :]
    else:
        messages = [move(message, level=d) for d in range(1, pairs)]
    map_lines = MAP_PARTS * total
    *local, maps = pl.pallas_call(
        functools.partial(prepare_kernel, sizes),
        out_shape=(
            pltpu.VMEM((rows, 2, total, LANES), f32),
            pltpu.VMEM((rows, total, LANES), f32),
            pltpu.VMEM((rows, total, LANES), f32),
            pltpu.VMEM((3, map_lines, LANES), f32),
        ),
        in_specs=[VMEM] * (3 + mode_count),
        out_specs=(VMEM,) * 4,
        name="prepare",
    )(*near(spectral, table, side, *sources))
    late = None if quads else late_level(pairs)
    level_maps = []
    for d in range(1, 2 if quads else pairs):
        if d != late:
            level_maps.append(
                pl.pallas_call(
                    functools.partial(level_kernel, sizes, d),
                    out_shape=pltpu.VMEM((map_lines, LANES), f32),
                    in_specs=[VMEM] * 2,
                    out_specs=VMEM,
                    name="levels",
                )(*near(spectral, messages[d - 1]))
            )
    if quads:
        kernel = functools.partial(quads_kernel, sizes)
        operands = (*local, maps, level_maps[0], owned_neighbour, other, *owned)
    else:
        kernel = functools.partial(levels_kernel, sizes, pairs, late)
        operands = (spectral, side, *local, maps, *pair_parts, *messages, *level_maps)
    out = pl.pallas_call(
        kernel,
        out_shape=jax.ShapeDtypeStruct((rows, 2, mode_count, height, LANES), f32),
        in_specs=[VMEM] * len(operands),
        out_specs=ANY,
        scratch_shapes=[pltpu.VMEM((rows, 2, mode_count, height, LANES), f32), chunk_sems],
        name="solve",
        compiler_params=LIMIT,
    )(*near(*operands))
    out = out.reshape(rows, 2, mode_count * tiles, kx_count, LANES).transpose(0, 1, 3, 2, 4)
    return out.reshape(rows, 2, kx_count, -1)


def late_level(pairs):
    return min(2, pairs - 1)


def solution(mesh):
    in_specs = (P("gz", None, None, "modes"), P("gz"), P("gz"), P(), P())
    out_specs = P("gz", None, "modes", None)
    return jax.shard_map(solve, mesh=mesh, in_specs=in_specs, out_specs=out_specs, check_vma=False)
```
